32 devices in a mesh: dp: 4 (over y, x), context: 2 (over core), expert: 4 (over z).
Axes of the slice: x: 2, y: 2, z: 4, core: 2. Of those that a mesh axis runs over, the one named last changes fastest.
Arguments:
- tokens: bfloat16 [16, 1024, 1536], P(('dp', 'expert'), 'context'), may hold values from -6 to 6
- cotangent: bfloat16 [16, 1024, 1536], P(('dp', 'expert'), 'context'), may hold values from -6 to 6
- segment_ids: int32 [16, 1024], P(('dp', 'expert')), may hold values from 0 to 5, never falling along the last dimension, each value on 1 to 512 neighbouring positions
- routes: int32 [16, 1024, 4], P(('dp', 'expert'), 'context'), may hold values from 0 to 7, all different within a row
- fill_rank: int32 [16, 2, 2048], P(('dp', 'expert'), 'context'), may hold values from 0 to 2047, each once within a row
- query_weight: bfloat16 [1536, 1536], P('context'), may hold values from -0.3125 to 0.3125
- key_projection_weight: bfloat16 [1536, 256], P('context'), may hold values from -0.15625 to 0.15625
- value_projection_weight: bfloat16 [1536, 256], P('context'), may hold values from -0.15625 to 0.15625
- output_weight: bfloat16 [1536, 1536], P('context'), may hold values from -0.625 to 0.625
- router_weight: bfloat16 [1536, 8], P('context'), may hold values from -0.078125 to 0.078125
- gain_attention: bfloat16 [1536], P('context'), may hold values from 0.5 to 1.5
- gain_experts: bfloat16 [1536], P('context'), may hold values from 0.5 to 1.5
- gate_weight: bfloat16 [8, 1536, 768], P('expert'), may hold values from -0.15625 to 0.15625
- up_weight: bfloat16 [8, 1536, 768], P('expert'), may hold values from -0.15625 to 0.15625
- down_weight: bfloat16 [8, 1536, 768], P('expert'), may hold values from -0.4375 to 0.4375
Outputs:
- layer_out: bfloat16 [16, 1024, 1536], P(('dp', 'expert'), 'context')
- grad_tokens: bfloat16 [16, 1024, 1536], P(('dp', 'expert'), 'context')
- query_grad: float32 [1536, 1536], P('context')
- key_grad: float32 [1536, 256], P('context')
- value_grad: float32 [1536, 256], P('context')
- output_grad: float32 [1536, 1536], P('context')
- router_grad: float32 [1536, 8], P('context')
- gain_attention_grad: float32 [1536], P('context')
- gain_experts_grad: float32 [1536], P('context')
- gate_grad: float32 [8, 1536, 768], P('expert', ('dp', 'context'))
- up_grad: float32 [8, 1536, 768], P('expert', ('dp', 'context'))
- down_grad: float32 [8, 1536, 768], P('expert', ('dp', 'context'))
The draws below stay inside these ranges and needn't reach their ends.
Inputs may be any that keep to these rules, and one draw needn't show every extreme that they name: `segment_ids`: segment ids never fall along a sequence; each id covers 1 to 512 positions and some id covers exactly 512. `routes`: each token names 4 different experts. `fill_rank`: each device's row is a permutation of its 2048 pairs.
All inputs are finite; a program needn't handle non-finite values.
Results may differ from the reference program's by a relative error of at most 0.022.
Values may be sent and summed in bfloat16 or wider, within the bound.
A program may use at most 384 MiB of HBM per device.

```python
import math
import jax
import jax.numpy as jnp
import numpy as np
from jax import lax

MODEL_WIDTH = 1536
QUERY_HEADS = 12
KEY_VALUE_HEADS = 2
HEAD_SIZE = 128
FF = 768
TOP = 4
DOCS = 6
EXPERTS = 8
SEQUENCE_TOKENS = 1024
TOK_DEV = 512
SEQS = 16
CAP = 320
N_CONTEXT = 2


def block_scale(rng, shape, shards, low, high):
    factor_of, own = 1.0, jax.random.fold_in(rng, 6)
    for dim, parts in shards:
        steps = jnp.exp(jax.random.uniform(jax.random.fold_in(own, dim), (parts,), jnp.float32, low / len(shards), high / len(shards)))
        factor_of = factor_of * jnp.repeat(steps, shape[dim] // parts).reshape([-1 if axis == dim else 1 for axis in range(len(shape))])
    return factor_of


def distinct(own_key, rows, number_of, top, lift):
    order = jax.random.permutation(jax.random.fold_in(own_key, 1), number_of)
    pull = order
    for power in range(3):
        pull = pull * pull // number_of
    pull = pull * lift // number_of
    chance = jax.random.randint(jax.random.fold_in(own_key, 2), (rows, number_of), 0, 4096) + pull
    fixed_rows = jax.random.permutation(jax.random.fold_in(own_key, 3), rows)[jnp.arange(number_of) % rows]
    chance = jnp.where(jnp.arange(rows)[:, None] == fixed_rows[None, :], 1 << 14, chance)
    merit = chance * number_of + jnp.arange(number_of)
    return lax.top_k(merit.astype(jnp.int32), top)[1].astype(jnp.int32)


def split_up(count, total, reach, skew):
    loads = [(1 << 20) // math.isqrt(grade ** skew) + 1 for grade in range(2, count + 1)]
    spare, holding = total - reach - (count - 1), [1] * (count - 1)
    while spare > 0:
        movable = [i for i in range(count - 1) if holding[i] < reach]
        whole, left = sum([loads[i] for i in movable]), spare
        for i in movable:
            extra = min(reach - holding[i], max(1, left * loads[i] // whole), spare)
            holding[i] = holding[i] + extra
            spare = spare - extra
    return np.array([reach] + holding)


def uneven(stream_key, number_of, total, most, skew):
    if number_of == 2:
        one = jax.random.randint(stream_key, (), max(1, total - most), min(most, total - 1) + 1)
        return jnp.stack([one, total - one])
    lengths = jnp.asarray(split_up(number_of, total, most, skew), jnp.int32)
    twos = (number_of - 1) // 2
    source_of, receiver = lengths[1:1 + 2 * twos:2], lengths[2:2 + 2 * twos:2]
    margin = jnp.minimum(source_of - 1, most - receiver)
    moved = jax.random.randint(jax.random.fold_in(stream_key, 1), (twos,), 0, 1 << 20) % (margin + 1)
    lengths = lengths.at[1:1 + 2 * twos:2].set(source_of - moved).at[2:2 + 2 * twos:2].set(receiver + moved)
    return lengths[jax.random.permutation(jax.random.fold_in(stream_key, 2), number_of)]


def noise(rng, dims, deviation, reach, shards=(), kind=jnp.bfloat16):
    values = jax.random.normal(rng, dims, jnp.float32) * deviation
    if len(shards) > 0:
        values = block_scale(rng, dims, shards, -0.22, 0.18) * values
    return jnp.clip(values, min=-reach, max=reach).astype(kind)


def setup_inputs(seed: int = 0) -> dict:
    arg_keys = jax.random.split(jax.random.key(seed), 16)
    return {
        "tokens": noise(arg_keys[0], (SEQS, SEQUENCE_TOKENS, MODEL_WIDTH), 1.0, 6.0, ((0, 16), (1, 2))),
        "cotangent": noise(arg_keys[1], (SEQS, SEQUENCE_TOKENS, MODEL_WIDTH), 1.0, 6.0, ((0, 16), (1, 2))),
        "segment_ids": jax.vmap(lambda own: jnp.searchsorted(jnp.cumsum(uneven(own, DOCS, SEQUENCE_TOKENS, SEQUENCE_TOKENS // 2, 1)), jnp.arange(SEQUENCE_TOKENS), side="right"))(jax.random.split(arg_keys[2], SEQS)).reshape((SEQS, SEQUENCE_TOKENS)).astype(jnp.int32),
        "routes": distinct(arg_keys[3], SEQS * SEQUENCE_TOKENS, EXPERTS, TOP, 4096).reshape((SEQS, SEQUENCE_TOKENS, TOP)),
        "fill_rank": jax.vmap(lambda own: jax.random.permutation(own, TOK_DEV * TOP))(jax.random.split(arg_keys[4], SEQS * N_CONTEXT)).reshape((SEQS, N_CONTEXT, TOK_DEV * TOP)).astype(jnp.int32),
        "query_weight": noise(arg_keys[5], (MODEL_WIDTH, QUERY_HEADS * HEAD_SIZE), (MODEL_WIDTH // 4) ** -0.5, 0.3125, ((0, 2),)),
        "key_projection_weight": noise(arg_keys[6], (MODEL_WIDTH, KEY_VALUE_HEADS * HEAD_SIZE), MODEL_WIDTH ** -0.5, 0.15625, ((0, 2),)),
        "value_projection_weight": noise(arg_keys[7], (MODEL_WIDTH, KEY_VALUE_HEADS * HEAD_SIZE), MODEL_WIDTH ** -0.5, 0.15625, ((0, 2),)),
        "output_weight": noise(arg_keys[8], (QUERY_HEADS * HEAD_SIZE, MODEL_WIDTH), (QUERY_HEADS * HEAD_SIZE // 16) ** -0.5, 0.625, ((0, 2),)),
        "router_weight": noise(arg_keys[9], (MODEL_WIDTH, EXPERTS), (4 * MODEL_WIDTH) ** -0.5, 0.078125, ((0, 2),)),
        "gain_attention": jnp.clip(1.0 + 0.1 * jax.random.normal(arg_keys[10], (MODEL_WIDTH,), jnp.float32), 0.5, 1.5).astype(jnp.bfloat16),
        "gain_experts": jnp.clip(1.0 + 0.1 * jax.random.normal(arg_keys[11], (MODEL_WIDTH,), jnp.float32), 0.5, 1.5).astype(jnp.bfloat16),
        "gate_weight": noise(arg_keys[12], (EXPERTS, MODEL_WIDTH, FF), MODEL_WIDTH ** -0.5, 0.15625, ((0, 4),)),
        "up_weight": noise(arg_keys[13], (EXPERTS, MODEL_WIDTH, FF), MODEL_WIDTH ** -0.5, 0.15625, ((0, 4),)),
        "down_weight": noise(arg_keys[14], (EXPERTS, MODEL_WIDTH, FF), (FF // 4) ** -0.5, 0.4375, ((0, 4),)),
    }


@jax.custom_vjp
def low(v):
    return lax.optimization_barrier(v.astype(jnp.bfloat16)).astype(jnp.float32)

@jax.custom_vjp
def low_back(v):
    return v

def low_keep(v):
    return (low(v), None)

def low_pass(kept, grad):
    return (grad,)

def back_keep(v):
    return (v, None)

def back_low(kept, grad):
    return (low(grad),)
low.defvjp(low_keep, low_pass)
low_back.defvjp(back_keep, back_low)
norm_eps = 1e-06
rope_base = 10000.0
masked_fill_value = -1e+30

def highest(first_operand, second_operand):
    return jnp.dot(first_operand, second_operand, precision=lax.Precision.HIGHEST, preferred_element_type=jnp.float32)

def rms_norm(value_tensor, gain_vector):
    root_scale = lax.rsqrt(lax.optimization_barrier(jnp.mean(value_tensor * value_tensor, axis=-1, keepdims=True)) + norm_eps)
    return value_tensor * root_scale * gain_vector

def rope_tables(positions, head_width):
    half_width = head_width // 2
    frequency = jnp.exp(-(jnp.arange(half_width, dtype=jnp.float32) * (2.0 / head_width)) * math.log(rope_base))
    angle = positions.astype(jnp.float32)[:, None] * frequency[None, :]
    return (jnp.cos(angle)[:, None, :], jnp.sin(angle)[:, None, :])

def apply_rotary(value_tensor, cosine_lookup, sine_lookup):
    half_width = value_tensor.shape[-1] // 2
    first_half = value_tensor[..., :half_width]
    second_half = value_tensor[..., half_width:]
    return jnp.concatenate([first_half * cosine_lookup - second_half * sine_lookup, second_half * cosine_lookup + first_half * sine_lookup], axis=-1)

def block_slots(route_pairs, rank_pairs):
    pair_count = route_pairs.shape[0]
    ordering = jnp.zeros((pair_count,), jnp.int32).at[rank_pairs].set(jnp.arange(pair_count, dtype=jnp.int32))
    ordered = route_pairs[ordering]
    onehot = (ordered[:, None] == jnp.arange(EXPERTS, dtype=jnp.int32)[None, :]).astype(jnp.int32)
    before = jnp.cumsum(onehot, axis=0) - onehot
    slot_ordered = lax.optimization_barrier(jnp.sum(before * onehot, axis=1))
    return slot_ordered[rank_pairs]

def reference(tokens, cotangent, segment_ids, routes, fill_rank, query_weight, key_projection_weight, value_projection_weight, output_weight, router_weight, gain_attention, gain_experts, gate_weight, up_weight, down_weight):
    block_count = SEQS * N_CONTEXT
    pair_count = TOK_DEV * TOP
    token_total = SEQS * SEQUENCE_TOKENS
    route_blocks = routes.reshape(block_count, pair_count).astype(jnp.int32)
    rank_blocks = fill_rank.reshape(block_count, pair_count).astype(jnp.int32)
    slot_number = jax.vmap(block_slots)(route_blocks, rank_blocks)
    kept = slot_number < CAP
    block_index = jnp.arange(block_count, dtype=jnp.int32)[:, None]
    pair_index = jnp.arange(pair_count, dtype=jnp.int32)[None, :]
    token_global = block_index * TOK_DEV + pair_index // TOP
    slot_global = route_blocks * (block_count * CAP) + block_index * CAP + slot_number
    destination = jnp.where(kept, slot_global, EXPERTS * block_count * CAP).astype(jnp.int32)
    slot_token = jnp.full((EXPERTS * block_count * CAP,), token_total, jnp.int32)
    slot_token = slot_token.at[destination.reshape(-1)].set(token_global.reshape(-1).astype(jnp.int32), mode='drop')
    slot_token = slot_token.reshape(EXPERTS, block_count * CAP)
    pair_slot = jnp.where(kept, slot_global, 0).reshape(token_total, TOP).astype(jnp.int32)
    pair_kept = kept.reshape(token_total, TOP).astype(jnp.float32)
    token_routes = routes.reshape(token_total, TOP).astype(jnp.int32)
    positions = jnp.arange(SEQUENCE_TOKENS, dtype=jnp.int32)
    cosine_lookup, sine_lookup = rope_tables(positions, HEAD_SIZE)
    query_group_size = QUERY_HEADS // KEY_VALUE_HEADS
    score_scale = 1.0 / math.sqrt(HEAD_SIZE)
    query_block = min(512, SEQUENCE_TOKENS)
    query_blocks = SEQUENCE_TOKENS // query_block

    def attend_sequence(residual, segments, query_w, key_w, value_w, output_w, gain_a):
        normed = low(rms_norm(residual, gain_a))
        query_unrotated = low_back(highest(normed, query_w))
        key_unrotated = low_back(highest(normed, key_w))
        value_low = low(low_back(highest(normed, value_w))).reshape(SEQUENCE_TOKENS, KEY_VALUE_HEADS, HEAD_SIZE)
        query_rotated = low(apply_rotary(query_unrotated.reshape(SEQUENCE_TOKENS, QUERY_HEADS, HEAD_SIZE), cosine_lookup, sine_lookup)).reshape(SEQUENCE_TOKENS, KEY_VALUE_HEADS, query_group_size, HEAD_SIZE)
        key_rotated = low(apply_rotary(key_unrotated.reshape(SEQUENCE_TOKENS, KEY_VALUE_HEADS, HEAD_SIZE), cosine_lookup, sine_lookup))

        def query_part(part_item):
            query_rows, row_positions, row_segments = part_item
            scores = jnp.einsum('qngd,knd->ngqk', query_rows, key_rotated, precision=lax.Precision.HIGHEST) * score_scale
            scores = low_back(scores)
            allowed = (positions[None, :] <= row_positions[:, None]) & (segments[None, :] == row_segments[:, None])
            scores = jnp.where(allowed[None, None], scores, masked_fill_value)
            weight_bundle = low(jax.nn.softmax(scores, axis=-1))
            return jnp.einsum('rhom,mru->orhu', weight_bundle, value_low, precision=lax.Precision.HIGHEST)
        combined_heads = lax.map(jax.checkpoint(query_part), (query_rotated.reshape(query_blocks, query_block, KEY_VALUE_HEADS, query_group_size, HEAD_SIZE), positions.reshape(query_blocks, query_block), segments.reshape(query_blocks, query_block)))
        combined_heads = low(low_back(combined_heads.reshape(SEQUENCE_TOKENS, QUERY_HEADS * HEAD_SIZE)))
        return residual + low_back(highest(combined_heads, output_w))

    def forward(residual, query_w, key_w, value_w, output_w, router_w, gain_a, gain_e, gate_w, up_w, down_w):

        def one_sequence(sequence_item):
            return attend_sequence(sequence_item[0], sequence_item[1], query_w, key_w, value_w, output_w, gain_a)
        hidden = lax.map(jax.checkpoint(one_sequence), (residual, segment_ids)).reshape(token_total, MODEL_WIDTH)
        normed = rms_norm(hidden, gain_e)
        rounded = low(normed)
        padded = jnp.concatenate([rounded, jnp.zeros((1, MODEL_WIDTH), jnp.float32)], axis=0)
        logits = highest(normed, router_w)
        chosen = jnp.take_along_axis(logits, token_routes, axis=1)
        weight_bundle = jax.nn.softmax(chosen, axis=-1)

        def one_expert(expert_item):
            tokens_of_slots, gate_e, up_e, down_e = expert_item
            inputs = low_back(padded[tokens_of_slots])
            gate_pre = low_back(highest(inputs, gate_e))
            up_pre = low_back(highest(inputs, up_e))
            hidden_e = low(jax.nn.silu(gate_pre) * up_pre)
            projected = lax.dot_general(hidden_e, down_e, (((1,), (1,)), ((), ())), precision=lax.Precision.HIGHEST, preferred_element_type=jnp.float32)
            return low(low_back(projected))
        outputs = lax.map(jax.checkpoint(one_expert), (slot_token, gate_w, up_w, down_w)).reshape(EXPERTS * block_count * CAP, MODEL_WIDTH)
        mixture = jnp.zeros((token_total, MODEL_WIDTH), jnp.float32)
        for route_index in range(TOP):
            scale_column = weight_bundle[:, route_index] * pair_kept[:, route_index]
            mixture = mixture + scale_column[:, None] * outputs[pair_slot[:, route_index]]
        return (hidden + mixture).reshape(SEQS, SEQUENCE_TOKENS, MODEL_WIDTH)
    primals = (tokens.astype(jnp.float32), query_weight.astype(jnp.float32), key_projection_weight.astype(jnp.float32), value_projection_weight.astype(jnp.float32), output_weight.astype(jnp.float32), router_weight.astype(jnp.float32), gain_attention.astype(jnp.float32), gain_experts.astype(jnp.float32), gate_weight.astype(jnp.float32), up_weight.astype(jnp.float32), down_weight.astype(jnp.float32))
    result, pullback = jax.vjp(forward, *primals)
    grads = pullback(cotangent.astype(jnp.float32))
    return (result.astype(jnp.bfloat16), grads[0].astype(jnp.bfloat16), grads[1], grads[2], grads[3], grads[4], grads[5], grads[6], grads[7], grads[8], grads[9], grads[10])
```

```python
import functools
import math

import jax
import jax.numpy as jnp
from jax import lax
from jax.experimental import pallas as pl
from jax.experimental.pallas import tpu as pltpu
from jax.sharding import PartitionSpec as P

MODEL_WIDTH = 1536
QUERY_HEADS = 12
KEY_VALUE_HEADS = 2
HEAD_SIZE = 128
TOP = 4
GROUP = QUERY_HEADS // KEY_VALUE_HEADS
norm_eps = 1e-06
rope_base = 10000.0
NEG = -1e30
SCALE = 1.0 / math.sqrt(HEAD_SIZE)
BF = jnp.bfloat16
F32 = jnp.float32
VMEM_LIMIT = 60 * 1024 * 1024


def mm(a, b):
    return jnp.dot(a, b, preferred_element_type=F32)


def mm_nt(a, b):
    return lax.dot_general(a, b, (((1,), (1,)), ((), ())), preferred_element_type=F32)


def mm_tn(a, b):
    return lax.dot_general(a, b, (((0,), (0,)), ((), ())), preferred_element_type=F32)


def precise_dims(a, b, dims):
    return lax.dot_general(
        a, b, (dims, ((), ())), precision=lax.Precision.HIGHEST, preferred_element_type=F32
    )


def inverse_root(v):
    return lax.rsqrt(jnp.mean(v * v, axis=-1, keepdims=True) + norm_eps)


def norm_back(v, root, gain, upstream):
    scaled = upstream * gain
    cubed = root * root * root
    return root * scaled - v * cubed * jnp.mean(v * scaled, axis=-1, keepdims=True)


def rope_tables(positions):
    half = HEAD_SIZE // 2
    frequency = jnp.exp(
        -(jnp.arange(half, dtype=F32) * (2.0 / HEAD_SIZE)) * math.log(rope_base)
    )
    angle = positions.astype(F32)[:, None] * frequency[None, :]
    return jnp.cos(angle), jnp.sin(angle)


def apply_rotary(v, cosine, sine, direction):
    half = HEAD_SIZE // 2
    a, b = v[..., :half], v[..., half:]
    c, s = cosine[:, None, :], sine[:, None, :]
    return jnp.concatenate([a * c - direction * b * s, b * c + direction * a * s], axis=-1)


def fold_rows(v, op):
    rows, cols = v.shape
    return op(v.reshape(rows // 8, 8, cols), axis=0)


def make_bias(ctx, tokens, segk_ref, segq_ref, bias_ref):
    length = segk_ref.shape[0]
    key_pos = lax.broadcasted_iota(jnp.int32, (length, tokens), 0)
    query_pos = lax.broadcasted_iota(jnp.int32, (length, tokens), 1) + ctx * tokens
    same = segk_ref[...] == segq_ref[...]
    bias_ref[...] = jnp.where(same & (key_pos <= query_pos), 0.0, NEG)


def attn_fwd_kernel(kb, tq, meta, q_ref, k_ref, v_ref, segk_ref, segq_ref, o_ref, lse_ref,
                    bias_ref, s_ref, vt_ref):
    head = pl.program_id(0)
    tokens = q_ref.shape[0]

    @pl.when(head == 0)
    def _():
        make_bias(meta[0], tokens, segk_ref, segq_ref, bias_ref)

    @pl.when(lax.rem(head, GROUP) == 0)
    def _():
        vt_ref[...] = v_ref[...].astype(F32).T.astype(BF)

    for part in range(tokens // tq):
        cols = pl.ds(part * tq, tq)
        q = q_ref[cols, :]
        low, high = meta[1 + 2 * part], meta[2 + 2 * part]

        def score(i, top):
            rows = pl.ds(pl.multiple_of(i * kb, kb), kb)
            s = mm_nt(k_ref[rows, :], q) * SCALE + bias_ref[rows, cols]
            s_ref[rows, :] = s
            return jnp.maximum(top, fold_rows(s, jnp.max))

        top = lax.fori_loop(low, high, score, jnp.full((8, tq), NEG, F32))
        top = jnp.max(top, axis=0, keepdims=True)

        def value(i, carry):
            total, out = carry
            rows = pl.ds(pl.multiple_of(i * kb, kb), kb)
            p = jnp.exp(s_ref[rows, :] - top)
            total = total + fold_rows(p, jnp.sum)
            return total, out + mm(vt_ref[:, rows], p.astype(BF))

        total, out = lax.fori_loop(
            low, high, value, (jnp.zeros((8, tq), F32), jnp.zeros((HEAD_SIZE, tq), F32))
        )
        total = jnp.sum(total, axis=0, keepdims=True)
        o_ref[cols, :] = (out / total).T.astype(BF)
        lse_ref[0, :, cols] = top + jnp.log(total)


def attn_bwd_kernel(kb, tq, meta, q_ref, k_ref, v_ref, do_ref, lse_ref, cos_ref, sin_ref,
                    segk_ref, segq_ref, dq_ref, dk_ref, dv_ref,
                    bias_ref, p_ref, dp_ref, kt_ref, dk_acc, dv_acc):
    head = pl.program_id(0)
    tokens = q_ref.shape[0]

    @pl.when(head == 0)
    def _():
        make_bias(meta[0], tokens, segk_ref, segq_ref, bias_ref)

    @pl.when(lax.rem(head, GROUP) == 0)
    def _():
        kt_ref[...] = k_ref[...].astype(F32).T.astype(BF)
        dk_acc[...] = jnp.zeros_like(dk_acc)
        dv_acc[...] = jnp.zeros_like(dv_acc)

    for part in range(tokens // tq):
        cols = pl.ds(part * tq, tq)
        q = q_ref[cols, :]
        do = do_ref[cols, :]
        lse = lse_ref[0, :, cols]
        low, high = meta[1 + 2 * part], meta[2 + 2 * part]

        def score(i, delta):
            rows = pl.ds(pl.multiple_of(i * kb, kb), kb)
            s = mm_nt(k_ref[rows, :], q) * SCALE + bias_ref[rows, cols]
            p = jnp.exp(s - lse)
            dp = mm_nt(v_ref[rows, :], do)
            p_ref[rows, :] = p
            dp_ref[rows, :] = dp
            return delta + fold_rows(p * dp, jnp.sum)

        delta = lax.fori_loop(low, high, score, jnp.zeros((8, tq), F32))
        delta = jnp.sum(delta, axis=0, keepdims=True)

        def grads(i, dq):
            rows = pl.ds(pl.multiple_of(i * kb, kb), kb)
            p = p_ref[rows, :]
            ds = (p * (dp_ref[rows, :] - delta)).astype(BF)
            dv_acc[rows, :] += mm(p.astype(BF), do)
            dk_acc[rows, :] += mm(ds, q)
            return dq + mm(kt_ref[:, rows], ds)

        dq = lax.fori_loop(low, high, grads, jnp.zeros((HEAD_SIZE, tq), F32))
        dq = dq.T * SCALE
        turned = pltpu.roll(dq, HEAD_SIZE // 2, 1)
        dq_ref[cols, :] = (dq * cos_ref[cols, :] - turned * sin_ref[cols, :]).astype(BF)

    @pl.when(lax.rem(head, GROUP) == GROUP - 1)
    def _():
        dk_ref[...] = (dk_acc[...] * SCALE).astype(BF)
        dv_ref[...] = dv_acc[...].astype(BF)


def attention_sizes(tokens, length):
    tq = 256 if tokens % 256 == 0 else tokens
    kb = 256 if length % 256 == 0 else 128
    return tq, kb


def attention_meta(ctx, tokens, segments, tq, kb):
    entries = [ctx]
    for part in range(tokens // tq):
        first = ctx * tokens + part * tq
        own = lax.dynamic_slice_in_dim(segments, first, 1)
        start = jnp.sum((segments < own).astype(jnp.int32))
        entries += [start // kb, (first + tq + kb - 1) // kb]
    return jnp.stack(entries).astype(jnp.int32)


def attention_forward(q, k, v, meta, segk, segq):
    tokens, length = q.shape[0], k.shape[0]
    tq, kb = attention_sizes(tokens, length)
    const = lambda h, m: (0, 0)
    return pl.pallas_call(
        functools.partial(attn_fwd_kernel, kb, tq),
        out_shape=(
            jax.ShapeDtypeStruct(q.shape, BF),
            jax.ShapeDtypeStruct((QUERY_HEADS, 1, tokens), F32),
        ),
        grid_spec=pltpu.PrefetchScalarGridSpec(
            num_scalar_prefetch=1,
            grid=(QUERY_HEADS,),
            in_specs=[
                pl.BlockSpec((tokens, HEAD_SIZE), lambda h, m: (0, h)),
                pl.BlockSpec((length, HEAD_SIZE), lambda h, m: (0, h // GROUP)),
                pl.BlockSpec((length, HEAD_SIZE), lambda h, m: (0, h // GROUP)),
                pl.BlockSpec((length, 1), const),
                pl.BlockSpec((1, tokens), const),
            ],
            out_specs=[
                pl.BlockSpec((tokens, HEAD_SIZE), lambda h, m: (0, h)),
                pl.BlockSpec((1, 1, tokens), lambda h, m: (h, 0, 0)),
            ],
            scratch_shapes=[
                pltpu.VMEM((length, tokens), F32),
                pltpu.VMEM((length, tq), F32),
                pltpu.VMEM((HEAD_SIZE, length), BF),
            ],
        ),
        compiler_params=pltpu.CompilerParams(vmem_limit_bytes=VMEM_LIMIT),
        cost_estimate=pl.CostEstimate(
            flops=3 * QUERY_HEADS * tokens * length * HEAD_SIZE,
            transcendentals=QUERY_HEADS * tokens * length,
            bytes_accessed=4 * tokens * MODEL_WIDTH,
        ),
        name="attn_fwd",
    )(meta, q, k, v, segk, segq)


def attention_backward(q, k, v, do, lse, cos, sin, meta, segk, segq):
    tokens, length = q.shape[0], k.shape[0]
    tq, kb = attention_sizes(tokens, length)
    const = lambda h, m: (0, 0)
    by_head = lambda h, m: (0, h)
    by_group = lambda h, m: (0, h // GROUP)
    return pl.pallas_call(
        functools.partial(attn_bwd_kernel, kb, tq),
        out_shape=(
            jax.ShapeDtypeStruct(q.shape, BF),
            jax.ShapeDtypeStruct(k.shape, BF),
            jax.ShapeDtypeStruct(v.shape, BF),
        ),
        grid_spec=pltpu.PrefetchScalarGridSpec(
            num_scalar_prefetch=1,
            grid=(QUERY_HEADS,),
            in_specs=[
                pl.BlockSpec((tokens, HEAD_SIZE), by_head),
                pl.BlockSpec((length, HEAD_SIZE), by_group),
                pl.BlockSpec((length, HEAD_SIZE), by_group),
                pl.BlockSpec((tokens, HEAD_SIZE), by_head),
                pl.BlockSpec((1, 1, tokens), lambda h, m: (h, 0, 0)),
                pl.BlockSpec((tokens, HEAD_SIZE), const),
                pl.BlockSpec((tokens, HEAD_SIZE), const),
                pl.BlockSpec((length, 1), const),
                pl.BlockSpec((1, tokens), const),
            ],
            out_specs=[
                pl.BlockSpec((tokens, HEAD_SIZE), by_head),
                pl.BlockSpec((length, HEAD_SIZE), by_group),
                pl.BlockSpec((length, HEAD_SIZE), by_group),
            ],
            scratch_shapes=[
                pltpu.VMEM((length, tokens), F32),
                pltpu.VMEM((length, tq), F32),
                pltpu.VMEM((length, tq), F32),
                pltpu.VMEM((HEAD_SIZE, length), BF),
                pltpu.VMEM((length, HEAD_SIZE), F32),
                pltpu.VMEM((length, HEAD_SIZE), F32),
            ],
        ),
        compiler_params=pltpu.CompilerParams(vmem_limit_bytes=VMEM_LIMIT),
        cost_estimate=pl.CostEstimate(
            flops=8 * QUERY_HEADS * tokens * length * HEAD_SIZE,
            transcendentals=QUERY_HEADS * tokens * length,
            bytes_accessed=8 * tokens * MODEL_WIDTH,
        ),
        name="attn_bwd",
    )(meta, q, k, v, do, lse, cos, sin, segk, segq)


def expert_kernel(cap, tile, x_ref, cot_ref, srow_ref, scol_ref, grow_ref,
                  gate_ref, up_ref, down_ref,
                  py_ref, pdn_ref, dw_ref, xs_ref, dy_ref, hb_ref, dg_ref, du_ref,
                  pick_ref, put_ref, cg_ref, ys_ref, acc_ref):
    local = gate_ref.shape[0]
    tokens, width = x_ref.shape[1], x_ref.shape[2]
    hidden = gate_ref.shape[2]
    weights = []
    spread = lax.broadcasted_iota(jnp.int32, (tokens, local * cap), 1)
    put = None
    for e in range(local):
        slot = lax.broadcasted_iota(jnp.int32, (cap, tokens), 0)
        hit = slot == srow_ref[0, e : e + 1, :]
        pick_ref[pl.ds(e * cap, cap), :] = jnp.where(hit, 1.0, 0.0).astype(BF)
        weights.append(
            jnp.sum(jnp.where(hit, grow_ref[0, e : e + 1, :], 0.0), axis=1, keepdims=True)
        )
        own = scol_ref[0, :, e : e + 1]
        here = spread == jnp.where(own < 0, -1, own + e * cap)
        put = here if put is None else put | here
    put_ref[...] = jnp.where(put, 1.0, 0.0).astype(BF)

    def gather(j, _):
        cols = pl.ds(pl.multiple_of(j * tile, tile), tile)
        xs = mm(pick_ref[...], x_ref[0, :, cols]).astype(BF)
        cg = mm(pick_ref[...], cot_ref[0, :, cols])
        cg_ref[:, cols] = cg.astype(BF)
        for e in range(local):
            rows = slice(e * cap, (e + 1) * cap)
            xs_ref[0, e, :, cols] = xs[rows]
            dy_ref[0, e, :, cols] = (weights[e] * cg[rows]).astype(BF)
        return 0

    lax.fori_loop(0, width // tile, gather, 0)

    def middle(j, _):
        cols = pl.ds(pl.multiple_of(j * tile, tile), tile)
        for e in range(local):
            g = mm(xs_ref[0, e], gate_ref[e, :, cols])
            u = mm(xs_ref[0, e], up_ref[e, :, cols])
            dh = mm(dy_ref[0, e], down_ref[e, :, cols])
            s = 1.0 / (1.0 + jnp.exp(-g))
            act = g * s
            hb_ref[0, e, :, cols] = (act * u).astype(BF)
            dg_ref[0, e, :, cols] = (dh * u * (s * (1.0 + g * (1.0 - s)))).astype(BF)
            du_ref[0, e, :, cols] = (dh * act).astype(BF)
        return 0

    lax.fori_loop(0, hidden // tile, middle, 0)

    acc_ref[...] = jnp.zeros_like(acc_ref)

    def finish(j, _):
        cols = pl.ds(pl.multiple_of(j * tile, tile), tile)
        for e in range(local):
            rows = pl.ds(e * cap, cap)
            y = mm_nt(hb_ref[0, e], down_ref[e, cols, :])
            acc_ref[rows, :] += cg_ref[rows, cols].astype(F32) * y
            ys_ref[rows, :] = (weights[e] * y).astype(BF)
        py_ref[0, :, cols] = mm(put_ref[...], ys_ref[...]).astype(BF)
        for e in range(local):
            rows = pl.ds(e * cap, cap)
            dxs = mm_nt(dg_ref[0, e], gate_ref[e, cols, :])
            dxs = dxs + mm_nt(du_ref[0, e], up_ref[e, cols, :])
            ys_ref[rows, :] = dxs.astype(BF)
        pdn_ref[0, :, cols] = mm(put_ref[...], ys_ref[...]).astype(BF)
        return 0

    lax.fori_loop(0, width // tile, finish, 0)
    for e in range(local):
        dot = jnp.sum(acc_ref[pl.ds(e * cap, cap), :], axis=1, keepdims=True)
        slot = lax.broadcasted_iota(jnp.int32, (cap, tokens), 0)
        hit = slot == srow_ref[0, e : e + 1, :]
        dw_ref[0, e : e + 1, :] = jnp.sum(jnp.where(hit, dot, 0.0), axis=0, keepdims=True)


def expert_block(x, cot, srow, scol, grow, gate, up, down, cap):
    n, tokens, width = x.shape
    local, _, hidden = gate.shape
    tile = 256
    by_source = lambda s: (s, 0, 0)
    by_source4 = lambda s: (s, 0, 0, 0)
    const3 = lambda s: (0, 0, 0)
    weight_spec = pl.BlockSpec((local, width, hidden), const3, pipeline_mode=pl.Buffered(1))
    slot_in = lambda d: jax.ShapeDtypeStruct((n, local, cap, d), BF)
    slot_spec = lambda d: pl.BlockSpec((1, local, cap, d), by_source4)
    return pl.pallas_call(
        functools.partial(expert_kernel, cap, tile),
        out_shape=(
            jax.ShapeDtypeStruct((n, tokens, width), BF),
            jax.ShapeDtypeStruct((n, tokens, width), BF),
            jax.ShapeDtypeStruct((n, local, tokens), F32),
            slot_in(width), slot_in(width), slot_in(hidden), slot_in(hidden), slot_in(hidden),
        ),
        grid=(n,),
        in_specs=[
            pl.BlockSpec((1, tokens, width), by_source),
            pl.BlockSpec((1, tokens, width), by_source),
            pl.BlockSpec((1, local, tokens), by_source),
            pl.BlockSpec((1, tokens, local), by_source),
            pl.BlockSpec((1, local, tokens), by_source),
            weight_spec, weight_spec, weight_spec,
        ],
        out_specs=[
            pl.BlockSpec((1, tokens, width), by_source),
            pl.BlockSpec((1, tokens, width), by_source),
            pl.BlockSpec((1, local, tokens), by_source),
            slot_spec(width), slot_spec(width), slot_spec(hidden), slot_spec(hidden),
            slot_spec(hidden),
        ],
        scratch_shapes=[
            pltpu.VMEM((local * cap, tokens), BF),
            pltpu.VMEM((tokens, local * cap), BF),
            pltpu.VMEM((local * cap, width), BF),
            pltpu.VMEM((local * cap, tile), BF),
            pltpu.VMEM((local * cap, tile), F32),
        ],
        compiler_params=pltpu.CompilerParams(vmem_limit_bytes=VMEM_LIMIT),
        cost_estimate=pl.CostEstimate(
            flops=2 * n * local * cap * width * (6 * hidden + 4 * tokens),
            transcendentals=n * local * cap * hidden,
            bytes_accessed=2 * (4 * n * tokens * width + 3 * local * width * hidden),
        ),
        name="experts",
    )(x, cot, srow, scol, grow, gate, up, down)


def expert_grad_kernel(xs_ref, dy_ref, hb_ref, dg_ref, du_ref, out_ref):
    n, _, cap, tile = xs_ref.shape
    hidden = hb_ref.shape[3]
    flat = lambda ref: ref[...].reshape(n * cap, ref.shape[3])
    xs = flat(xs_ref)
    out_ref[0, :, 0:hidden] = mm_tn(xs, flat(dg_ref)).astype(BF)
    out_ref[0, :, hidden : 2 * hidden] = mm_tn(xs, flat(du_ref)).astype(BF)
    out_ref[0, :, 2 * hidden : 3 * hidden] = mm_tn(flat(dy_ref), flat(hb_ref)).astype(BF)


def expert_grads(xs, dy, hb, dg, du):
    n, local, cap, width = xs.shape
    hidden = hb.shape[3]
    tile = 256
    wide = pl.BlockSpec((n, 1, cap, tile), lambda e, j: (0, e, 0, j))
    deep = pl.BlockSpec((n, 1, cap, hidden), lambda e, j: (0, e, 0, 0))
    return pl.pallas_call(
        expert_grad_kernel,
        out_shape=jax.ShapeDtypeStruct((local, width, 3 * hidden), BF),
        grid=(local, width // tile),
        in_specs=[wide, wide, deep, deep, deep],
        out_specs=pl.BlockSpec((1, tile, 3 * hidden), lambda e, j: (e, j, 0)),
        compiler_params=pltpu.CompilerParams(vmem_limit_bytes=VMEM_LIMIT),
        cost_estimate=pl.CostEstimate(
            flops=6 * n * local * cap * width * hidden,
            transcendentals=0,
            bytes_accessed=2 * n * local * cap * (2 * width + 3 * hidden),
        ),
        name="expert_grads",
    )(xs, dy, hb, dg, du)


def body(
    tokens, cotangent, segment_ids, routes, fill_rank, query_weight, key_projection_weight,
    value_projection_weight, output_weight, router_weight, gain_attention, gain_experts,
    gate_weight, up_weight, down_weight,
):
    context_index = lax.axis_index("context")
    expert_size = lax.axis_size("expert")
    expert_index = lax.axis_index("expert")
    rows = tokens.shape[1]
    length = segment_ids.shape[1]
    kv_width = KEY_VALUE_HEADS * HEAD_SIZE
    gather = lambda w: lax.all_gather(w, "context", axis=0, tiled=True)

    upstream_low = cotangent[0]
    cot_all = lax.all_gather(upstream_low, "expert", axis=0)

    expert_count = router_weight.shape[1]
    local = gate_weight.shape[0]
    capacity = 5 * rows * TOP // (4 * expert_count)
    cap = -(-capacity // 64) * 64
    names = jnp.arange(expert_count, dtype=jnp.int32)
    route_hit = routes[0][:, :, None] == names[None, None, :]
    routed = jnp.any(route_hit, axis=1)
    ranks = fill_rank[0, 0].reshape(rows, TOP)
    order = jnp.sum(jnp.where(route_hit, ranks[:, :, None], 0), axis=1)
    order = jnp.where(routed, order, rows * TOP).T
    slots = jnp.sum((order[:, :, None] < order[:, None, :]).astype(jnp.int32), axis=1)
    kept = routed.T & (slots < capacity)
    slots = jnp.where(kept, slots, -1)
    slots_all = lax.all_gather(slots, "expert", axis=0)
    slots_mine = lax.dynamic_slice_in_dim(slots_all, expert_index * local, local, axis=1)
    kept_float = kept.T.astype(F32)

    query_full, key_full, value_full, output_full, router_full, gain_first, gain_second = (
        gather(query_weight), gather(key_projection_weight), gather(value_projection_weight),
        gather(output_weight), gather(router_weight), gather(gain_attention), gather(gain_experts),
    )
    router_float = router_full.astype(F32)
    gain_first = gain_first.astype(F32)
    gain_second = gain_second.astype(F32)
    residual = tokens[0].astype(F32)
    root_first = inverse_root(residual)
    attn_input = (residual * root_first * gain_first).astype(BF)
    positions = context_index * rows + jnp.arange(rows, dtype=jnp.int32)
    cosine, sine = rope_tables(positions)
    cos_full = jnp.concatenate([cosine, cosine], axis=-1)
    sin_full = jnp.concatenate([-sine, sine], axis=-1)
    turn = lambda v, heads, d: apply_rotary(
        v.reshape(rows, heads, HEAD_SIZE), cosine, sine, d
    ).reshape(rows, heads * HEAD_SIZE)
    q = turn(mm(attn_input, query_full), QUERY_HEADS, 1.0).astype(BF)
    k_own = turn(mm(attn_input, key_full), KEY_VALUE_HEADS, 1.0).astype(BF)
    v_own = mm(attn_input, value_full).astype(BF)
    kv = gather(jnp.concatenate([k_own, v_own], axis=1))
    k_all, v_all = kv[:, :kv_width], kv[:, kv_width:]
    segments = segment_ids[0]
    tq, kb = attention_sizes(rows, length)
    meta = attention_meta(context_index, rows, segments, tq, kb)
    segk = segments[:, None]
    segq = lax.dynamic_slice_in_dim(segments, context_index * rows, rows)[None, :]
    mixed, lse = attention_forward(q, k_all, v_all, meta, segk, segq)

    hidden = residual + mm(mixed, output_full)
    root_second = inverse_root(hidden)
    normed = hidden * root_second * gain_second
    expert_input = normed.astype(BF)
    logits = precise_dims(normed, router_float, ((1,), (0,)))
    gates = jax.nn.softmax(jnp.where(routed, logits, -jnp.inf), axis=-1)
    kept_gates = gates * kept_float

    x_all = lax.all_gather(expert_input, "expert", axis=0)
    gates_all = lax.all_gather(kept_gates.T, "expert", axis=0)
    gates_mine = lax.dynamic_slice_in_dim(gates_all, expert_index * local, local, axis=1)
    part_y, part_dn, dw, xs, dy, hb, dg, du = expert_block(
        x_all, cot_all, slots_mine, slots_mine.transpose(0, 2, 1), gates_mine,
        gate_weight, up_weight, down_weight, cap,
    )
    scatter = lambda v: lax.psum_scatter(v, "expert", scatter_dimension=0, tiled=False)
    dn_low = scatter(part_dn)
    dw_back = lax.all_to_all(dw, "expert", split_axis=0, concat_axis=0, tiled=True)
    gate_dot = dw_back.reshape(expert_count, rows).T * kept_float
    grads_low = expert_grads(xs, dy, hb, dg, du)
    grads_shard = lax.psum_scatter(
        grads_low, ("dp", "context"), scatter_dimension=1, tiled=True
    ).astype(F32)
    ff = gate_weight.shape[2]
    gate_grad, up_grad, down_grad = (grads_shard[:, :, i * ff : (i + 1) * ff] for i in range(3))
    mixture = scatter(part_y)
    layer_out = (hidden + mixture.astype(F32)).astype(BF)

    upstream = upstream_low.astype(F32)
    logit_grad = gates * (gate_dot - jnp.sum(gates * gate_dot, axis=-1, keepdims=True))
    normed_grad = dn_low.astype(F32) + precise_dims(logit_grad, router_float, ((1,), (1,)))
    router_local = precise_dims(normed, logit_grad, ((0,), (0,)))
    hidden_total = upstream + norm_back(hidden, root_second, gain_second, normed_grad)
    gain_second_grad = jnp.sum(normed_grad * hidden * root_second, axis=0)
    attn_grad_low = hidden_total.astype(BF)
    output_local = mm_tn(mixed, attn_grad_low)
    mixed_grad_low = mm_nt(attn_grad_low, output_full).astype(BF)

    dq_low, dk_part, dv_part = attention_backward(
        q, k_all, v_all, mixed_grad_low, lse, cos_full, sin_full, meta, segk, segq
    )
    dkv = lax.psum_scatter(
        jnp.concatenate([dk_part, dv_part], axis=1), "context", scatter_dimension=0, tiled=True
    )
    dk_low = turn(dkv[:, :kv_width].astype(F32), KEY_VALUE_HEADS, -1.0).astype(BF)
    dv_low = dkv[:, kv_width:]
    input_total = mm_nt(dq_low, query_full) + mm_nt(dk_low, key_full) + mm_nt(dv_low, value_full)
    query_local = mm_tn(attn_input, dq_low)
    key_local = mm_tn(attn_input, dk_low)
    value_local = mm_tn(attn_input, dv_low)
    grad_tokens = (hidden_total + norm_back(residual, root_first, gain_first, input_total)).astype(BF)
    gain_first_grad = jnp.sum(input_total * residual * root_first, axis=0)

    reduce_rows = lambda v: lax.psum(
        lax.psum_scatter(v.astype(BF), "context", scatter_dimension=0, tiled=True), ("dp", "expert")
    ).astype(F32)
    return (
        layer_out[None], grad_tokens[None],
        reduce_rows(query_local), reduce_rows(key_local), reduce_rows(value_local),
        reduce_rows(output_local), reduce_rows(router_local),
        reduce_rows(gain_first_grad), reduce_rows(gain_second_grad),
        gate_grad, up_grad, down_grad,
    )


def solution(mesh):
    both = ("dp", "expert")
    token_spec = P(both, "context", None)
    row_spec = P("context", None)
    expert_out = P("expert", ("dp", "context"), None)
    return jax.shard_map(
        body,
        mesh=mesh,
        in_specs=(
            token_spec, token_spec, P(both, None), token_spec, token_spec,
            row_spec, row_spec, row_spec, row_spec, row_spec, P("context"), P("context"),
            P("expert", None, None), P("expert", None, None), P("expert", None, None),
        ),
        out_specs=(
            token_spec, token_spec, row_spec, row_spec, row_spec, row_spec, row_spec,
            P("context"), P("context"), expert_out, expert_out, expert_out,
        ),
        check_vma=False,
    )
```

```python
import functools
import math

import jax
import jax.numpy as jnp
from jax import lax
from jax.experimental import pallas as pl
from jax.experimental.pallas import tpu as pltpu
from jax.sharding import PartitionSpec as P

MODEL_WIDTH = 1536
QUERY_HEADS = 12
KEY_VALUE_HEADS = 2
HEAD_SIZE = 128
TOP = 4
GROUP = QUERY_HEADS // KEY_VALUE_HEADS
norm_eps = 1e-06
rope_base = 10000.0
NEG = -1e30
SCALE = 1.0 / math.sqrt(HEAD_SIZE)
BF = jnp.bfloat16
F32 = jnp.float32
VMEM_LIMIT = 60 * 1024 * 1024
MOE_VMEM = 63 * 1024 * 1024


def mm(a, b):
    return jnp.dot(a, b, preferred_element_type=F32)


def mm_nt(a, b):
    return lax.dot_general(a, b, (((1,), (1,)), ((), ())), preferred_element_type=F32)


def mm_tn(a, b):
    return lax.dot_general(a, b, (((0,), (0,)), ((), ())), preferred_element_type=F32)


def precise_dims(a, b, dims):
    return lax.dot_general(
        a, b, (dims, ((), ())), precision=lax.Precision.HIGHEST, preferred_element_type=F32
    )


def inverse_root(v):
    return lax.rsqrt(jnp.mean(v * v, axis=-1, keepdims=True) + norm_eps)


def norm_back(v, root, gain, upstream):
    scaled = upstream * gain
    cubed = root * root * root
    return root * scaled - v * cubed * jnp.mean(v * scaled, axis=-1, keepdims=True)


def rope_tables(positions):
    half = HEAD_SIZE // 2
    frequency = jnp.exp(
        -(jnp.arange(half, dtype=F32) * (2.0 / HEAD_SIZE)) * math.log(rope_base)
    )
    angle = positions.astype(F32)[:, None] * frequency[None, :]
    return jnp.cos(angle), jnp.sin(angle)


def apply_rotary(v, cosine, sine, direction):
    half = HEAD_SIZE // 2
    a, b = v[..., :half], v[..., half:]
    c, s = cosine[:, None, :], sine[:, None, :]
    return jnp.concatenate([a * c - direction * b * s, b * c + direction * a * s], axis=-1)


def fold_rows(v, op):
    rows, cols = v.shape
    return op(v.reshape(rows // 8, 8, cols), axis=0)


def make_bias(ctx, tokens, segk_ref, segq_ref, bias_ref):
    length = segk_ref.shape[0]
    key_pos = lax.broadcasted_iota(jnp.int32, (length, tokens), 0)
    query_pos = lax.broadcasted_iota(jnp.int32, (length, tokens), 1) + ctx * tokens
    same = segk_ref[...] == segq_ref[...]
    bias_ref[...] = jnp.where(same & (key_pos <= query_pos), 0.0, NEG)


def attn_fwd_kernel(kb, tq, meta, q_ref, k_ref, v_ref, segk_ref, segq_ref, o_ref, lse_ref,
                    bias_ref, s_ref, vt_ref):
    head = pl.program_id(0)
    tokens = q_ref.shape[0]

    @pl.when(head == 0)
    def _():
        make_bias(meta[0], tokens, segk_ref, segq_ref, bias_ref)

    @pl.when(lax.rem(head, GROUP) == 0)
    def _():
        vt_ref[...] = v_ref[...].astype(F32).T.astype(BF)

    for part in range(tokens // tq):
        cols = pl.ds(part * tq, tq)
        q = q_ref[cols, :]
        low, high = meta[1 + 2 * part], meta[2 + 2 * part]

        def score(i, top):
            rows = pl.ds(pl.multiple_of(i * kb, kb), kb)
            s = mm_nt(k_ref[rows, :], q) * SCALE + bias_ref[rows, cols]
            s_ref[rows, :] = s
            return jnp.maximum(top, fold_rows(s, jnp.max))

        top = lax.fori_loop(low, high, score, jnp.full((8, tq), NEG, F32))
        top = jnp.max(top, axis=0, keepdims=True)

        def value(i, carry):
            total, out = carry
            rows = pl.ds(pl.multiple_of(i * kb, kb), kb)
            p = jnp.exp(s_ref[rows, :] - top)
            total = total + fold_rows(p, jnp.sum)
            return total, out + mm(vt_ref[:, rows], p.astype(BF))

        total, out = lax.fori_loop(
            low, high, value, (jnp.zeros((8, tq), F32), jnp.zeros((HEAD_SIZE, tq), F32))
        )
        total = jnp.sum(total, axis=0, keepdims=True)
        o_ref[cols, :] = (out / total).T.astype(BF)
        lse_ref[0, :, cols] = top + jnp.log(total)


def attn_bwd_kernel(kb, tq, meta, q_ref, k_ref, v_ref, do_ref, lse_ref, cos_ref, sin_ref,
                    segk_ref, segq_ref, dq_ref, dk_ref, dv_ref,
                    bias_ref, p_ref, dp_ref, kt_ref, dk_acc, dv_acc):
    head = pl.program_id(0)
    tokens = q_ref.shape[0]

    @pl.when(head == 0)
    def _():
        make_bias(meta[0], tokens, segk_ref, segq_ref, bias_ref)

    @pl.when(lax.rem(head, GROUP) == 0)
    def _():
        kt_ref[...] = k_ref[...].astype(F32).T.astype(BF)
        dk_acc[...] = jnp.zeros_like(dk_acc)
        dv_acc[...] = jnp.zeros_like(dv_acc)

    for part in range(tokens // tq):
        cols = pl.ds(part * tq, tq)
        q = q_ref[cols, :]
        do = do_ref[cols, :]
        lse = lse_ref[0, :, cols]
        low, high = meta[1 + 2 * part], meta[2 + 2 * part]

        def score(i, delta):
            rows = pl.ds(pl.multiple_of(i * kb, kb), kb)
            s = mm_nt(k_ref[rows, :], q) * SCALE + bias_ref[rows, cols]
            p = jnp.exp(s - lse)
            dp = mm_nt(v_ref[rows, :], do)
            p_ref[rows, :] = p
            dp_ref[rows, :] = dp
            return delta + fold_rows(p * dp, jnp.sum)

        delta = lax.fori_loop(low, high, score, jnp.zeros((8, tq), F32))
        delta = jnp.sum(delta, axis=0, keepdims=True)

        def grads(i, dq):
            rows = pl.ds(pl.multiple_of(i * kb, kb), kb)
            p = p_ref[rows, :]
            ds = (p * (dp_ref[rows, :] - delta)).astype(BF)
            dv_acc[rows, :] += mm(p.astype(BF), do)
            dk_acc[rows, :] += mm(ds, q)
            return dq + mm(kt_ref[:, rows], ds)

        dq = lax.fori_loop(low, high, grads, jnp.zeros((HEAD_SIZE, tq), F32))
        dq = dq.T * SCALE
        turned = pltpu.roll(dq, HEAD_SIZE // 2, 1)
        dq_ref[cols, :] = (dq * cos_ref[cols, :] - turned * sin_ref[cols, :]).astype(BF)

    @pl.when(lax.rem(head, GROUP) == GROUP - 1)
    def _():
        dk_ref[...] = (dk_acc[...] * SCALE).astype(BF)
        dv_ref[...] = dv_acc[...].astype(BF)


def attention_sizes(tokens, length):
    tq = 256 if tokens % 256 == 0 else tokens
    kb = 256 if length % 256 == 0 else 128
    return tq, kb


def attention_meta(ctx, tokens, segments, tq, kb):
    entries = [ctx]
    for part in range(tokens // tq):
        first = ctx * tokens + part * tq
        own = lax.dynamic_slice_in_dim(segments, first, 1)
        start = jnp.sum((segments < own).astype(jnp.int32))
        entries += [start // kb, (first + tq + kb - 1) // kb]
    return jnp.stack(entries).astype(jnp.int32)


def attention_forward(q, k, v, meta, segk, segq):
    tokens, length = q.shape[0], k.shape[0]
    tq, kb = attention_sizes(tokens, length)
    const = lambda h, m: (0, 0)
    return pl.pallas_call(
        functools.partial(attn_fwd_kernel, kb, tq),
        out_shape=(
            jax.ShapeDtypeStruct(q.shape, BF),
            jax.ShapeDtypeStruct((QUERY_HEADS, 1, tokens), F32),
        ),
        grid_spec=pltpu.PrefetchScalarGridSpec(
            num_scalar_prefetch=1,
            grid=(QUERY_HEADS,),
            in_specs=[
                pl.BlockSpec((tokens, HEAD_SIZE), lambda h, m: (0, h)),
                pl.BlockSpec((length, HEAD_SIZE), lambda h, m: (0, h // GROUP)),
                pl.BlockSpec((length, HEAD_SIZE), lambda h, m: (0, h // GROUP)),
                pl.BlockSpec((length, 1), const),
                pl.BlockSpec((1, tokens), const),
            ],
            out_specs=[
                pl.BlockSpec((tokens, HEAD_SIZE), lambda h, m: (0, h)),
                pl.BlockSpec((1, 1, tokens), lambda h, m: (h, 0, 0)),
            ],
            scratch_shapes=[
                pltpu.VMEM((length, tokens), F32),
                pltpu.VMEM((length, tq), F32),
                pltpu.VMEM((HEAD_SIZE, length), BF),
            ],
        ),
        compiler_params=pltpu.CompilerParams(vmem_limit_bytes=VMEM_LIMIT),
        cost_estimate=pl.CostEstimate(
            flops=3 * QUERY_HEADS * tokens * length * HEAD_SIZE,
            transcendentals=QUERY_HEADS * tokens * length,
            bytes_accessed=4 * tokens * MODEL_WIDTH,
        ),
        name="attn_fwd",
    )(meta, q, k, v, segk, segq)


def attention_backward(q, k, v, do, lse, cos, sin, meta, segk, segq):
    tokens, length = q.shape[0], k.shape[0]
    tq, kb = attention_sizes(tokens, length)
    const = lambda h, m: (0, 0)
    by_head = lambda h, m: (0, h)
    by_group = lambda h, m: (0, h // GROUP)
    return pl.pallas_call(
        functools.partial(attn_bwd_kernel, kb, tq),
        out_shape=(
            jax.ShapeDtypeStruct(q.shape, BF),
            jax.ShapeDtypeStruct(k.shape, BF),
            jax.ShapeDtypeStruct(v.shape, BF),
        ),
        grid_spec=pltpu.PrefetchScalarGridSpec(
            num_scalar_prefetch=1,
            grid=(QUERY_HEADS,),
            in_specs=[
                pl.BlockSpec((tokens, HEAD_SIZE), by_head),
                pl.BlockSpec((length, HEAD_SIZE), by_group),
                pl.BlockSpec((length, HEAD_SIZE), by_group),
                pl.BlockSpec((tokens, HEAD_SIZE), by_head),
                pl.BlockSpec((1, 1, tokens), lambda h, m: (h, 0, 0)),
                pl.BlockSpec((tokens, HEAD_SIZE), const),
                pl.BlockSpec((tokens, HEAD_SIZE), const),
                pl.BlockSpec((length, 1), const),
                pl.BlockSpec((1, tokens), const),
            ],
            out_specs=[
                pl.BlockSpec((tokens, HEAD_SIZE), by_head),
                pl.BlockSpec((length, HEAD_SIZE), by_group),
                pl.BlockSpec((length, HEAD_SIZE), by_group),
            ],
            scratch_shapes=[
                pltpu.VMEM((length, tokens), F32),
                pltpu.VMEM((length, tq), F32),
                pltpu.VMEM((length, tq), F32),
                pltpu.VMEM((HEAD_SIZE, length), BF),
                pltpu.VMEM((length, HEAD_SIZE), F32),
                pltpu.VMEM((length, HEAD_SIZE), F32),
            ],
        ),
        compiler_params=pltpu.CompilerParams(vmem_limit_bytes=VMEM_LIMIT),
        cost_estimate=pl.CostEstimate(
            flops=8 * QUERY_HEADS * tokens * length * HEAD_SIZE,
            transcendentals=QUERY_HEADS * tokens * length,
            bytes_accessed=8 * tokens * MODEL_WIDTH,
        ),
        name="attn_bwd",
    )(meta, q, k, v, do, lse, cos, sin, segk, segq)


def remote(src, dst, ss, rs, axis, dev):
    return pltpu.make_async_remote_copy(
        src_ref=src, dst_ref=dst, send_sem=ss, recv_sem=rs, device_id={axis: dev},
        device_id_type=pl.DeviceIdType.MESH,
    )


def moe_kernel(cap, tile, n,
               x_hbm, cot_hbm, cotl_hbm, cotr_hbm, meta_hbm, gate_hbm, up_hbm, down_hbm,
               dn_out, dw_out, py_out, grads_out, xall, cotall,
               gate_ref, up_ref, down_ref, x_ref, cot_ref, metas, xs_ref, dy_ref, hb_ref, dg_ref,
               du_ref, pdn_ref, py_ref, dws, pick_ref, put_ref, ys_ref, acc_ref, stage,
               wsem, lsem, xs_send, xs_recv, cs_send, cs_recv, m_send, m_recv, dn_send, dn_recv,
               dw_send, dw_recv, py_sem, own_sem, st_sem):
    me = lax.axis_index("expert")
    tokens, width = x_ref.shape
    local, _, hidden = gate_ref.shape
    edge = (me == 0) | (me == n - 1)

    barrier = pltpu.get_barrier_semaphore()
    for d in range(1, n):
        pl.semaphore_signal(barrier, inc=1, device_id={"expert": lax.rem(me + d, n)},
                            device_id_type=pl.DeviceIdType.MESH)
    pl.semaphore_wait(barrier, n - 1)

    def exists(direction, step):
        return (me - 1 - step >= 0) if direction == 0 else (me + 1 + step <= n - 1)

    def sends(direction, step):
        if direction == 0:
            return (me - step >= 0) & (me < n - 1)
        return (me + step <= n - 1) & (me > 0)

    def stream(direction, step, own, table, ss, rs, near=None):
        block = me - step if direction == 0 else me + step
        block = jnp.clip(block, 0, n - 1)
        target = jnp.clip(me + 1 if direction == 0 else me - 1, 0, n - 1)
        if step == 0:
            src = own
        elif step == 1 and near is not None:
            src = near[direction]
        else:
            src = table.at[block]
        return remote(src, table.at[block], ss.at[direction, step], rs.at[direction, step],
                      "expert", target)

    xcopy = lambda d, s: stream(d, s, x_hbm, xall, xs_send, xs_recv)
    ccopy = lambda d, s: stream(d, s, cot_hbm, cotall, cs_send, cs_recv, (cotl_hbm, cotr_hbm))

    for d in range(2):
        @pl.when(sends(d, 0))
        def _():
            xcopy(d, 0).start()

    def meta_copy(j):
        return remote(meta_hbm.at[j], metas.at[me], m_send.at[j], m_recv.at[me], "expert", j)

    for j in range(n):
        @pl.when(me != j)
        def _():
            meta_copy(j).start()

    loads = [pltpu.make_async_copy(a, b, wsem.at[k]) for k, (a, b) in enumerate(
        ((gate_hbm, gate_ref), (up_hbm, up_ref), (down_hbm, down_ref)))]
    for load in loads:
        load.start()
    own_meta = pltpu.make_async_copy(meta_hbm.at[me], metas.at[me], lsem.at[2])
    own_meta.start()

    def fetch(a, b):
        cx = pltpu.make_async_copy(a, x_ref, lsem.at[0])
        cc = pltpu.make_async_copy(b, cot_ref, lsem.at[1])
        cx.start()
        cc.start()
        cx.wait()
        cc.wait()

    mirror = me >= 2
    side = jnp.where(mirror, n - 1 - me, me)

    def source_of(p):
        base = jnp.where(p == 0, side, jnp.where(p == 1, 1 - side, p))
        return jnp.where(mirror, n - 1 - base, base)

    def arrive(direction, step):
        @pl.when(exists(direction, step))
        def _():
            xcopy(direction, step).wait_recv()
            if step > 0:
                ccopy(direction, step).wait_recv()

    def forward(direction, step):
        @pl.when(sends(direction, step))
        def _():
            xcopy(direction, step).start()
            ccopy(direction, step).start()

    def one_source(p, _):
        src = source_of(p)

        @pl.when(p == 0)
        def _():
            fetch(x_hbm, cot_hbm)
            own_meta.wait()
            for load in loads:
                load.wait()

        @pl.when(p == 1)
        def _():
            for d in range(2):
                arrive(d, 0)
                forward(d, 1)

        @pl.when(((p == 2) & edge) | ((p == 3) & jnp.logical_not(edge)))
        def _():
            for d in range(2):
                arrive(d, 1)
                forward(d, 2)

        @pl.when((p == 3) & edge)
        def _():
            for d in range(2):
                arrive(d, 2)

        @pl.when((p > 0) & (src == me - 1))
        def _():
            fetch(xall.at[src], cotl_hbm)

        @pl.when((p > 0) & (src == me + 1))
        def _():
            fetch(xall.at[src], cotr_hbm)

        @pl.when((src < me - 1) | (src > me + 1))
        def _():
            fetch(xall.at[src], cotall.at[src])

        @pl.when(p > 0)
        def _():
            remote(meta_hbm.at[src], metas.at[src], m_send.at[src], m_recv.at[src], "expert",
                   src).wait_recv()

        meta = metas[src]
        columns = meta.T
        spread = lax.broadcasted_iota(jnp.int32, (tokens, local * cap), 1).astype(F32)
        slot = lax.broadcasted_iota(jnp.int32, (cap, tokens), 0).astype(F32)
        weights, put = [], None
        for e in range(local):
            hit = slot == meta[e : e + 1, :]
            pick_ref[pl.ds(e * cap, cap), :] = jnp.where(hit, 1.0, 0.0).astype(BF)
            weights.append(
                jnp.sum(jnp.where(hit, meta[local + e : local + e + 1, :], 0.0), axis=1,
                        keepdims=True)
            )
            own = columns[:, e : e + 1]
            here = spread == jnp.where(own < 0.0, -1.0, own + e * cap)
            put = here if put is None else put | here
        put_ref[...] = jnp.where(put, 1.0, 0.0).astype(BF)
        mine = pl.ds(pl.multiple_of(p * cap, cap), cap)
        buf = lax.rem(p, 2)

        def gather(j, _):
            cols = pl.ds(pl.multiple_of(j * tile, tile), tile)
            xs = mm(pick_ref[...], x_ref[:, cols]).astype(BF)
            cg = mm(pick_ref[...], cot_ref[:, cols])
            for e in range(local):
                rows = slice(e * cap, (e + 1) * cap)
                xs_ref[e, mine, cols] = xs[rows]
                dy_ref[e, mine, cols] = (weights[e] * cg[rows]).astype(BF)
            return 0

        lax.fori_loop(0, width // tile, gather, 0)

        def middle(j, _):
            cols = pl.ds(pl.multiple_of(j * tile, tile), tile)
            for e in range(local):
                g = mm(xs_ref[e, mine, :], gate_ref[e, :, cols])
                u = mm(xs_ref[e, mine, :], up_ref[e, :, cols])
                dh = mm(dy_ref[e, mine, :], down_ref[e, :, cols])
                s = 1.0 / (1.0 + jnp.exp(-g))
                act = g * s
                hb_ref[e, mine, cols] = (act * u).astype(BF)
                dg_ref[e, mine, cols] = (dh * u * (s * (1.0 + g * (1.0 - s)))).astype(BF)
                du_ref[e, mine, cols] = (dh * act).astype(BF)
            return 0

        lax.fori_loop(0, hidden // tile, middle, 0)

        @pl.when(p >= 2)
        def _():
            pltpu.make_async_copy(py_ref.at[buf], py_out.at[0], py_sem.at[buf]).wait()
            @pl.when(p == 2)
            def _():
                pltpu.make_async_copy(pdn_ref.at[buf], dn_out.at[me], own_sem.at[0]).wait()
            @pl.when(p == 3)
            def _():
                earlier = source_of(1)
                remote(pdn_ref.at[buf], dn_out.at[me], dn_send.at[earlier], dn_recv.at[me],
                       "expert", earlier).wait_send()

        acc_ref[...] = jnp.zeros_like(acc_ref)

        def back(j, _):
            cols = pl.ds(pl.multiple_of(j * tile, tile), tile)
            for e in range(local):
                dxs = mm_nt(dg_ref[e, mine, :], gate_ref[e, cols, :])
                dxs = dxs + mm_nt(du_ref[e, mine, :], up_ref[e, cols, :])
                ys_ref[pl.ds(e * cap, cap), :] = dxs.astype(BF)
            pdn_ref[buf, :, cols] = mm(put_ref[...], ys_ref[...]).astype(BF)
            return 0

        lax.fori_loop(0, width // tile, back, 0)

        @pl.when(p == 0)
        def _():
            pltpu.make_async_copy(pdn_ref.at[buf], dn_out.at[me], own_sem.at[0]).start()

        @pl.when(p > 0)
        def _():
            remote(pdn_ref.at[buf], dn_out.at[me], dn_send.at[src], dn_recv.at[me], "expert",
                   src).start()

        def ahead(j, _):
            cols = pl.ds(pl.multiple_of(j * tile, tile), tile)
            for e in range(local):
                rows = pl.ds(e * cap, cap)
                y = mm_nt(hb_ref[e, mine, :], down_ref[e, cols, :])
                acc_ref[rows, :] += mm(pick_ref[rows, :], cot_ref[:, cols]) * y
                ys_ref[rows, :] = (weights[e] * y).astype(BF)
            py_ref[buf, :, cols] = mm(put_ref[...], ys_ref[...]).astype(BF)
            return 0

        lax.fori_loop(0, width // tile, ahead, 0)
        pltpu.make_async_copy(py_ref.at[buf], py_out.at[src], py_sem.at[buf]).start()
        dws[p] = jnp.zeros((8, tokens), F32)
        for e in range(local):
            dot = jnp.sum(acc_ref[pl.ds(e * cap, cap), :], axis=1, keepdims=True)
            hit = slot == meta[e : e + 1, :]
            dws[p, e : e + 1, :] = jnp.sum(jnp.where(hit, dot, 0.0), axis=0, keepdims=True)

        @pl.when(p == 0)
        def _():
            pltpu.make_async_copy(dws.at[p], dw_out.at[me], own_sem.at[1]).start()

        @pl.when(p > 0)
        def _():
            remote(dws.at[p], dw_out.at[me], dw_send.at[src], dw_recv.at[me], "expert",
                   src).start()
        return 0

    lax.fori_loop(0, n, one_source, 0)

    tiles = width // tile
    store = lambda k, e, j: pltpu.make_async_copy(
        stage.at[k], grads_out.at[e, pl.ds(pl.multiple_of(j * tile, tile), tile), :], st_sem.at[k])

    def weight_grads(k, _):
        e, j = lax.div(k, tiles), lax.rem(k, tiles)
        cols = pl.ds(pl.multiple_of(j * tile, tile), tile)
        slot_k = lax.rem(k, 2)

        @pl.when(k >= 2)
        def _():
            store(slot_k, 0, 0).wait()

        xs = xs_ref[e, :, cols]
        stage[slot_k, :, 0:hidden] = mm_tn(xs, dg_ref[e]).astype(BF)
        stage[slot_k, :, hidden : 2 * hidden] = mm_tn(xs, du_ref[e]).astype(BF)
        stage[slot_k, :, 2 * hidden : 3 * hidden] = mm_tn(dy_ref[e, :, cols], hb_ref[e]).astype(BF)
        store(slot_k, e, j).start()
        return 0

    lax.fori_loop(0, local * tiles, weight_grads, 0)
    for k in range(2):
        store(k, 0, 0).wait()

    for k in range(2):
        pltpu.make_async_copy(py_ref.at[k], py_out.at[0], py_sem.at[k]).wait()
    pltpu.make_async_copy(dws.at[0], dw_out.at[me], own_sem.at[1]).wait()
    for d in range(2):
        for s in range(n - 1):
            @pl.when(sends(d, s))
            def _():
                xcopy(d, s).wait_send()
                if s > 0:
                    ccopy(d, s).wait_send()
    last = [source_of(p) for p in range(n)]
    for p in (2, 3):
        remote(pdn_ref.at[p % 2], dn_out.at[me], dn_send.at[last[p]], dn_recv.at[me], "expert",
               last[p]).wait_send()
    for j in range(n):
        @pl.when(me != j)
        def _():
            meta_copy(j).wait_send()
            remote(dws.at[0], dw_out.at[me], dw_send.at[j], dw_recv.at[me], "expert",
                   j).wait_send()
            remote(dws.at[0], dw_out.at[j], dw_send.at[j], dw_recv.at[j], "expert", j).wait_recv()
            remote(pdn_ref.at[0], dn_out.at[j], dn_send.at[j], dn_recv.at[j], "expert",
                   j).wait_recv()


def moe(x, cot, cot_left, cot_right, meta, gate, up, down, cap):
    n = meta.shape[0]
    tokens, width = x.shape
    local, _, hidden = gate.shape
    tile = 256
    anywhere = pl.BlockSpec(memory_space=pl.ANY)
    dma = pltpu.SemaphoreType.DMA
    shape = jax.ShapeDtypeStruct
    return pl.pallas_call(
        functools.partial(moe_kernel, cap, tile, n),
        out_shape=(
            shape((n, tokens, width), BF), shape((n, 8, tokens), F32), shape((n, tokens, width), BF),
            shape((local, width, 3 * hidden), BF),
            shape((n, tokens, width), BF), shape((n, tokens, width), BF),
        ),
        in_specs=[anywhere] * 8,
        out_specs=[anywhere] * 6,
        scratch_shapes=[
            pltpu.VMEM((local, width, hidden), BF), pltpu.VMEM((local, width, hidden), BF),
            pltpu.VMEM((local, width, hidden), BF),
            pltpu.VMEM((tokens, width), BF), pltpu.VMEM((tokens, width), BF),
            pltpu.VMEM((n, 8, tokens), F32),
            pltpu.VMEM((local, n * cap, width), BF), pltpu.VMEM((local, n * cap, width), BF),
            pltpu.VMEM((local, n * cap, hidden), BF), pltpu.VMEM((local, n * cap, hidden), BF),
            pltpu.VMEM((local, n * cap, hidden), BF),
            pltpu.VMEM((2, tokens, width), BF), pltpu.VMEM((2, tokens, width), BF),
            pltpu.VMEM((n, 8, tokens), F32),
            pltpu.VMEM((local * cap, tokens), BF), pltpu.VMEM((tokens, local * cap), BF),
            pltpu.VMEM((local * cap, tile), BF), pltpu.VMEM((local * cap, tile), F32),
            pltpu.VMEM((2, tile, 3 * hidden), BF),
            dma((3,)), dma((3,)), dma((2, n - 1)), dma((2, n - 1)), dma((2, n - 1)),
            dma((2, n - 1)), dma((n,)), dma((n,)), dma((n,)), dma((n,)), dma((n,)), dma((n,)),
            dma((2,)), dma((2,)), dma((2,)),
        ],
        compiler_params=pltpu.CompilerParams(
            vmem_limit_bytes=MOE_VMEM, collective_id=1, has_side_effects=True
        ),
        cost_estimate=pl.CostEstimate(
            flops=2 * n * local * cap * width * (9 * hidden + 5 * tokens),
            transcendentals=n * local * cap * hidden,
            bytes_accessed=2 * (8 * n * tokens * width + 6 * local * width * hidden),
        ),
        name="moe",
    )(x, cot, cot_left, cot_right, meta, gate, up, down)


RIGHT = [(0, 1), (1, 2), (2, 3)]
LEFT = [(1, 0), (2, 1), (3, 2)]


def body(
    tokens, cotangent, segment_ids, routes, fill_rank, query_weight, key_projection_weight,
    value_projection_weight, output_weight, router_weight, gain_attention, gain_experts,
    gate_weight, up_weight, down_weight,
):
    context_index = lax.axis_index("context")
    expert_size = lax.axis_size("expert")
    rows = tokens.shape[1]
    length = segment_ids.shape[1]
    kv_width = KEY_VALUE_HEADS * HEAD_SIZE
    gather = lambda w: lax.all_gather(w, "context", axis=0, tiled=True)

    upstream_low = cotangent[0]
    cot_left = lax.ppermute(upstream_low, "expert", RIGHT)
    cot_right = lax.ppermute(upstream_low, "expert", LEFT)

    expert_count = router_weight.shape[1]
    local = gate_weight.shape[0]
    capacity = 5 * rows * TOP // (4 * expert_count)
    cap = -(-capacity // 64) * 64
    names = jnp.arange(expert_count, dtype=jnp.int32)
    route_hit = routes[0][:, :, None] == names[None, None, :]
    routed = jnp.any(route_hit, axis=1)
    ranks = fill_rank[0, 0].reshape(rows, TOP)
    order = jnp.sum(jnp.where(route_hit, ranks[:, :, None], 0), axis=1)
    order = jnp.where(routed, order, rows * TOP).T
    slots = jnp.sum((order[:, :, None] < order[:, None, :]).astype(jnp.int32), axis=1)
    kept = routed.T & (slots < capacity)
    slots = jnp.where(kept, slots, -1)
    kept_float = kept.T.astype(F32)

    query_full, key_full, value_full, output_full, router_full, gain_first, gain_second = (
        gather(query_weight), gather(key_projection_weight), gather(value_projection_weight),
        gather(output_weight), gather(router_weight), gather(gain_attention), gather(gain_experts),
    )
    router_float = router_full.astype(F32)
    gain_first = gain_first.astype(F32)
    gain_second = gain_second.astype(F32)
    residual = tokens[0].astype(F32)
    root_first = inverse_root(residual)
    attn_input = (residual * root_first * gain_first).astype(BF)
    positions = context_index * rows + jnp.arange(rows, dtype=jnp.int32)
    cosine, sine = rope_tables(positions)
    cos_full = jnp.concatenate([cosine, cosine], axis=-1)
    sin_full = jnp.concatenate([-sine, sine], axis=-1)
    turn = lambda v, heads, d: apply_rotary(
        v.reshape(rows, heads, HEAD_SIZE), cosine, sine, d
    ).reshape(rows, heads * HEAD_SIZE)
    q = turn(mm(attn_input, query_full), QUERY_HEADS, 1.0).astype(BF)
    k_own = turn(mm(attn_input, key_full), KEY_VALUE_HEADS, 1.0).astype(BF)
    v_own = mm(attn_input, value_full).astype(BF)
    kv = gather(jnp.concatenate([k_own, v_own], axis=1))
    k_all, v_all = kv[:, :kv_width], kv[:, kv_width:]
    segments = segment_ids[0]
    tq, kb = attention_sizes(rows, length)
    meta = attention_meta(context_index, rows, segments, tq, kb)
    segk = segments[:, None]
    segq = lax.dynamic_slice_in_dim(segments, context_index * rows, rows)[None, :]
    mixed, lse = attention_forward(q, k_all, v_all, meta, segk, segq)

    hidden = residual + mm(mixed, output_full)
    root_second = inverse_root(hidden)
    normed = hidden * root_second * gain_second
    expert_input = normed.astype(BF)
    logits = precise_dims(normed, router_float, ((1,), (0,)))
    gates = jax.nn.softmax(jnp.where(routed, logits, -jnp.inf), axis=-1)
    kept_gates = gates * kept_float

    routing = jnp.stack([slots.astype(F32), kept_gates.T], axis=0)
    routing = routing.reshape(2, expert_size, local, rows).transpose(1, 0, 2, 3)
    routing = routing.reshape(expert_size, 2 * local, rows)
    routing = jnp.pad(routing, ((0, 0), (0, 8 - 2 * local), (0, 0)))
    dn_parts, dw_parts, part_y, grads_low, _, _ = moe(
        expert_input, upstream_low, cot_left, cot_right, routing, gate_weight, up_weight,
        down_weight, cap,
    )
    gate_dot = dw_parts[:, :local].reshape(expert_count, rows).T * kept_float
    y_parts = lax.all_to_all(part_y, "expert", split_axis=0, concat_axis=0, tiled=True)
    layer_out = (hidden + jnp.sum(y_parts.astype(F32), axis=0)).astype(BF)
    grads_shard = lax.psum_scatter(
        grads_low, ("dp", "context"), scatter_dimension=1, tiled=True
    ).astype(F32)
    ff = gate_weight.shape[2]
    gate_grad, up_grad, down_grad = (grads_shard[:, :, i * ff : (i + 1) * ff] for i in range(3))

    upstream = upstream_low.astype(F32)
    logit_grad = gates * (gate_dot - jnp.sum(gates * gate_dot, axis=-1, keepdims=True))
    normed_grad = jnp.sum(dn_parts.astype(F32), axis=0) + precise_dims(logit_grad, router_float, ((1,), (1,)))
    router_local = precise_dims(normed, logit_grad, ((0,), (0,)))
    hidden_total = upstream + norm_back(hidden, root_second, gain_second, normed_grad)
    gain_second_grad = jnp.sum(normed_grad * hidden * root_second, axis=0)
    attn_grad_low = hidden_total.astype(BF)
    output_local = mm_tn(mixed, attn_grad_low)
    mixed_grad_low = mm_nt(attn_grad_low, output_full).astype(BF)

    dq_low, dk_part, dv_part = attention_backward(
        q, k_all, v_all, mixed_grad_low, lse, cos_full, sin_full, meta, segk, segq
    )
    dkv = lax.psum_scatter(
        jnp.concatenate([dk_part, dv_part], axis=1), "context", scatter_dimension=0, tiled=True
    )
    dk_low = turn(dkv[:, :kv_width].astype(F32), KEY_VALUE_HEADS, -1.0).astype(BF)
    dv_low = dkv[:, kv_width:]
    input_total = mm_nt(dq_low, query_full) + mm_nt(dk_low, key_full) + mm_nt(dv_low, value_full)
    query_local = mm_tn(attn_input, dq_low)
    key_local = mm_tn(attn_input, dk_low)
    value_local = mm_tn(attn_input, dv_low)
    grad_tokens = (hidden_total + norm_back(residual, root_first, gain_first, input_total)).astype(BF)
    gain_first_grad = jnp.sum(input_total * residual * root_first, axis=0)

    reduce_rows = lambda v: lax.psum(
        lax.psum_scatter(v.astype(BF), "context", scatter_dimension=0, tiled=True), ("dp", "expert")
    ).astype(F32)
    return (
        layer_out[None], grad_tokens[None],
        reduce_rows(query_local), reduce_rows(key_local), reduce_rows(value_local),
        reduce_rows(output_local), reduce_rows(router_local),
        reduce_rows(gain_first_grad), reduce_rows(gain_second_grad),
        gate_grad, up_grad, down_grad,
    )


def solution(mesh):
    both = ("dp", "expert")
    token_spec = P(both, "context", None)
    row_spec = P("context", None)
    expert_out = P("expert", ("dp", "context"), None)
    return jax.shard_map(
        body,
        mesh=mesh,
        in_specs=(
            token_spec, token_spec, P(both, None), token_spec, token_spec,
            row_spec, row_spec, row_spec, row_spec, row_spec, P("context"), P("context"),
            P("expert", None, None), P("expert", None, None), P("expert", None, None),
        ),
        out_specs=(
            token_spec, token_spec, row_spec, row_spec, row_spec, row_spec, row_spec,
            P("context"), P("context"), expert_out, expert_out, expert_out,
        ),
        check_vma=False,
    )
```

```python
import functools
import math

import jax
import jax.numpy as jnp
from jax import lax
from jax.experimental import pallas as pl
from jax.experimental.pallas import tpu as pltpu
from jax.sharding import PartitionSpec as P

MODEL_WIDTH = 1536
QUERY_HEADS = 12
KEY_VALUE_HEADS = 2
HEAD_SIZE = 128
TOP = 4
GROUP = QUERY_HEADS // KEY_VALUE_HEADS
norm_eps = 1e-06
rope_base = 10000.0
NEG = -1e30
SCALE = 1.0 / math.sqrt(HEAD_SIZE)
BF = jnp.bfloat16
F32 = jnp.float32
VMEM_LIMIT = 60 * 1024 * 1024
MOE_VMEM = 63 * 1024 * 1024


def mm(a, b):
    return jnp.dot(a, b, preferred_element_type=F32)


def mm_nt(a, b):
    return lax.dot_general(a, b, (((1,), (1,)), ((), ())), preferred_element_type=F32)


def mm_tn(a, b):
    return lax.dot_general(a, b, (((0,), (0,)), ((), ())), preferred_element_type=F32)


def precise_dims(a, b, dims):
    return lax.dot_general(
        a, b, (dims, ((), ())), precision=lax.Precision.HIGHEST, preferred_element_type=F32
    )


def inverse_root(v):
    return lax.rsqrt(jnp.mean(v * v, axis=-1, keepdims=True) + norm_eps)


def norm_back(v, root, gain, upstream):
    scaled = upstream * gain
    cubed = root * root * root
    return root * scaled - v * cubed * jnp.mean(v * scaled, axis=-1, keepdims=True)


def rope_tables(positions):
    half = HEAD_SIZE // 2
    frequency = jnp.exp(
        -(jnp.arange(half, dtype=F32) * (2.0 / HEAD_SIZE)) * math.log(rope_base)
    )
    angle = positions.astype(F32)[:, None] * frequency[None, :]
    return jnp.cos(angle), jnp.sin(angle)


def apply_rotary(v, cosine, sine, direction):
    half = HEAD_SIZE // 2
    a, b = v[..., :half], v[..., half:]
    c, s = cosine[:, None, :], sine[:, None, :]
    return jnp.concatenate([a * c - direction * b * s, b * c + direction * a * s], axis=-1)


def fold_rows(v, op):
    rows, cols = v.shape
    return op(v.reshape(rows // 8, 8, cols), axis=0)


def make_bias(ctx, tokens, segk_ref, segq_ref, bias_ref):
    length = segk_ref.shape[0]
    key_pos = lax.broadcasted_iota(jnp.int32, (length, tokens), 0)
    query_pos = lax.broadcasted_iota(jnp.int32, (length, tokens), 1) + ctx * tokens
    same = segk_ref[...] == segq_ref[...]
    bias_ref[...] = jnp.where(same & (key_pos <= query_pos), 0.0, NEG)


def attn_fwd_kernel(kb, tq, meta, q_ref, k_ref, v_ref, segk_ref, segq_ref, o_ref, lse_ref,
                    bias_ref, s_ref, vt_ref):
    head = pl.program_id(0)
    tokens = q_ref.shape[0]

    @pl.when(head == 0)
    def _():
        make_bias(meta[0], tokens, segk_ref, segq_ref, bias_ref)

    @pl.when(lax.rem(head, GROUP) == 0)
    def _():
        vt_ref[...] = v_ref[...].astype(F32).T.astype(BF)

    for part in range(tokens // tq):
        cols = pl.ds(part * tq, tq)
        q = q_ref[cols, :]
        low, high = meta[1 + 2 * part], meta[2 + 2 * part]

        def score(i, top):
            rows = pl.ds(pl.multiple_of(i * kb, kb), kb)
            s = mm_nt(k_ref[rows, :], q) * SCALE + bias_ref[rows, cols]
            s_ref[rows, :] = s
            return jnp.maximum(top, fold_rows(s, jnp.max))

        top = lax.fori_loop(low, high, score, jnp.full((8, tq), NEG, F32))
        top = jnp.max(top, axis=0, keepdims=True)

        def value(i, carry):
            total, out = carry
            rows = pl.ds(pl.multiple_of(i * kb, kb), kb)
            p = jnp.exp(s_ref[rows, :] - top)
            total = total + fold_rows(p, jnp.sum)
            return total, out + mm(vt_ref[:, rows], p.astype(BF))

        total, out = lax.fori_loop(
            low, high, value, (jnp.zeros((8, tq), F32), jnp.zeros((HEAD_SIZE, tq), F32))
        )
        total = jnp.sum(total, axis=0, keepdims=True)
        o_ref[cols, :] = (out / total).T.astype(BF)
        lse_ref[0, :, cols] = top + jnp.log(total)


def attn_bwd_kernel(kb, tq, meta, q_ref, k_ref, v_ref, do_ref, lse_ref, cos_ref, sin_ref,
                    segk_ref, segq_ref, dq_ref, dk_ref, dv_ref,
                    bias_ref, p_ref, dp_ref, kt_ref, dk_acc, dv_acc):
    head = pl.program_id(0)
    tokens = q_ref.shape[0]

    @pl.when(head == 0)
    def _():
        make_bias(meta[0], tokens, segk_ref, segq_ref, bias_ref)

    @pl.when(lax.rem(head, GROUP) == 0)
    def _():
        kt_ref[...] = k_ref[...].astype(F32).T.astype(BF)
        dk_acc[...] = jnp.zeros_like(dk_acc)
        dv_acc[...] = jnp.zeros_like(dv_acc)

    for part in range(tokens // tq):
        cols = pl.ds(part * tq, tq)
        q = q_ref[cols, :]
        do = do_ref[cols, :]
        lse = lse_ref[0, :, cols]
        low, high = meta[1 + 2 * part], meta[2 + 2 * part]

        def score(i, delta):
            rows = pl.ds(pl.multiple_of(i * kb, kb), kb)
            s = mm_nt(k_ref[rows, :], q) * SCALE + bias_ref[rows, cols]
            p = jnp.exp(s - lse)
            dp = mm_nt(v_ref[rows, :], do)
            p_ref[rows, :] = p
            dp_ref[rows, :] = dp
            return delta + fold_rows(p * dp, jnp.sum)

        delta = lax.fori_loop(low, high, score, jnp.zeros((8, tq), F32))
        delta = jnp.sum(delta, axis=0, keepdims=True)

        def grads(i, dq):
            rows = pl.ds(pl.multiple_of(i * kb, kb), kb)
            p = p_ref[rows, :]
            ds = (p * (dp_ref[rows, :] - delta)).astype(BF)
            dv_acc[rows, :] += mm(p.astype(BF), do)
            dk_acc[rows, :] += mm(ds, q)
            return dq + mm(kt_ref[:, rows], ds)

        dq = lax.fori_loop(low, high, grads, jnp.zeros((HEAD_SIZE, tq), F32))
        dq = dq.T * SCALE
        turned = pltpu.roll(dq, HEAD_SIZE // 2, 1)
        dq_ref[cols, :] = (dq * cos_ref[cols, :] - turned * sin_ref[cols, :]).astype(BF)

    @pl.when(lax.rem(head, GROUP) == GROUP - 1)
    def _():
        dk_ref[...] = (dk_acc[...] * SCALE).astype(BF)
        dv_ref[...] = dv_acc[...].astype(BF)


def attention_sizes(tokens, length):
    tq = 256 if tokens % 256 == 0 else tokens
    kb = 256 if length % 256 == 0 else 128
    return tq, kb


def attention_meta(ctx, tokens, segments, tq, kb):
    entries = [ctx]
    for part in range(tokens // tq):
        first = ctx * tokens + part * tq
        own = lax.dynamic_slice_in_dim(segments, first, 1)
        start = jnp.sum((segments < own).astype(jnp.int32))
        entries += [start // kb, (first + tq + kb - 1) // kb]
    return jnp.stack(entries).astype(jnp.int32)


def attention_forward(q, k, v, meta, segk, segq):
    tokens, length = q.shape[0], k.shape[0]
    tq, kb = attention_sizes(tokens, length)
    const = lambda h, m: (0, 0)
    return pl.pallas_call(
        functools.partial(attn_fwd_kernel, kb, tq),
        out_shape=(
            jax.ShapeDtypeStruct(q.shape, BF),
            jax.ShapeDtypeStruct((QUERY_HEADS, 1, tokens), F32),
        ),
        grid_spec=pltpu.PrefetchScalarGridSpec(
            num_scalar_prefetch=1,
            grid=(QUERY_HEADS,),
            in_specs=[
                pl.BlockSpec((tokens, HEAD_SIZE), lambda h, m: (0, h)),
                pl.BlockSpec((length, HEAD_SIZE), lambda h, m: (0, h // GROUP)),
                pl.BlockSpec((length, HEAD_SIZE), lambda h, m: (0, h // GROUP)),
                pl.BlockSpec((length, 1), const),
                pl.BlockSpec((1, tokens), const),
            ],
            out_specs=[
                pl.BlockSpec((tokens, HEAD_SIZE), lambda h, m: (0, h)),
                pl.BlockSpec((1, 1, tokens), lambda h, m: (h, 0, 0)),
            ],
            scratch_shapes=[
                pltpu.VMEM((length, tokens), F32),
                pltpu.VMEM((length, tq), F32),
                pltpu.VMEM((HEAD_SIZE, length), BF),
            ],
        ),
        compiler_params=pltpu.CompilerParams(vmem_limit_bytes=VMEM_LIMIT),
        cost_estimate=pl.CostEstimate(
            flops=3 * QUERY_HEADS * tokens * length * HEAD_SIZE,
            transcendentals=QUERY_HEADS * tokens * length,
            bytes_accessed=4 * tokens * MODEL_WIDTH,
        ),
        name="attn_fwd",
    )(meta, q, k, v, segk, segq)


def attention_backward(q, k, v, do, lse, cos, sin, meta, segk, segq):
    tokens, length = q.shape[0], k.shape[0]
    tq, kb = attention_sizes(tokens, length)
    const = lambda h, m: (0, 0)
    by_head = lambda h, m: (0, h)
    by_group = lambda h, m: (0, h // GROUP)
    return pl.pallas_call(
        functools.partial(attn_bwd_kernel, kb, tq),
        out_shape=(
            jax.ShapeDtypeStruct(q.shape, BF),
            jax.ShapeDtypeStruct(k.shape, BF),
            jax.ShapeDtypeStruct(v.shape, BF),
        ),
        grid_spec=pltpu.PrefetchScalarGridSpec(
            num_scalar_prefetch=1,
            grid=(QUERY_HEADS,),
            in_specs=[
                pl.BlockSpec((tokens, HEAD_SIZE), by_head),
                pl.BlockSpec((length, HEAD_SIZE), by_group),
                pl.BlockSpec((length, HEAD_SIZE), by_group),
                pl.BlockSpec((tokens, HEAD_SIZE), by_head),
                pl.BlockSpec((1, 1, tokens), lambda h, m: (h, 0, 0)),
                pl.BlockSpec((tokens, HEAD_SIZE), const),
                pl.BlockSpec((tokens, HEAD_SIZE), const),
                pl.BlockSpec((length, 1), const),
                pl.BlockSpec((1, tokens), const),
            ],
            out_specs=[
                pl.BlockSpec((tokens, HEAD_SIZE), by_head),
                pl.BlockSpec((length, HEAD_SIZE), by_group),
                pl.BlockSpec((length, HEAD_SIZE), by_group),
            ],
            scratch_shapes=[
                pltpu.VMEM((length, tokens), F32),
                pltpu.VMEM((length, tq), F32),
                pltpu.VMEM((length, tq), F32),
                pltpu.VMEM((HEAD_SIZE, length), BF),
                pltpu.VMEM((length, HEAD_SIZE), F32),
                pltpu.VMEM((length, HEAD_SIZE), F32),
            ],
        ),
        compiler_params=pltpu.CompilerParams(vmem_limit_bytes=VMEM_LIMIT),
        cost_estimate=pl.CostEstimate(
            flops=8 * QUERY_HEADS * tokens * length * HEAD_SIZE,
            transcendentals=QUERY_HEADS * tokens * length,
            bytes_accessed=8 * tokens * MODEL_WIDTH,
        ),
        name="attn_bwd",
    )(meta, q, k, v, do, lse, cos, sin, segk, segq)


def remote(src, dst, ss, rs, axis, dev):
    return pltpu.make_async_remote_copy(
        src_ref=src, dst_ref=dst, send_sem=ss, recv_sem=rs, device_id={axis: dev},
        device_id_type=pl.DeviceIdType.MESH,
    )


def moe_kernel(cap, tile, n,
               x_hbm, cot_hbm, cotl_hbm, cotr_hbm, meta_hbm, gate_hbm, up_hbm, down_hbm,
               dn_out, dw_out, py_out, grads_out, xall, cotall,
               gate_ref, up_ref, down_ref, x_ref, cot_ref, metas, xs_ref, dy_ref, hb_ref, dg_ref,
               du_ref, pdn_ref, py_ref, dws, pick_ref, put_ref, ys_ref, acc_ref, stage,
               wsem, lsem, xs_send, xs_recv, cs_send, cs_recv, m_send, m_recv, dn_send, dn_recv,
               dw_send, dw_recv, py_sem, own_sem, st_sem):
    me = lax.axis_index("expert")
    tokens, width = x_ref.shape
    local, _, hidden = gate_ref.shape
    edge = (me == 0) | (me == n - 1)

    barrier = pltpu.get_barrier_semaphore()
    for d in range(1, n):
        pl.semaphore_signal(barrier, inc=1, device_id={"expert": lax.rem(me + d, n)},
                            device_id_type=pl.DeviceIdType.MESH)
    pl.semaphore_wait(barrier, n - 1)

    def exists(direction, step):
        return (me - 1 - step >= 0) if direction == 0 else (me + 1 + step <= n - 1)

    def sends(direction, step):
        if direction == 0:
            return (me - step >= 0) & (me < n - 1)
        return (me + step <= n - 1) & (me > 0)

    def stream(direction, step, own, table, ss, rs, near=None):
        block = me - step if direction == 0 else me + step
        block = jnp.clip(block, 0, n - 1)
        target = jnp.clip(me + 1 if direction == 0 else me - 1, 0, n - 1)
        if step == 0:
            src = own
        elif step == 1 and near is not None:
            src = near[direction]
        else:
            src = table.at[block]
        return remote(src, table.at[block], ss.at[direction, step], rs.at[direction, step],
                      "expert", target)

    xcopy = lambda d, s: stream(d, s, x_hbm, xall, xs_send, xs_recv)
    ccopy = lambda d, s: stream(d, s, cot_hbm, cotall, cs_send, cs_recv, (cotl_hbm, cotr_hbm))

    for d in range(2):
        @pl.when(sends(d, 0))
        def _():
            xcopy(d, 0).start()

    def meta_copy(j):
        return remote(meta_hbm.at[j], metas.at[me], m_send.at[j], m_recv.at[me], "expert", j)

    for j in range(n):
        @pl.when(me != j)
        def _():
            meta_copy(j).start()

    loads = [pltpu.make_async_copy(a, b, wsem.at[k]) for k, (a, b) in enumerate(
        ((gate_hbm, gate_ref), (up_hbm, up_ref), (down_hbm, down_ref)))]
    for load in loads:
        load.start()
    own_meta = pltpu.make_async_copy(meta_hbm.at[me], metas.at[me], lsem.at[2])
    own_meta.start()

    def fetch(a, b):
        cx = pltpu.make_async_copy(a, x_ref, lsem.at[0])
        cc = pltpu.make_async_copy(b, cot_ref, lsem.at[1])
        cx.start()
        cc.start()
        cx.wait()
        cc.wait()

    mirror = me >= 2
    side = jnp.where(mirror, n - 1 - me, me)

    def source_of(p):
        base = jnp.where(p == 0, side, jnp.where(p == 1, 1 - side, p))
        return jnp.where(mirror, n - 1 - base, base)

    def arrive(direction, step):
        @pl.when(exists(direction, step))
        def _():
            xcopy(direction, step).wait_recv()
            if step > 0:
                ccopy(direction, step).wait_recv()

    def forward(direction, step):
        @pl.when(sends(direction, step))
        def _():
            xcopy(direction, step).start()
            ccopy(direction, step).start()

    def one_source(p, _):
        src = source_of(p)

        @pl.when(p == 0)
        def _():
            fetch(x_hbm, cot_hbm)
            own_meta.wait()
            for load in loads:
                load.wait()

        @pl.when(p == 1)
        def _():
            for d in range(2):
                arrive(d, 0)
                forward(d, 1)

        @pl.when(((p == 2) & edge) | ((p == 3) & jnp.logical_not(edge)))
        def _():
            for d in range(2):
                arrive(d, 1)
                forward(d, 2)

        @pl.when((p == 3) & edge)
        def _():
            for d in range(2):
                arrive(d, 2)

        @pl.when((p > 0) & (src == me - 1))
        def _():
            fetch(xall.at[src], cotl_hbm)

        @pl.when((p > 0) & (src == me + 1))
        def _():
            fetch(xall.at[src], cotr_hbm)

        @pl.when((src < me - 1) | (src > me + 1))
        def _():
            fetch(xall.at[src], cotall.at[src])

        @pl.when(p > 0)
        def _():
            remote(meta_hbm.at[src], metas.at[src], m_send.at[src], m_recv.at[src], "expert",
                   src).wait_recv()

        meta = metas[src]
        columns = meta.T
        spread = lax.broadcasted_iota(jnp.int32, (tokens, local * cap), 1).astype(F32)
        slot = lax.broadcasted_iota(jnp.int32, (cap, tokens), 0).astype(F32)
        weights, put = [], None
        for e in range(local):
            hit = slot == meta[e : e + 1, :]
            pick_ref[pl.ds(e * cap, cap), :] = jnp.where(hit, 1.0, 0.0).astype(BF)
            weights.append(
                jnp.sum(jnp.where(hit, meta[local + e : local + e + 1, :], 0.0), axis=1,
                        keepdims=True)
            )
            own = columns[:, e : e + 1]
            here = spread == jnp.where(own < 0.0, -1.0, own + e * cap)
            put = here if put is None else put | here
        put_ref[...] = jnp.where(put, 1.0, 0.0).astype(BF)
        mine = pl.ds(pl.multiple_of(p * cap, cap), cap)
        buf = lax.rem(p, 2)

        def gather(j, _):
            cols = pl.ds(pl.multiple_of(j * tile, tile), tile)
            xs = mm(pick_ref[...], x_ref[:, cols]).astype(BF)
            cg = mm(pick_ref[...], cot_ref[:, cols])
            for e in range(local):
                rows = slice(e * cap, (e + 1) * cap)
                xs_ref[e, mine, cols] = xs[rows]
                dy_ref[e, mine, cols] = (weights[e] * cg[rows]).astype(BF)
            return 0

        lax.fori_loop(0, width // tile, gather, 0)

        def middle(j, _):
            cols = pl.ds(pl.multiple_of(j * tile, tile), tile)
            for e in range(local):
                g = mm(xs_ref[e, mine, :], gate_ref[e, :, cols])
                u = mm(xs_ref[e, mine, :], up_ref[e, :, cols])
                dh = mm(dy_ref[e, mine, :], down_ref[e, :, cols])
                s = 1.0 / (1.0 + jnp.exp(-g))
                act = g * s
                hb_ref[e, mine, cols] = (act * u).astype(BF)
                dg_ref[e, mine, cols] = (dh * u * (s * (1.0 + g * (1.0 - s)))).astype(BF)
                du_ref[e, mine, cols] = (dh * act).astype(BF)
            return 0

        lax.fori_loop(0, hidden // tile, middle, 0)

        @pl.when(p >= 2)
        def _():
            pltpu.make_async_copy(py_ref.at[buf], py_out.at[0], py_sem.at[buf]).wait()
            @pl.when(p == 2)
            def _():
                pltpu.make_async_copy(pdn_ref.at[buf], dn_out.at[me], own_sem.at[0]).wait()
            @pl.when(p == 3)
            def _():
                earlier = source_of(1)
                remote(pdn_ref.at[buf], dn_out.at[me], dn_send.at[earlier], dn_recv.at[me],
                       "expert", earlier).wait_send()

        acc_ref[...] = jnp.zeros_like(acc_ref)

        def back(j, _):
            cols = pl.ds(pl.multiple_of(j * tile, tile), tile)
            for e in range(local):
                dxs = mm_nt(dg_ref[e, mine, :], gate_ref[e, cols, :])
                dxs = dxs + mm_nt(du_ref[e, mine, :], up_ref[e, cols, :])
                ys_ref[pl.ds(e * cap, cap), :] = dxs.astype(BF)
            pdn_ref[buf, :, cols] = mm(put_ref[...], ys_ref[...]).astype(BF)
            return 0

        lax.fori_loop(0, width // tile, back, 0)

        @pl.when(p == 0)
        def _():
            pltpu.make_async_copy(pdn_ref.at[buf], dn_out.at[me], own_sem.at[0]).start()

        @pl.when(p > 0)
        def _():
            remote(pdn_ref.at[buf], dn_out.at[me], dn_send.at[src], dn_recv.at[me], "expert",
                   src).start()

        def ahead(j, _):
            cols = pl.ds(pl.multiple_of(j * tile, tile), tile)
            for e in range(local):
                rows = pl.ds(e * cap, cap)
                y = mm_nt(hb_ref[e, mine, :], down_ref[e, cols, :])
                acc_ref[rows, :] += mm(pick_ref[rows, :], cot_ref[:, cols]) * y
                ys_ref[rows, :] = (weights[e] * y).astype(BF)
            py_ref[buf, :, cols] = mm(put_ref[...], ys_ref[...]).astype(BF)
            return 0

        lax.fori_loop(0, width // tile, ahead, 0)
        pltpu.make_async_copy(py_ref.at[buf], py_out.at[src], py_sem.at[buf]).start()
        dws[p] = jnp.zeros((8, tokens), F32)
        for e in range(local):
            dot = jnp.sum(acc_ref[pl.ds(e * cap, cap), :], axis=1, keepdims=True)
            hit = slot == meta[e : e + 1, :]
            dws[p, e : e + 1, :] = jnp.sum(jnp.where(hit, dot, 0.0), axis=0, keepdims=True)

        @pl.when(p == 0)
        def _():
            pltpu.make_async_copy(dws.at[p], dw_out.at[me], own_sem.at[1]).start()

        @pl.when(p > 0)
        def _():
            remote(dws.at[p], dw_out.at[me], dw_send.at[src], dw_recv.at[me], "expert",
                   src).start()
        return 0

    lax.fori_loop(0, n, one_source, 0)

    tiles = width // tile
    store = lambda k, e, j: pltpu.make_async_copy(
        stage.at[k], grads_out.at[e, pl.ds(pl.multiple_of(j * tile, tile), tile), :], st_sem.at[k])

    def weight_grads(k, _):
        e, j = lax.div(k, tiles), lax.rem(k, tiles)
        cols = pl.ds(pl.multiple_of(j * tile, tile), tile)
        slot_k = lax.rem(k, 2)

        @pl.when(k >= 2)
        def _():
            store(slot_k, 0, 0).wait()

        xs = xs_ref[e, :, cols]
        stage[slot_k, :, 0:hidden] = mm_tn(xs, dg_ref[e]).astype(BF)
        stage[slot_k, :, hidden : 2 * hidden] = mm_tn(xs, du_ref[e]).astype(BF)
        stage[slot_k, :, 2 * hidden : 3 * hidden] = mm_tn(dy_ref[e, :, cols], hb_ref[e]).astype(BF)
        store(slot_k, e, j).start()
        return 0

    lax.fori_loop(0, local * tiles, weight_grads, 0)
    for k in range(2):
        store(k, 0, 0).wait()

    for k in range(2):
        pltpu.make_async_copy(py_ref.at[k], py_out.at[0], py_sem.at[k]).wait()
    pltpu.make_async_copy(dws.at[0], dw_out.at[me], own_sem.at[1]).wait()
    for d in range(2):
        for s in range(n - 1):
            @pl.when(sends(d, s))
            def _():
                xcopy(d, s).wait_send()
                if s > 0:
                    ccopy(d, s).wait_send()
    last = [source_of(p) for p in range(n)]
    for p in (2, 3):
        remote(pdn_ref.at[p % 2], dn_out.at[me], dn_send.at[last[p]], dn_recv.at[me], "expert",
               last[p]).wait_send()
    for j in range(n):
        @pl.when(me != j)
        def _():
            meta_copy(j).wait_send()
            remote(dws.at[0], dw_out.at[me], dw_send.at[j], dw_recv.at[me], "expert",
                   j).wait_send()
            remote(dws.at[0], dw_out.at[j], dw_send.at[j], dw_recv.at[j], "expert", j).wait_recv()
            remote(pdn_ref.at[0], dn_out.at[j], dn_send.at[j], dn_recv.at[j], "expert",
                   j).wait_recv()


def moe(x, cot, cot_left, cot_right, meta, gate, up, down, cap):
    n = meta.shape[0]
    tokens, width = x.shape
    local, _, hidden = gate.shape
    tile = 256
    anywhere = pl.BlockSpec(memory_space=pl.ANY)
    dma = pltpu.SemaphoreType.DMA
    shape = jax.ShapeDtypeStruct
    return pl.pallas_call(
        functools.partial(moe_kernel, cap, tile, n),
        out_shape=(
            shape((n, tokens, width), BF), shape((n, 8, tokens), F32), shape((n, tokens, width), BF),
            shape((local, width, 3 * hidden), BF),
            shape((n, tokens, width), BF), shape((n, tokens, width), BF),
        ),
        in_specs=[anywhere] * 8,
        out_specs=[anywhere] * 6,
        scratch_shapes=[
            pltpu.VMEM((local, width, hidden), BF), pltpu.VMEM((local, width, hidden), BF),
            pltpu.VMEM((local, width, hidden), BF),
            pltpu.VMEM((tokens, width), BF), pltpu.VMEM((tokens, width), BF),
            pltpu.VMEM((n, 8, tokens), F32),
            pltpu.VMEM((local, n * cap, width), BF), pltpu.VMEM((local, n * cap, width), BF),
            pltpu.VMEM((local, n * cap, hidden), BF), pltpu.VMEM((local, n * cap, hidden), BF),
            pltpu.VMEM((local, n * cap, hidden), BF),
            pltpu.VMEM((2, tokens, width), BF), pltpu.VMEM((2, tokens, width), BF),
            pltpu.VMEM((n, 8, tokens), F32),
            pltpu.VMEM((local * cap, tokens), BF), pltpu.VMEM((tokens, local * cap), BF),
            pltpu.VMEM((local * cap, tile), BF), pltpu.VMEM((local * cap, tile), F32),
            pltpu.VMEM((2, tile, 3 * hidden), BF),
            dma((3,)), dma((3,)), dma((2, n - 1)), dma((2, n - 1)), dma((2, n - 1)),
            dma((2, n - 1)), dma((n,)), dma((n,)), dma((n,)), dma((n,)), dma((n,)), dma((n,)),
            dma((2,)), dma((2,)), dma((2,)),
        ],
        compiler_params=pltpu.CompilerParams(
            vmem_limit_bytes=MOE_VMEM, collective_id=1, has_side_effects=True
        ),
        cost_estimate=pl.CostEstimate(
            flops=2 * n * local * cap * width * (9 * hidden + 5 * tokens),
            transcendentals=n * local * cap * hidden,
            bytes_accessed=2 * (8 * n * tokens * width + 6 * local * width * hidden),
        ),
        name="moe",
    )(x, cot, cot_left, cot_right, meta, gate, up, down)


RIGHT = [(0, 1), (1, 2), (2, 3)]
LEFT = [(1, 0), (2, 1), (3, 2)]


WIDE = 512
LINKS = 9


def tail_kernel(ob_ref, da_ref, xa_ref, dq_ref, dkp_ref, dvp_ref, cos_ref, sin_ref, wq_ref, wk_ref,
                wv_ref, dh_ref, x_ref, gain_ref, misc_ref,
                qg_out, kg_out, vg_out, og_out, mg_out, gt_ref,
                dkv_in, dkv_ref, part, buf0, buf1, buf2, buf3, buf4, res,
                kv_sem, send_sem, recv_sem, out_sem):
    ctx = lax.axis_index("context")
    dp = lax.axis_index("dp")
    z = lax.axis_index("expert")
    tokens, width = xa_ref.shape
    kv_width = dkp_ref.shape[1]
    half = width // 2
    chunks = 8
    bit = lambda v: lax.rem(v, 2)
    flip = lambda v: v + 1 - 2 * bit(v)
    far = lambda v: lax.rem(v + 2, 4)
    partner = {"c": ("context", 1 - ctx), "x": ("dp", flip(dp)), "y": ("dp", far(dp)),
               "n": ("expert", flip(z)), "f": ("expert", far(z))}
    side = {"c": ctx, "x": bit(dp), "y": lax.div(dp, 2), "n": bit(z), "f": lax.div(z, 2)}

    barrier = pltpu.get_barrier_semaphore()
    for axis, other in partner.values():
        pl.semaphore_signal(barrier, inc=1, device_id={axis: other},
                            device_id_type=pl.DeviceIdType.MESH)
    pl.semaphore_wait(barrier, len(partner))

    def exchange(src, dst, ss, rs, way):
        axis, other = partner[way]
        return remote(src, dst, ss, rs, axis, other)

    theirs = pl.ds(pl.multiple_of((1 - ctx) * tokens, 16), tokens)
    ours = pl.ds(pl.multiple_of(ctx * tokens, 16), tokens)
    kv_copies = [
        exchange(ref.at[theirs], dkv_in.at[k], kv_sem.at[0, k], kv_sem.at[1, k], "c")
        for k, ref in enumerate((dkp_ref, dvp_ref))
    ]
    for copy in kv_copies:
        copy.start()

    sizes = [half // 2, half // 4, half // 8, half // 16]
    bufs = [buf1, buf2, buf3, buf4]
    columns = [WIDE] * (chunks - 1) + [128]

    def flows(c):
        w = columns[c] // 2 if columns[c] >= 256 else columns[c]
        ways = [("x", "y", "n", "f"), ("y", "x", "n", "f")]
        return [(k, k * w, w, ways[(k + c) % 2]) for k in range(columns[c] // w)]

    def rows_at(ways, depth):
        first = 0
        for k in range(depth):
            first = first + side[ways[k]] * sizes[k]
        return pl.multiple_of(first, 16)

    def plus(dst, drows, dcols, a, arows, size):
        strip = 48
        def one(k, _):
            d = pl.ds(pl.multiple_of(drows + k * strip, 16), strip)
            s = pl.ds(pl.multiple_of(arows + k * strip, 16), strip)
            dst[d, dcols] = (dst[d, dcols].astype(F32) + a[s, dcols].astype(F32)).astype(BF)
            return 0
        lax.fori_loop(0, size // strip, one, 0)

    def link(c, flow, level):
        k, first, w, ways = flow
        cols = pl.ds(first, w)
        ss, rs = send_sem.at[c, k, level], recv_sem.at[c, k, level]
        if level == 0:
            src = part.at[c % 3, pl.ds(pl.multiple_of((1 - ctx) * half, 16), half), cols]
            return exchange(src, buf0.at[c, :, cols], ss, rs, "c")
        if level <= 4:
            way, size = ways[level - 1], sizes[level - 1]
            before = buf0 if level == 1 else bufs[level - 2]
            src = before.at[c, pl.ds(pl.multiple_of((1 - side[way]) * size, 16), size), cols]
            return exchange(src, bufs[level - 1].at[c, :, cols], ss, rs, way)
        depth = 8 - level + 1
        size = sizes[depth - 1]
        rows = pl.ds(rows_at(ways, depth), size)
        return exchange(res.at[c, rows, cols], res.at[c, rows, cols], ss, rs, ways[depth - 1])

    def produce(c):
        if c < 7:
            left, right, first = ((ob_ref, da_ref, c * WIDE) if c < 3 else
                                  (xa_ref, dq_ref, (c - 3) * WIDE) if c < 6 else
                                  (xa_ref, dkv_ref, 0))
            def one(j, _):
                rows = pl.ds(pl.multiple_of(j * 256, 256), 256)
                part[c % 3, rows, :] = mm_tn(left[:, rows], right[:, first : first + WIDE]).astype(BF)
                return 0
            lax.fori_loop(0, width // 256, one, 0)
        else:
            part[c % 3, :, 0:128] = misc_ref[...]
            part[c % 3, :, 16:24] = gain_rows.T.astype(BF)

    def finish(c):
        for copy in out_copy(c):
            copy.start()

    def out_copy(c):
        copy = lambda first, w, dst, at, k: pltpu.make_async_copy(
            res.at[c, :, pl.ds(first, w)], dst.at[:, pl.ds(at, w)], out_sem.at[c, k])
        if c < 3:
            return [copy(0, WIDE, og_out, c * WIDE, 0)]
        if c < 6:
            return [copy(0, WIDE, qg_out, (c - 3) * WIDE, 0)]
        if c == 6:
            return [copy(0, kv_width, kg_out, 0, 0), copy(kv_width, kv_width, vg_out, 0, 1)]
        return [copy(0, 128, mg_out, 0, 0)]

    def do(c, level):
        if level == 0:
            produce(c)
        for flow in flows(c):
            k, first, w, ways = flow
            cols = pl.ds(first, w)
            if level > 0:
                link(c, flow, level - 1).wait()
            if level == 1:
                plus(buf0.at[c], 0, cols, part.at[c % 3], ctx * half, half)
            elif 1 < level <= 4:
                before = buf0 if level == 2 else bufs[level - 3]
                plus(bufs[level - 2].at[c], 0, cols, before.at[c],
                     side[ways[level - 2]] * sizes[level - 2], sizes[level - 2])
            elif level == 5:
                rows = pl.ds(rows_at(ways, 4), sizes[3])
                keep = pl.ds(pl.multiple_of(side[ways[3]] * sizes[3], 16), sizes[3])
                res[c, rows, cols] = (buf4[c, :, cols].astype(F32)
                                      + buf3[c, keep, cols].astype(F32)).astype(BF)
            if level < LINKS:
                link(c, flow, level).start()
        if level == LINKS:
            finish(c)

    gain_rows = None
    for t in range(chunks + LINKS):
        for c in range(chunks):
            if 0 <= t - c <= LINKS:
                do(c, t - c)
        if t == 1:
            for copy in kv_copies:
                copy.wait()
            for h in range(kv_width // HEAD_SIZE):
                at = slice(h * HEAD_SIZE, (h + 1) * HEAD_SIZE)
                dk = dkp_ref[ours, at].astype(F32) + dkv_in[0, :, at].astype(F32)
                turned = pltpu.roll(dk, HEAD_SIZE // 2, 1)
                dkv_ref[:, at] = (dk * cos_ref[...] - turned * sin_ref[...]).astype(BF)
            dv = dvp_ref[ours, :].astype(F32) + dkv_in[1].astype(F32)
            dkv_ref[:, kv_width : 2 * kv_width] = dv.astype(BF)
        if t == 2:
            step = 64
            def strip(k, total):
                rows = pl.ds(pl.multiple_of(k * step, step), step)
                dxa = mm_nt(dq_ref[rows, :], wq_ref[...])
                dxa = dxa + mm_nt(dkv_ref[rows, 0:kv_width], wk_ref[...])
                dxa = dxa + mm_nt(dkv_ref[rows, kv_width : 2 * kv_width], wv_ref[...])
                v = x_ref[rows, :].astype(F32)
                root = inverse_root(v)
                back = dh_ref[rows, :] + norm_back(v, root, gain_ref[...], dxa)
                gt_ref[rows, :] = back.astype(BF)
                return total + fold_rows(dxa * v * root, jnp.sum)
            total = lax.fori_loop(0, tokens // step, strip, jnp.zeros((8, width), F32))
            gain_rows = jnp.broadcast_to(jnp.sum(total, axis=0, keepdims=True), (8, width))
    for c in range(chunks):
        for copy in out_copy(c):
            copy.wait()


def tail(ob, da, xa, dq, dk_part, dv_part, cos, sin, wq, wk, wv, dh, x, gain, misc):
    tokens, width = xa.shape
    kv_width = dk_part.shape[1]
    half = width // 2
    vmem = pl.BlockSpec(memory_space=pltpu.VMEM)
    anywhere = pl.BlockSpec(memory_space=pl.ANY)
    dma = pltpu.SemaphoreType.DMA
    shape = jax.ShapeDtypeStruct
    chunks = 8
    return pl.pallas_call(
        tail_kernel,
        out_shape=(
            shape((half, width), BF), shape((half, kv_width), BF), shape((half, kv_width), BF),
            shape((half, width), BF), shape((half, 128), BF), shape((tokens, width), BF),
        ),
        in_specs=[vmem] * 15,
        out_specs=[anywhere] * 5 + [vmem],
        scratch_shapes=[
            pltpu.VMEM((2, tokens, kv_width), BF), pltpu.VMEM((tokens, 2 * kv_width), BF),
            pltpu.VMEM((3, width, WIDE), BF),
            pltpu.VMEM((chunks, half, WIDE), BF), pltpu.VMEM((chunks, half // 2, WIDE), BF),
            pltpu.VMEM((chunks, half // 4, WIDE), BF), pltpu.VMEM((chunks, half // 8, WIDE), BF),
            pltpu.VMEM((chunks, half // 16, WIDE), BF), pltpu.VMEM((chunks, half, WIDE), BF),
            dma((2, 2)), dma((chunks, 2, LINKS)), dma((chunks, 2, LINKS)), dma((chunks, 2)),
        ],
        compiler_params=pltpu.CompilerParams(
            vmem_limit_bytes=MOE_VMEM, collective_id=2, has_side_effects=True
        ),
        cost_estimate=pl.CostEstimate(
            flops=2 * tokens * width * (2 * width + 4 * kv_width + width),
            transcendentals=0, bytes_accessed=16 * width * width,
        ),
        name="tail",
    )(ob, da, xa, dq, dk_part, dv_part, cos, sin, wq, wk, wv, dh, x, gain, misc)


def body(
    tokens, cotangent, segment_ids, routes, fill_rank, query_weight, key_projection_weight,
    value_projection_weight, output_weight, router_weight, gain_attention, gain_experts,
    gate_weight, up_weight, down_weight,
):
    context_index = lax.axis_index("context")
    expert_size = lax.axis_size("expert")
    rows = tokens.shape[1]
    length = segment_ids.shape[1]
    kv_width = KEY_VALUE_HEADS * HEAD_SIZE
    gather = lambda w: lax.all_gather(w, "context", axis=0, tiled=True)

    upstream_low = cotangent[0]
    cot_left = lax.ppermute(upstream_low, "expert", RIGHT)
    cot_right = lax.ppermute(upstream_low, "expert", LEFT)

    expert_count = router_weight.shape[1]
    local = gate_weight.shape[0]
    capacity = 5 * rows * TOP // (4 * expert_count)
    cap = -(-capacity // 64) * 64
    names = jnp.arange(expert_count, dtype=jnp.int32)
    route_hit = routes[0][:, :, None] == names[None, None, :]
    routed = jnp.any(route_hit, axis=1)
    ranks = fill_rank[0, 0].reshape(rows, TOP)
    order = jnp.sum(jnp.where(route_hit, ranks[:, :, None], 0), axis=1)
    order = jnp.where(routed, order, rows * TOP).T
    slots = jnp.sum((order[:, :, None] < order[:, None, :]).astype(jnp.int32), axis=1)
    kept = routed.T & (slots < capacity)
    slots = jnp.where(kept, slots, -1)
    kept_float = kept.T.astype(F32)

    query_full, key_full, value_full, output_full, router_full, gain_first, gain_second = (
        gather(query_weight), gather(key_projection_weight), gather(value_projection_weight),
        gather(output_weight), gather(router_weight), gather(gain_attention), gather(gain_experts),
    )
    router_float = router_full.astype(F32)
    gain_first = gain_first.astype(F32)
    gain_second = gain_second.astype(F32)
    residual = tokens[0].astype(F32)
    root_first = inverse_root(residual)
    attn_input = (residual * root_first * gain_first).astype(BF)
    positions = context_index * rows + jnp.arange(rows, dtype=jnp.int32)
    cosine, sine = rope_tables(positions)
    cos_full = jnp.concatenate([cosine, cosine], axis=-1)
    sin_full = jnp.concatenate([-sine, sine], axis=-1)
    turn = lambda v, heads, d: apply_rotary(
        v.reshape(rows, heads, HEAD_SIZE), cosine, sine, d
    ).reshape(rows, heads * HEAD_SIZE)
    q = turn(mm(attn_input, query_full), QUERY_HEADS, 1.0).astype(BF)
    k_own = turn(mm(attn_input, key_full), KEY_VALUE_HEADS, 1.0).astype(BF)
    v_own = mm(attn_input, value_full).astype(BF)
    kv = gather(jnp.concatenate([k_own, v_own], axis=1))
    k_all, v_all = kv[:, :kv_width], kv[:, kv_width:]
    segments = segment_ids[0]
    tq, kb = attention_sizes(rows, length)
    meta = attention_meta(context_index, rows, segments, tq, kb)
    segk = segments[:, None]
    segq = lax.dynamic_slice_in_dim(segments, context_index * rows, rows)[None, :]
    mixed, lse = attention_forward(q, k_all, v_all, meta, segk, segq)

    hidden = residual + mm(mixed, output_full)
    root_second = inverse_root(hidden)
    normed = hidden * root_second * gain_second
    expert_input = normed.astype(BF)
    logits = precise_dims(normed, router_float, ((1,), (0,)))
    gates = jax.nn.softmax(jnp.where(routed, logits, -jnp.inf), axis=-1)
    kept_gates = gates * kept_float

    routing = jnp.stack([slots.astype(F32), kept_gates.T], axis=0)
    routing = routing.reshape(2, expert_size, local, rows).transpose(1, 0, 2, 3)
    routing = routing.reshape(expert_size, 2 * local, rows)
    routing = jnp.pad(routing, ((0, 0), (0, 8 - 2 * local), (0, 0)))
    dn_parts, dw_parts, part_y, grads_low, _, _ = moe(
        expert_input, upstream_low, cot_left, cot_right, routing, gate_weight, up_weight,
        down_weight, cap,
    )
    gate_dot = dw_parts[:, :local].reshape(expert_count, rows).T * kept_float
    y_parts = lax.all_to_all(part_y, "expert", split_axis=0, concat_axis=0, tiled=True)
    grads_shard = lax.psum_scatter(
        grads_low, ("dp", "context"), scatter_dimension=1, tiled=True
    ).astype(F32)
    ff = gate_weight.shape[2]
    gate_grad, up_grad, down_grad = (grads_shard[:, :, i * ff : (i + 1) * ff] for i in range(3))

    upstream = upstream_low.astype(F32)
    logit_grad = gates * (gate_dot - jnp.sum(gates * gate_dot, axis=-1, keepdims=True))
    normed_grad = jnp.sum(dn_parts.astype(F32), axis=0) + precise_dims(logit_grad, router_float, ((1,), (1,)))
    router_local = precise_dims(normed, logit_grad, ((0,), (0,)))
    hidden_total = upstream + norm_back(hidden, root_second, gain_second, normed_grad)
    gain_second_grad = jnp.sum(normed_grad * hidden * root_second, axis=0)
    attn_grad_low = hidden_total.astype(BF)
    mixed_grad_low = mm_nt(attn_grad_low, output_full).astype(BF)

    dq_low, dk_part, dv_part = attention_backward(
        q, k_all, v_all, mixed_grad_low, lse, cos_full, sin_full, meta, segk, segq
    )
    if (lax.axis_size("dp"), lax.axis_size("context"), expert_size) == (4, 2, 4):
        misc = jnp.concatenate([router_local, gain_second_grad[:, None]], axis=1)
        misc = jnp.pad(misc, ((0, 0), (0, 128 - misc.shape[1]))).astype(BF)
        query_grad, key_grad, value_grad, output_grad, misc_grad, grad_tokens = tail(
            mixed, attn_grad_low, attn_input, dq_low, dk_part, dv_part, cos_full, sin_full,
            query_full, key_full, value_full, hidden_total, tokens[0], gain_first[None], misc,
        )
        query_grad, key_grad, value_grad, output_grad, misc_grad = (
            v.astype(F32) for v in (query_grad, key_grad, value_grad, output_grad, misc_grad)
        )
        sums = (
            query_grad, key_grad, value_grad, output_grad, misc_grad[:, :expert_count],
            misc_grad[:, 16], misc_grad[:, expert_count],
        )
    else:
        dkv = lax.psum_scatter(
            jnp.concatenate([dk_part, dv_part], axis=1), "context", scatter_dimension=0, tiled=True
        )
        dk_low = turn(dkv[:, :kv_width].astype(F32), KEY_VALUE_HEADS, -1.0).astype(BF)
        dv_low = dkv[:, kv_width:]
        input_total = mm_nt(dq_low, query_full) + mm_nt(dk_low, key_full) + mm_nt(dv_low, value_full)
        query_local = mm_tn(attn_input, dq_low)
        key_local = mm_tn(attn_input, dk_low)
        value_local = mm_tn(attn_input, dv_low)
        grad_tokens = (hidden_total + norm_back(residual, root_first, gain_first, input_total)).astype(BF)
        gain_first_grad = jnp.sum(input_total * residual * root_first, axis=0)

        reduce_rows = lambda v: lax.psum(
            lax.psum_scatter(v.astype(BF), "context", scatter_dimension=0, tiled=True), ("dp", "expert")
        ).astype(F32)
        sums = tuple(reduce_rows(v) for v in (
            query_local, key_local, value_local, mm_tn(mixed, attn_grad_low), router_local,
            gain_first_grad, gain_second_grad,
        ))
    late, grad_tokens = lax.optimization_barrier((hidden, grad_tokens))
    layer_out = (late + jnp.sum(y_parts.astype(F32), axis=0)).astype(BF)
    return (layer_out[None], grad_tokens[None], *sums, gate_grad, up_grad, down_grad)


def solution(mesh):
    both = ("dp", "expert")
    token_spec = P(both, "context", None)
    row_spec = P("context", None)
    expert_out = P("expert", ("dp", "context"), None)
    return jax.shard_map(
        body,
        mesh=mesh,
        in_specs=(
            token_spec, token_spec, P(both, None), token_spec, token_spec,
            row_spec, row_spec, row_spec, row_spec, row_spec, P("context"), P("context"),
            P("expert", None, None), P("expert", None, None), P("expert", None, None),
        ),
        out_specs=(
            token_spec, token_spec, row_spec, row_spec, row_spec, row_spec, row_spec,
            P("context"), P("context"), expert_out, expert_out, expert_out,
        ),
        check_vma=False,
    )
```

```python
import functools
import math

import jax
import jax.numpy as jnp
from jax import lax
from jax.experimental import pallas as pl
from jax.experimental.pallas import tpu as pltpu
from jax.sharding import PartitionSpec as P

MODEL_WIDTH = 1536
QUERY_HEADS = 12
KEY_VALUE_HEADS = 2
HEAD_SIZE = 128
TOP = 4
GROUP = QUERY_HEADS // KEY_VALUE_HEADS
norm_eps = 1e-06
rope_base = 10000.0
NEG = -1e30
HEADS_AT_ONCE = 3
SCALE = 1.0 / math.sqrt(HEAD_SIZE)
BF = jnp.bfloat16
F32 = jnp.float32
VMEM_LIMIT = 60 * 1024 * 1024
MOE_VMEM = 63 * 1024 * 1024


def mm(a, b):
    return jnp.dot(a, b, preferred_element_type=F32)


def mm_nt(a, b):
    return lax.dot_general(a, b, (((1,), (1,)), ((), ())), preferred_element_type=F32)


def mm_tn(a, b):
    return lax.dot_general(a, b, (((0,), (0,)), ((), ())), preferred_element_type=F32)


def inverse_root(v):
    return lax.rsqrt(jnp.mean(v * v, axis=-1, keepdims=True) + norm_eps)


def norm_back(v, root, gain, upstream):
    scaled = upstream * gain
    cubed = root * root * root
    return root * scaled - v * cubed * jnp.mean(v * scaled, axis=-1, keepdims=True)


def rope_tables(positions):
    half = HEAD_SIZE // 2
    frequency = jnp.exp(
        -(jnp.arange(half, dtype=F32) * (2.0 / HEAD_SIZE)) * math.log(rope_base)
    )
    angle = positions.astype(F32)[:, None] * frequency[None, :]
    return jnp.cos(angle), jnp.sin(angle)


def apply_rotary(v, cosine, sine, direction):
    half = HEAD_SIZE // 2
    a, b = v[..., :half], v[..., half:]
    c, s = cosine[:, None, :], sine[:, None, :]
    return jnp.concatenate([a * c - direction * b * s, b * c + direction * a * s], axis=-1)


def fold_rows(v, op):
    rows, cols = v.shape
    return op(v.reshape(rows // 8, 8, cols), axis=0)


def make_bias(ctx, tokens, segk_ref, segq_ref, bias_ref):
    length = segk_ref.shape[0]
    key_pos = lax.broadcasted_iota(jnp.int32, (length, tokens), 0)
    query_pos = lax.broadcasted_iota(jnp.int32, (length, tokens), 1) + ctx * tokens
    same = segk_ref[...] == segq_ref[...]
    bias_ref[...] = jnp.where(same & (key_pos <= query_pos), 0.0, NEG)


def attn_fwd_kernel(kb, tq, meta, q_ref, k_ref, v_ref, segk_ref, segq_ref, o_ref, lse_ref,
                    bias_ref, s_ref, vt_ref):
    step = pl.program_id(0)
    tokens = q_ref.shape[0]

    @pl.when(step == 0)
    def _():
        make_bias(meta[0], tokens, segk_ref, segq_ref, bias_ref)

    @pl.when(lax.rem(step * HEADS_AT_ONCE, GROUP) == 0)
    def _():
        vt_ref[...] = v_ref[...].astype(F32).T.astype(BF)

    heads = [slice(h * HEAD_SIZE, (h + 1) * HEAD_SIZE) for h in range(HEADS_AT_ONCE)]
    for part in range(tokens // tq):
        cols = pl.ds(part * tq, tq)
        low, high = meta[1 + 2 * part], meta[2 + 2 * part]

        def score(i, tops):
            rows = pl.ds(pl.multiple_of(i * kb, kb), kb)
            key, bias = k_ref[rows, :], bias_ref[rows, cols]
            out = []
            for h, at in enumerate(heads):
                s = mm_nt(key, q_ref[cols, at]) * SCALE + bias
                s_ref[h, rows, :] = s
                out.append(jnp.maximum(tops[h], fold_rows(s, jnp.max)))
            return tuple(out)

        tops = lax.fori_loop(low, high, score,
                             tuple(jnp.full((8, tq), NEG, F32) for _ in heads))
        tops = [jnp.max(t, axis=0, keepdims=True) for t in tops]

        def value(i, carry):
            totals, outs = carry
            rows = pl.ds(pl.multiple_of(i * kb, kb), kb)
            vt = vt_ref[:, rows]
            new_totals, new_outs = [], []
            for h in range(HEADS_AT_ONCE):
                p = jnp.exp(s_ref[h, rows, :] - tops[h])
                new_totals.append(totals[h] + fold_rows(p, jnp.sum))
                new_outs.append(outs[h] + mm(vt, p.astype(BF)))
            return tuple(new_totals), tuple(new_outs)

        totals, outs = lax.fori_loop(
            low, high, value, (tuple(jnp.zeros((8, tq), F32) for _ in heads),
                               tuple(jnp.zeros((HEAD_SIZE, tq), F32) for _ in heads)))
        for h, at in enumerate(heads):
            total = jnp.sum(totals[h], axis=0, keepdims=True)
            o_ref[cols, at] = (outs[h] / total).T.astype(BF)
            lse_ref[h, :, cols] = tops[h] + jnp.log(total)


def attn_bwd_kernel(kb, tq, meta, q_ref, k_ref, v_ref, do_ref, lse_ref, cos_ref, sin_ref,
                    segk_ref, segq_ref, dq_ref, dk_ref, dv_ref,
                    bias_ref, p_ref, dp_ref, kt_ref, dk_acc, dv_acc):
    step = pl.program_id(0)
    tokens = q_ref.shape[0]

    @pl.when(step == 0)
    def _():
        make_bias(meta[0], tokens, segk_ref, segq_ref, bias_ref)

    place = lax.rem(step * HEADS_AT_ONCE, GROUP)

    @pl.when(place == 0)
    def _():
        kt_ref[...] = k_ref[...].astype(F32).T.astype(BF)
        dk_acc[...] = jnp.zeros_like(dk_acc)
        dv_acc[...] = jnp.zeros_like(dv_acc)

    heads = [slice(h * HEAD_SIZE, (h + 1) * HEAD_SIZE) for h in range(HEADS_AT_ONCE)]
    for part in range(tokens // tq):
        cols = pl.ds(part * tq, tq)
        low, high = meta[1 + 2 * part], meta[2 + 2 * part]

        def score(i, deltas):
            rows = pl.ds(pl.multiple_of(i * kb, kb), kb)
            key, value, bias = k_ref[rows, :], v_ref[rows, :], bias_ref[rows, cols]
            out = []
            for h, at in enumerate(heads):
                s = mm_nt(key, q_ref[cols, at]) * SCALE + bias
                p = jnp.exp(s - lse_ref[h, :, cols])
                dp = mm_nt(value, do_ref[cols, at])
                p_ref[h, rows, :] = p
                dp_ref[h, rows, :] = dp
                out.append(deltas[h] + fold_rows(p * dp, jnp.sum))
            return tuple(out)

        deltas = lax.fori_loop(low, high, score, tuple(jnp.zeros((8, tq), F32) for _ in heads))
        deltas = [jnp.sum(d, axis=0, keepdims=True) for d in deltas]

        def grads(i, dqs):
            rows = pl.ds(pl.multiple_of(i * kb, kb), kb)
            kt = kt_ref[:, rows]
            out, dk, dv = [], dk_acc[rows, :], dv_acc[rows, :]
            for h, at in enumerate(heads):
                p = p_ref[h, rows, :]
                ds = (p * (dp_ref[h, rows, :] - deltas[h])).astype(BF)
                dv = dv + mm(p.astype(BF), do_ref[cols, at])
                dk = dk + mm(ds, q_ref[cols, at])
                out.append(dqs[h] + mm(kt, ds))
            dk_acc[rows, :] = dk
            dv_acc[rows, :] = dv
            return tuple(out)

        dqs = lax.fori_loop(low, high, grads,
                            tuple(jnp.zeros((HEAD_SIZE, tq), F32) for _ in heads))
        for h, at in enumerate(heads):
            dq = dqs[h].T * SCALE
            turned = pltpu.roll(dq, HEAD_SIZE // 2, 1)
            dq_ref[cols, at] = (dq * cos_ref[cols, :] - turned * sin_ref[cols, :]).astype(BF)

    @pl.when(place == GROUP - HEADS_AT_ONCE)
    def _():
        dk_ref[...] = (dk_acc[...] * SCALE).astype(BF)
        dv_ref[...] = dv_acc[...].astype(BF)


def attention_sizes(tokens, length):
    tq = 256 if tokens % 256 == 0 else tokens
    kb = 256 if length % 256 == 0 else 128
    return tq, kb


def attention_meta(ctx, tokens, segments, tq, kb):
    entries = [ctx]
    for part in range(tokens // tq):
        first = ctx * tokens + part * tq
        own = lax.dynamic_slice_in_dim(segments, first, 1)
        start = jnp.sum((segments < own).astype(jnp.int32))
        entries += [start // kb, (first + tq + kb - 1) // kb]
    return jnp.stack(entries).astype(jnp.int32)


def attention_forward(q, kv, meta, segk, segq):
    tokens, length = q.shape[0], kv.shape[0]
    tq, kb = attention_sizes(tokens, length)
    const = lambda h, m: (0, 0)
    return pl.pallas_call(
        functools.partial(attn_fwd_kernel, kb, tq),
        out_shape=(
            jax.ShapeDtypeStruct(q.shape, BF),
            jax.ShapeDtypeStruct((QUERY_HEADS, 1, tokens), F32),
        ),
        grid_spec=pltpu.PrefetchScalarGridSpec(
            num_scalar_prefetch=1,
            grid=(QUERY_HEADS // HEADS_AT_ONCE,),
            in_specs=[
                pl.BlockSpec((tokens, HEADS_AT_ONCE * HEAD_SIZE), lambda h, m: (0, h)),
                pl.BlockSpec((length, HEAD_SIZE), lambda h, m: (0, h * HEADS_AT_ONCE // GROUP)),
                pl.BlockSpec((length, HEAD_SIZE), lambda h, m: (0, KEY_VALUE_HEADS + h * HEADS_AT_ONCE // GROUP)),
                pl.BlockSpec((length, 1), const),
                pl.BlockSpec((1, tokens), const),
            ],
            out_specs=[
                pl.BlockSpec((tokens, HEADS_AT_ONCE * HEAD_SIZE), lambda h, m: (0, h)),
                pl.BlockSpec((HEADS_AT_ONCE, 1, tokens), lambda h, m: (h, 0, 0)),
            ],
            scratch_shapes=[
                pltpu.VMEM((length, tokens), F32),
                pltpu.VMEM((HEADS_AT_ONCE, length, tq), F32),
                pltpu.VMEM((HEAD_SIZE, length), BF),
            ],
        ),
        compiler_params=pltpu.CompilerParams(vmem_limit_bytes=VMEM_LIMIT),
        cost_estimate=pl.CostEstimate(
            flops=3 * QUERY_HEADS * tokens * length * HEAD_SIZE,
            transcendentals=QUERY_HEADS * tokens * length,
            bytes_accessed=4 * tokens * MODEL_WIDTH,
        ),
        name="attn_fwd",
    )(meta, q, kv, kv, segk, segq)


def attention_backward(q, kv, do, lse, cos, sin, meta, segk, segq):
    tokens, length = q.shape[0], kv.shape[0]
    tq, kb = attention_sizes(tokens, length)
    const = lambda h, m: (0, 0)
    by_head = lambda h, m: (0, h)
    by_group = lambda h, m: (0, h * HEADS_AT_ONCE // GROUP)
    return pl.pallas_call(
        functools.partial(attn_bwd_kernel, kb, tq),
        out_shape=(
            jax.ShapeDtypeStruct(q.shape, BF),
            jax.ShapeDtypeStruct((length, KEY_VALUE_HEADS * HEAD_SIZE), BF),
            jax.ShapeDtypeStruct((length, KEY_VALUE_HEADS * HEAD_SIZE), BF),
        ),
        grid_spec=pltpu.PrefetchScalarGridSpec(
            num_scalar_prefetch=1,
            grid=(QUERY_HEADS // HEADS_AT_ONCE,),
            in_specs=[
                pl.BlockSpec((tokens, HEADS_AT_ONCE * HEAD_SIZE), by_head),
                pl.BlockSpec((length, HEAD_SIZE), by_group),
                pl.BlockSpec((length, HEAD_SIZE), lambda h, m: (0, KEY_VALUE_HEADS + h * HEADS_AT_ONCE // GROUP)),
                pl.BlockSpec((tokens, HEADS_AT_ONCE * HEAD_SIZE), by_head),
                pl.BlockSpec((HEADS_AT_ONCE, 1, tokens), lambda h, m: (h, 0, 0)),
                pl.BlockSpec((tokens, HEAD_SIZE), const),
                pl.BlockSpec((tokens, HEAD_SIZE), const),
                pl.BlockSpec((length, 1), const),
                pl.BlockSpec((1, tokens), const),
            ],
            out_specs=[
                pl.BlockSpec((tokens, HEADS_AT_ONCE * HEAD_SIZE), by_head),
                pl.BlockSpec((length, HEAD_SIZE), by_group),
                pl.BlockSpec((length, HEAD_SIZE), by_group),
            ],
            scratch_shapes=[
                pltpu.VMEM((length, tokens), F32),
                pltpu.VMEM((HEADS_AT_ONCE, length, tq), F32),
                pltpu.VMEM((HEADS_AT_ONCE, length, tq), F32),
                pltpu.VMEM((HEAD_SIZE, length), BF),
                pltpu.VMEM((length, HEAD_SIZE), F32),
                pltpu.VMEM((length, HEAD_SIZE), F32),
            ],
        ),
        compiler_params=pltpu.CompilerParams(vmem_limit_bytes=VMEM_LIMIT),
        cost_estimate=pl.CostEstimate(
            flops=8 * QUERY_HEADS * tokens * length * HEAD_SIZE,
            transcendentals=QUERY_HEADS * tokens * length,
            bytes_accessed=8 * tokens * MODEL_WIDTH,
        ),
        name="attn_bwd",
    )(meta, q, kv, kv, do, lse, cos, sin, segk, segq)


def remote(src, dst, ss, rs, axis, dev):
    return pltpu.make_async_remote_copy(
        src_ref=src, dst_ref=dst, send_sem=ss, recv_sem=rs, device_id={axis: dev},
        device_id_type=pl.DeviceIdType.MESH,
    )


def moe_kernel(cap, tile, n,
               x_hbm, cot_hbm, cotl_hbm, cotr_hbm, cot2_hbm, meta_hbm, gate_hbm, up_hbm, down_hbm,
               dn_out, dw_out, py_out, grads_out, xall, cotfar,
               gate_ref, up_ref, down_ref, x_ref, cot_ref, metas, xs_ref, dy_ref, hb_ref, dg_ref,
               du_ref, pdn_ref, transit, py_ref, dws, pick_ref, put_ref, ys_ref, acc_ref, stage,
               wsem, lsem, xs_send, xs_recv, far_sem, m_send, m_recv, dn_send, dn_recv,
               dw_send, dw_recv, py_sem, own_sem, st_sem):
    me = lax.axis_index("expert")
    tokens, width = x_ref.shape
    local, _, hidden = gate_ref.shape
    edge = (me == 0) | (me == n - 1)

    barrier = pltpu.get_barrier_semaphore()
    for d in range(1, n):
        pl.semaphore_signal(barrier, inc=1, device_id={"expert": lax.rem(me + d, n)},
                            device_id_type=pl.DeviceIdType.MESH)
    pl.semaphore_wait(barrier, n - 1)

    def exists(direction, step):
        return (me - 1 - step >= 0) if direction == 0 else (me + 1 + step <= n - 1)

    def sends(direction, step):
        if direction == 0:
            return (me - step >= 0) & (me < n - 1)
        return (me + step <= n - 1) & (me > 0)

    def xcopy(direction, step):
        block = jnp.clip(me - step if direction == 0 else me + step, 0, n - 1)
        target = jnp.clip(me + 1 if direction == 0 else me - 1, 0, n - 1)
        src = x_hbm if step == 0 else xall.at[block]
        return remote(src, xall.at[block], xs_send.at[direction, step],
                      xs_recv.at[direction, step], "expert", target)

    outward = jnp.where(me < 2, 0, n - 1)
    inward = n - 1 - jnp.clip(me, 1, n - 2)
    inner = jnp.where(me < 2, 1, n - 2)
    far_copy = lambda: remote(cot2_hbm, cotfar, far_sem.at[0], far_sem.at[1], "expert", outward)
    middle_device = jnp.logical_not(edge)

    for d in range(2):
        @pl.when(sends(d, 0))
        def _():
            xcopy(d, 0).start()

    @pl.when(middle_device)
    def _():
        far_copy().start()

    def meta_copy(j):
        return remote(meta_hbm.at[j], metas.at[me], m_send.at[j], m_recv.at[me], "expert", j)

    for j in range(n):
        @pl.when(me != j)
        def _():
            meta_copy(j).start()

    loads = [pltpu.make_async_copy(a, b, wsem.at[k]) for k, (a, b) in enumerate(
        ((gate_hbm, gate_ref), (up_hbm, up_ref), (down_hbm, down_ref)))]
    for load in loads:
        load.start()
    own_meta = pltpu.make_async_copy(meta_hbm.at[me], metas.at[me], lsem.at[2])
    own_meta.start()

    def fetch(a, b):
        cx = pltpu.make_async_copy(a, x_ref, lsem.at[0])
        cc = pltpu.make_async_copy(b, cot_ref, lsem.at[1])
        cx.start()
        cc.start()
        cx.wait()
        cc.wait()

    pieces = 4
    part_rows = tokens // pieces
    piece = lambda part: pl.ds(part * part_rows, part_rows)

    def edge_copy(kind, part):
        dst = dn_out.at[1, piece(part)] if kind == 0 else transit.at[kind - 1, piece(part)]
        return remote(pdn_ref.at[kind, piece(part)], dst, dn_send.at[kind, part],
                      dn_recv.at[kind, part], "expert", inner)

    def pass_copy(kind, part):
        dst = transit.at[2, piece(part)] if kind == 1 else dn_out.at[2, piece(part)]
        arrival = dn_recv.at[3, part] if kind != 1 else dn_recv.at[4, part]
        return remote(transit.at[kind, piece(part)], dst, dn_send.at[kind, part], arrival,
                      "expert", outward if kind == 2 else inward)

    mirror = me >= 2
    side = jnp.where(mirror, n - 1 - me, me)

    def source_of(p):
        base = jnp.where(p == 0, side, jnp.where(p == 1, 1 - side, p))
        return jnp.where(mirror, n - 1 - base, base)

    def arrive(direction, step):
        @pl.when(exists(direction, step))
        def _():
            xcopy(direction, step).wait_recv()

    def forward(direction, step):
        @pl.when(sends(direction, step))
        def _():
            xcopy(direction, step).start()

    def one_source(p, _):
        src = source_of(p)

        @pl.when(p == 0)
        def _():
            fetch(x_hbm, cot_hbm)
            own_meta.wait()
            for load in loads:
                load.wait()

        @pl.when(p == 1)
        def _():
            for d in range(2):
                arrive(d, 0)
                forward(d, 1)

        @pl.when(((p == 2) & edge) | ((p == 3) & jnp.logical_not(edge)))
        def _():
            for d in range(2):
                arrive(d, 1)
                forward(d, 2)

        @pl.when((p == 3) & edge)
        def _():
            for d in range(2):
                arrive(d, 2)
            far_copy().wait_recv()

        @pl.when((p > 0) & (src == me - 1))
        def _():
            fetch(xall.at[src], cotl_hbm)

        @pl.when((p > 0) & (src == me + 1))
        def _():
            fetch(xall.at[src], cotr_hbm)

        @pl.when((src == me - 2) | (src == me + 2))
        def _():
            fetch(xall.at[src], cot2_hbm)

        @pl.when((src == me - 3) | (src == me + 3))
        def _():
            fetch(xall.at[src], cotfar)

        @pl.when(p > 0)
        def _():
            remote(meta_hbm.at[src], metas.at[src], m_send.at[src], m_recv.at[src], "expert",
                   src).wait_recv()

        meta = metas[src]
        columns = meta.T
        spread = lax.broadcasted_iota(jnp.int32, (tokens, local * cap), 1).astype(F32)
        slot = lax.broadcasted_iota(jnp.int32, (cap, tokens), 0).astype(F32)
        weights, put = [], None
        for e in range(local):
            hit = slot == meta[e : e + 1, :]
            pick_ref[pl.ds(e * cap, cap), :] = jnp.where(hit, 1.0, 0.0).astype(BF)
            weights.append(
                jnp.sum(jnp.where(hit, meta[local + e : local + e + 1, :], 0.0), axis=1,
                        keepdims=True)
            )
            own = columns[:, e : e + 1]
            here = spread == jnp.where(own < 0.0, -1.0, own + e * cap)
            put = here if put is None else put | here
        put_ref[...] = jnp.where(put, 1.0, 0.0).astype(BF)
        mine = pl.ds(pl.multiple_of(p * cap, cap), cap)
        buf = lax.rem(p + 2, 3)

        def gather(j, _):
            cols = pl.ds(pl.multiple_of(j * tile, tile), tile)
            xs = mm(pick_ref[...], x_ref[:, cols]).astype(BF)
            cg = mm(pick_ref[...], cot_ref[:, cols])
            for e in range(local):
                rows = slice(e * cap, (e + 1) * cap)
                xs_ref[e, mine, cols] = xs[rows]
                dy_ref[e, mine, cols] = (weights[e] * cg[rows]).astype(BF)
            return 0

        lax.fori_loop(0, width // tile, gather, 0)

        def middle(j, _):
            cols = pl.ds(pl.multiple_of(j * tile, tile), tile)
            for e in range(local):
                g = mm(xs_ref[e, mine, :], gate_ref[e, :, cols])
                u = mm(xs_ref[e, mine, :], up_ref[e, :, cols])
                dh = mm(dy_ref[e, mine, :], down_ref[e, :, cols])
                s = 1.0 / (1.0 + jnp.exp(-g))
                act = g * s
                hb_ref[e, mine, cols] = (act * u).astype(BF)
                dg_ref[e, mine, cols] = (dh * u * (s * (1.0 + g * (1.0 - s)))).astype(BF)
                du_ref[e, mine, cols] = (dh * act).astype(BF)
            return 0

        lax.fori_loop(0, hidden // tile, middle, 0)

        @pl.when(p > 0)
        def _():
            pltpu.make_async_copy(py_ref, py_out.at[0], py_sem.at[0]).wait()

        @pl.when(p == 3)
        def _():
            pltpu.make_async_copy(pdn_ref.at[2], dn_out.at[0], own_sem.at[0]).wait()

        acc_ref[...] = jnp.zeros_like(acc_ref)

        def back(j, _):
            cols = pl.ds(pl.multiple_of(j * tile, tile), tile)
            for e in range(local):
                dxs = mm_nt(dg_ref[e, mine, :], gate_ref[e, cols, :])
                dxs = dxs + mm_nt(du_ref[e, mine, :], up_ref[e, cols, :])
                ys_ref[pl.ds(e * cap, cap), :] = dxs.astype(BF)
            pdn_ref[buf, :, cols] = mm(put_ref[...], ys_ref[...]).astype(BF)
            return 0

        lax.fori_loop(0, width // tile, back, 0)

        @pl.when(p == 0)
        def _():
            pltpu.make_async_copy(pdn_ref.at[2], dn_out.at[0], own_sem.at[0]).start()

        for kind in range(3):
            @pl.when(edge & (p == kind + 1))
            def _():
                for part in range(pieces):
                    edge_copy(kind, part).start()

        def ahead(j, _):
            cols = pl.ds(pl.multiple_of(j * tile, tile), tile)
            for e in range(local):
                rows = pl.ds(e * cap, cap)
                y = mm_nt(hb_ref[e, mine, :], down_ref[e, cols, :])
                acc_ref[rows, :] += mm(pick_ref[rows, :], cot_ref[:, cols]) * y
                ys_ref[rows, :] = (weights[e] * y).astype(BF)
            py_ref[:, cols] = mm(put_ref[...], ys_ref[...]).astype(BF)
            return 0

        lax.fori_loop(0, width // tile, ahead, 0)
        pltpu.make_async_copy(py_ref, py_out.at[src], py_sem.at[0]).start()
        dws[p] = jnp.zeros((8, tokens), F32)
        for e in range(local):
            dot = jnp.sum(acc_ref[pl.ds(e * cap, cap), :], axis=1, keepdims=True)
            hit = slot == meta[e : e + 1, :]
            dws[p, e : e + 1, :] = jnp.sum(jnp.where(hit, dot, 0.0), axis=0, keepdims=True)

        @pl.when(p == 0)
        def _():
            pltpu.make_async_copy(dws.at[p], dw_out.at[me], own_sem.at[1]).start()

        @pl.when(p > 0)
        def _():
            remote(dws.at[p], dw_out.at[me], dw_send.at[src], dw_recv.at[me], "expert",
                   src).start()
        return 0

    lax.fori_loop(0, n, one_source, 0)

    tiles = width // tile
    store = lambda k, e, j: pltpu.make_async_copy(
        stage.at[k], grads_out.at[e, pl.ds(pl.multiple_of(j * tile, tile), tile), :], st_sem.at[k])

    def weight_grads(k, _):
        e, j = lax.div(k, tiles), lax.rem(k, tiles)
        cols = pl.ds(pl.multiple_of(j * tile, tile), tile)
        slot_k = lax.rem(k, 2)

        @pl.when(k >= 2)
        def _():
            store(slot_k, 0, 0).wait()

        xs = xs_ref[e, :, cols]
        stage[slot_k, :, 0:hidden] = mm_tn(xs, dg_ref[e]).astype(BF)
        stage[slot_k, :, hidden : 2 * hidden] = mm_tn(xs, du_ref[e]).astype(BF)
        stage[slot_k, :, 2 * hidden : 3 * hidden] = mm_tn(dy_ref[e, :, cols], hb_ref[e]).astype(BF)
        store(slot_k, e, j).start()
        return 0

    lax.fori_loop(0, local * tiles, weight_grads, 0)
    for k in range(2):
        store(k, 0, 0).wait()

    @pl.when(middle_device)
    def _():
        for kind, own in ((0, 1), (1, 2), (2, 0)):
            for part in range(pieces):
                landed = (edge_copy(kind + 1, part) if kind < 2 else pass_copy(1, part))
                landed.wait_recv()
                rows = piece(part)
                transit[kind, rows, :] = (transit[kind, rows, :].astype(F32)
                                          + pdn_ref[own, rows, :].astype(F32)).astype(BF)
                pass_copy(kind, part).start()
        for part in range(pieces):
            edge_copy(0, part).wait_recv()
            pass_copy(0, part).wait_recv()
            for kind in range(3):
                pass_copy(kind, part).wait_send()
        far_copy().wait_send()

    @pl.when(edge)
    def _():
        for part in range(pieces):
            pass_copy(0, part).wait_recv()
            for kind in range(3):
                edge_copy(kind, part).wait_send()

    pltpu.make_async_copy(py_ref, py_out.at[0], py_sem.at[0]).wait()
    pltpu.make_async_copy(dws.at[0], dw_out.at[me], own_sem.at[1]).wait()
    for d in range(2):
        for s in range(n - 1):
            @pl.when(sends(d, s))
            def _():
                xcopy(d, s).wait_send()
    for j in range(n):
        @pl.when(me != j)
        def _():
            meta_copy(j).wait_send()
            remote(dws.at[0], dw_out.at[me], dw_send.at[j], dw_recv.at[me], "expert",
                   j).wait_send()
            remote(dws.at[0], dw_out.at[j], dw_send.at[j], dw_recv.at[j], "expert", j).wait_recv()


def moe(x, cot, cot_left, cot_right, cot_second, meta, gate, up, down, cap):
    n = meta.shape[0]
    tokens, width = x.shape
    local, _, hidden = gate.shape
    tile = 256
    anywhere = pl.BlockSpec(memory_space=pl.ANY)
    dma = pltpu.SemaphoreType.DMA
    shape = jax.ShapeDtypeStruct
    return pl.pallas_call(
        functools.partial(moe_kernel, cap, tile, n),
        out_shape=(
            shape((3, tokens, width), BF), shape((n, 8, tokens), F32), shape((n, tokens, width), BF),
            shape((local, width, 3 * hidden), BF),
            shape((n, tokens, width), BF), shape((tokens, width), BF),
        ),
        in_specs=[anywhere] * 9,
        out_specs=[anywhere] * 6,
        scratch_shapes=[
            pltpu.VMEM((local, width, hidden), BF), pltpu.VMEM((local, width, hidden), BF),
            pltpu.VMEM((local, width, hidden), BF),
            pltpu.VMEM((tokens, width), BF), pltpu.VMEM((tokens, width), BF),
            pltpu.VMEM((n, 8, tokens), F32),
            pltpu.VMEM((local, n * cap, width), BF), pltpu.VMEM((local, n * cap, width), BF),
            pltpu.VMEM((local, n * cap, hidden), BF), pltpu.VMEM((local, n * cap, hidden), BF),
            pltpu.VMEM((local, n * cap, hidden), BF),
            pltpu.VMEM((3, tokens, width), BF), pltpu.VMEM((3, tokens, width), BF),
            pltpu.VMEM((tokens, width), BF), pltpu.VMEM((n, 8, tokens), F32),
            pltpu.VMEM((local * cap, tokens), BF), pltpu.VMEM((tokens, local * cap), BF),
            pltpu.VMEM((local * cap, tile), BF), pltpu.VMEM((local * cap, tile), F32),
            pltpu.VMEM((2, tile, 3 * hidden), BF),
            dma((3,)), dma((3,)), dma((2, n - 1)), dma((2, n - 1)), dma((2,)), dma((n,)), dma((n,)),
            dma((3, 4)), dma((5, 4)), dma((n,)), dma((n,)), dma((1,)), dma((2,)), dma((2,)),
        ],
        compiler_params=pltpu.CompilerParams(
            vmem_limit_bytes=MOE_VMEM, collective_id=1, has_side_effects=True
        ),
        cost_estimate=pl.CostEstimate(
            flops=2 * n * local * cap * width * (9 * hidden + 5 * tokens),
            transcendentals=n * local * cap * hidden,
            bytes_accessed=2 * (8 * n * tokens * width + 6 * local * width * hidden),
        ),
        name="moe",
    )(x, cot, cot_left, cot_right, cot_second, meta, gate, up, down)


RIGHT = [(0, 1), (1, 2), (2, 3)]
LEFT = [(1, 0), (2, 1), (3, 2)]
RIGHT_ON = [(1, 2), (2, 3)]
LEFT_ON = [(1, 0), (2, 1)]


def project_kernel(x_ref, wq_own, wk_own, wv_own, small_own, cos_ref, sin_ref,
                   q_ref, xa_ref, kv_ref, wq_ref, wk_ref, wv_ref, small_ref,
                   small_in, root_ref, acc_ref, send_sem, recv_sem, own_sem):
    ctx = lax.axis_index("context")
    tokens, width = x_ref.shape
    kv_width = wk_ref.shape[1]
    half = width // 2
    barrier = pltpu.get_barrier_semaphore()
    pl.semaphore_signal(barrier, inc=1, device_id={"context": 1 - ctx},
                        device_id_type=pl.DeviceIdType.MESH)
    pl.semaphore_wait(barrier, 1)

    own = pl.ds(pl.multiple_of(ctx * half, 128), half)
    other = pl.ds(pl.multiple_of((1 - ctx) * half, 128), half)
    ours = pl.ds(pl.multiple_of(ctx * tokens, 16), tokens)
    give = lambda k, src, dst: remote(src, dst, send_sem.at[k], recv_sem.at[k], "context", 1 - ctx)
    weights = ((wk_own, wk_ref), (wv_own, wv_ref), (wq_own, wq_ref))
    sends = [give(0, small_own, small_in)]
    sends += [give(1 + k, a, b.at[own, :]) for k, (a, b) in enumerate(weights)]
    for copy in sends:
        copy.start()
    keeps = [pltpu.make_async_copy(a, b.at[own, :], own_sem.at[k])
             for k, (a, b) in enumerate(weights)]
    for copy in keeps:
        copy.start()

    strip = 64

    def scale(k, _):
        rows = pl.ds(pl.multiple_of(k * strip, strip), strip)
        root = inverse_root(x_ref[rows, :].astype(F32))
        root_ref[rows, :] = root
        xa_ref[rows, own] = (x_ref[rows, own].astype(F32) * root * small_own[0:1, :]).astype(BF)
        return 0

    lax.fori_loop(0, tokens // strip, scale, 0)
    for copy in keeps:
        copy.wait()

    acc_ref[:, 0:kv_width] = mm(xa_ref[:, own], wk_ref[own, :])
    acc_ref[:, kv_width : 2 * kv_width] = mm(xa_ref[:, own], wv_ref[own, :])
    tile = 256

    def first(j, _):
        cols = pl.ds(pl.multiple_of(j * tile, tile), tile)
        at = pl.ds(pl.multiple_of(2 * kv_width + j * tile, tile), tile)
        acc_ref[:, at] = mm(xa_ref[:, own], wq_ref[own, cols])
        return 0

    lax.fori_loop(0, width // tile, first, 0)

    sends[0].wait()
    small_ref[:, own] = small_own[...]
    small_ref[:, other] = small_in[...]

    def rest(k, _):
        rows = pl.ds(pl.multiple_of(k * strip, strip), strip)
        xa_ref[rows, other] = (x_ref[rows, other].astype(F32) * root_ref[rows, :]
                               * small_in[0:1, :]).astype(BF)
        return 0

    lax.fori_loop(0, tokens // strip, rest, 0)

    def rope(v):
        parts = []
        for h in range(v.shape[1] // HEAD_SIZE):
            t = v[:, h * HEAD_SIZE : (h + 1) * HEAD_SIZE]
            t = t * cos_ref[...] + pltpu.roll(t, HEAD_SIZE // 2, 1) * sin_ref[...]
            parts.append(t.astype(BF))
        return jnp.concatenate(parts, axis=1)

    sends[1].wait()
    sends[2].wait()
    k = acc_ref[:, 0:kv_width] + mm(xa_ref[:, other], wk_ref[other, :])
    v = acc_ref[:, kv_width : 2 * kv_width] + mm(xa_ref[:, other], wv_ref[other, :])
    kv_ref[ours, 0:kv_width] = rope(k)
    kv_ref[ours, kv_width : 2 * kv_width] = v.astype(BF)
    kv_copy = give(4, kv_ref.at[ours, :], kv_ref.at[ours, :])
    kv_copy.start()
    sends[3].wait()

    def second(j, _):
        cols = pl.ds(pl.multiple_of(j * tile, tile), tile)
        at = pl.ds(pl.multiple_of(2 * kv_width + j * tile, tile), tile)
        q_ref[:, cols] = rope(acc_ref[:, at] + mm(xa_ref[:, other], wq_ref[other, cols]))
        return 0

    lax.fori_loop(0, width // tile, second, 0)
    kv_copy.wait()


def project(x, wq, wk, wv, small, cos, sin):
    tokens, width = x.shape
    kv_width = wk.shape[1]
    vmem = pl.BlockSpec(memory_space=pltpu.VMEM)
    anywhere = pl.BlockSpec(memory_space=pl.ANY)
    dma = pltpu.SemaphoreType.DMA
    shape = jax.ShapeDtypeStruct
    return pl.pallas_call(
        project_kernel,
        out_shape=(
            shape((tokens, width), BF), shape((tokens, width), BF),
            shape((2 * tokens, 2 * kv_width), BF), shape((width, width), BF),
            shape((width, kv_width), BF), shape((width, kv_width), BF),
            shape((small.shape[0], width), F32),
        ),
        in_specs=[vmem, anywhere, anywhere, anywhere, vmem, vmem, vmem],
        out_specs=[vmem] * 7,
        scratch_shapes=[
            pltpu.VMEM(small.shape, F32), pltpu.VMEM((tokens, 1), F32),
            pltpu.VMEM((tokens, width + 2 * kv_width), F32), dma((5,)), dma((5,)), dma((3,)),
        ],
        compiler_params=pltpu.CompilerParams(
            vmem_limit_bytes=VMEM_LIMIT, collective_id=3, has_side_effects=True
        ),
        cost_estimate=pl.CostEstimate(
            flops=2 * tokens * width * (width + 2 * kv_width), transcendentals=0,
            bytes_accessed=8 * width * width,
        ),
        name="project",
    )(x, wq, wk, wv, small, cos, sin)


def exact(a, b, dims):
    return lax.dot_general(a, b, (dims, ((), ())), precision=lax.Precision.HIGHEST,
                           preferred_element_type=F32)


def mix_kernel(strip, ob_ref, x_ref, wo_ref, small_ref, routed_ref,
               hidden_ref, xq_ref, gates_ref):
    j = pl.program_id(0)
    tile = wo_ref.shape[1]
    cols = pl.ds(pl.multiple_of(j * tile, tile), tile)
    hidden_ref[:, cols] = x_ref[:, cols].astype(F32) + mm(ob_ref[...], wo_ref[...])

    @pl.when(j == pl.num_programs(0) - 1)
    def _():
        def one(k, _):
            rows = pl.ds(pl.multiple_of(k * strip, strip), strip)
            h = hidden_ref[rows, :]
            normed = h * inverse_root(h) * small_ref[1:2, :]
            xq_ref[rows, :] = normed.astype(BF)
            logits = exact(normed, small_ref[8:16, :], ((1,), (1,)))
            routed = routed_ref[rows, :] > 0.0
            top = jnp.max(jnp.where(routed, logits, NEG), axis=1, keepdims=True)
            power = jnp.where(routed, jnp.exp(jnp.where(routed, logits, top) - top), 0.0)
            gates_ref[rows, :] = power / jnp.sum(power, axis=1, keepdims=True)
            return 0

        lax.fori_loop(0, hidden_ref.shape[0] // strip, one, 0)


def row_strip(tokens):
    return 128 if tokens % 128 == 0 else 64


def mix(ob, x, wo, small, routed):
    tokens, width = x.shape
    tile = 256
    shape = jax.ShapeDtypeStruct
    const = lambda v: pl.BlockSpec(v.shape, lambda j: (0, 0), pipeline_mode=pl.Buffered(1))
    whole = lambda d: pl.BlockSpec((tokens, d), lambda j: (0, 0))
    experts = routed.shape[1]
    return pl.pallas_call(
        functools.partial(mix_kernel, row_strip(tokens)),
        out_shape=(shape((tokens, width), F32), shape((tokens, width), BF),
                   shape((tokens, experts), F32)),
        grid=(width // tile,),
        in_specs=[const(ob), const(x), pl.BlockSpec((width, tile), lambda j: (0, j)), const(small),
                  const(routed)],
        out_specs=[whole(width), whole(width), whole(experts)],
        compiler_params=pltpu.CompilerParams(vmem_limit_bytes=VMEM_LIMIT),
        cost_estimate=pl.CostEstimate(
            flops=2 * tokens * width * width, transcendentals=0, bytes_accessed=4 * width * width),
        name="mix",
    )(ob, x, wo, small, routed)


def turn_kernel(strip, flags, dn_ref, dot_ref, gates_ref, hidden_ref, cot_ref, wo_ref, small_ref,
                dh_ref, da_ref, dob_ref, misc_ref, normed_ref, dlog_ref):
    j = pl.program_id(0)

    @pl.when(j == 0)
    def _():
        gain = small_ref[1:2, :]

        def one(k, total):
            rows = pl.ds(pl.multiple_of(k * strip, strip), strip)
            gates, dot = gates_ref[rows, :], dot_ref[rows, :]
            dlogits = gates * (dot - jnp.sum(gates * dot, axis=1, keepdims=True))
            dn = exact(dlogits, small_ref[8:16, :], ((1,), (0,)))
            for part in range(dn_ref.shape[0]):
                dn = dn + jnp.where(flags[part] > 0, dn_ref[part, rows, :].astype(F32), 0.0)
            h = hidden_ref[rows, :]
            root = inverse_root(h)
            scaled = h * root
            normed_ref[rows, :] = scaled * gain
            dlog_ref[rows, :] = dlogits
            dh = cot_ref[rows, :].astype(F32) + norm_back(h, root, gain, dn)
            dh_ref[rows, :] = dh
            da_ref[rows, :] = dh.astype(BF)
            return total + fold_rows(dn * scaled, jnp.sum)

        tokens, width = dh_ref.shape
        misc_ref[8:16, :] = lax.fori_loop(0, tokens // strip, one, jnp.zeros((8, width), F32))

    tile = wo_ref.shape[0]
    cols = pl.ds(pl.multiple_of(j * tile, tile), tile)
    dob_ref[:, cols] = mm_nt(da_ref[...], wo_ref[...]).astype(BF)
    misc_ref[0:8, cols] = exact(dlog_ref[...], normed_ref[:, cols], ((0,), (0,)))


def turn(flags, dn_parts, dot, gates, hidden, cot, wo, small):
    tokens, width = cot.shape
    tile = 256
    shape = jax.ShapeDtypeStruct
    once = pl.Buffered(1)
    const = lambda v: pl.BlockSpec(v.shape, lambda j, f: (0,) * v.ndim, pipeline_mode=once)
    whole = lambda r: pl.BlockSpec((r, width), lambda j, f: (0, 0))
    return pl.pallas_call(
        functools.partial(turn_kernel, row_strip(tokens)),
        out_shape=(shape((tokens, width), F32), shape((tokens, width), BF),
                   shape((tokens, width), BF), shape((16, width), F32)),
        grid_spec=pltpu.PrefetchScalarGridSpec(
            num_scalar_prefetch=1,
            grid=(width // tile,),
            in_specs=[const(dn_parts), const(dot), const(gates), const(hidden), const(cot),
                      pl.BlockSpec((tile, width), lambda j, f: (j, 0)), const(small)],
            out_specs=[whole(tokens), whole(tokens), whole(tokens), whole(16)],
            scratch_shapes=[pltpu.VMEM((tokens, width), F32),
                            pltpu.VMEM((tokens, gates.shape[1]), F32)],
        ),
        compiler_params=pltpu.CompilerParams(vmem_limit_bytes=VMEM_LIMIT),
        cost_estimate=pl.CostEstimate(
            flops=2 * tokens * width * width, transcendentals=0, bytes_accessed=8 * width * width),
        name="turn",
    )(flags, dn_parts, dot, gates, hidden, cot, wo, small)


WIDE = 512
LINKS = 9


def tail_kernel(ob_ref, da_ref, xa_ref, dq_ref, dkp_ref, dvp_ref, cos_ref, sin_ref, wq_ref, wk_ref,
                wv_ref, dh_ref, x_ref, gain_ref, misc_ref,
                qg_out, kg_out, vg_out, og_out, mg_out, gt_ref,
                dkv_in, dkv_ref, part, buf0, buf1, buf2, buf3, buf4, res,
                kv_sem, send_sem, recv_sem, out_sem):
    ctx = lax.axis_index("context")
    dp = lax.axis_index("dp")
    z = lax.axis_index("expert")
    tokens, width = xa_ref.shape
    kv_width = dkp_ref.shape[1]
    half = width // 2
    chunks = 8
    bit = lambda v: lax.rem(v, 2)
    flip = lambda v: v + 1 - 2 * bit(v)
    far = lambda v: lax.rem(v + 2, 4)
    partner = {"c": ("context", 1 - ctx), "x": ("dp", flip(dp)), "y": ("dp", far(dp)),
               "n": ("expert", flip(z)), "f": ("expert", far(z))}
    side = {"c": ctx, "x": bit(dp), "y": lax.div(dp, 2), "n": bit(z), "f": lax.div(z, 2)}

    barrier = pltpu.get_barrier_semaphore()
    for axis, other in partner.values():
        pl.semaphore_signal(barrier, inc=1, device_id={axis: other},
                            device_id_type=pl.DeviceIdType.MESH)
    pl.semaphore_wait(barrier, len(partner))

    def exchange(src, dst, ss, rs, way):
        axis, other = partner[way]
        return remote(src, dst, ss, rs, axis, other)

    theirs = pl.ds(pl.multiple_of((1 - ctx) * tokens, 16), tokens)
    ours = pl.ds(pl.multiple_of(ctx * tokens, 16), tokens)
    kv_copies = [
        exchange(ref.at[theirs], dkv_in.at[k], kv_sem.at[0, k], kv_sem.at[1, k], "c")
        for k, ref in enumerate((dkp_ref, dvp_ref))
    ]
    for copy in kv_copies:
        copy.start()

    sizes = [half // 2, half // 4, half // 8, half // 16]
    bufs = [buf1, buf2, buf3, buf4]
    columns = [WIDE] * (chunks - 1) + [128]

    def flows(c):
        w = columns[c] // 2 if columns[c] >= 256 else columns[c]
        ways = [("x", "y", "n", "f"), ("y", "x", "n", "f")]
        return [(k, k * w, w, ways[(k + c) % 2]) for k in range(columns[c] // w)]

    def rows_at(ways, depth):
        first = 0
        for k in range(depth):
            first = first + side[ways[k]] * sizes[k]
        return pl.multiple_of(first, 16)

    def plus(dst, drows, dcols, a, arows, size):
        strip = 48
        def one(k, _):
            d = pl.ds(pl.multiple_of(drows + k * strip, 16), strip)
            s = pl.ds(pl.multiple_of(arows + k * strip, 16), strip)
            dst[d, dcols] = (dst[d, dcols].astype(F32) + a[s, dcols].astype(F32)).astype(BF)
            return 0
        lax.fori_loop(0, size // strip, one, 0)

    def link(c, flow, level):
        k, first, w, ways = flow
        cols = pl.ds(first, w)
        ss, rs = send_sem.at[c, k, level], recv_sem.at[c, k, level]
        if level == 0:
            src = part.at[c % 3, pl.ds(pl.multiple_of((1 - ctx) * half, 16), half), cols]
            return exchange(src, buf0.at[c, :, cols], ss, rs, "c")
        if level <= 4:
            way, size = ways[level - 1], sizes[level - 1]
            before = buf0 if level == 1 else bufs[level - 2]
            src = before.at[c, pl.ds(pl.multiple_of((1 - side[way]) * size, 16), size), cols]
            return exchange(src, bufs[level - 1].at[c, :, cols], ss, rs, way)
        depth = 8 - level + 1
        size = sizes[depth - 1]
        rows = pl.ds(rows_at(ways, depth), size)
        return exchange(res.at[c, rows, cols], res.at[c, rows, cols], ss, rs, ways[depth - 1])

    def produce(c):
        if c < 7:
            left, right, first = ((ob_ref, da_ref, c * WIDE) if c < 3 else
                                  (xa_ref, dq_ref, (c - 3) * WIDE) if c < 6 else
                                  (xa_ref, dkv_ref, 0))
            def one(j, _):
                rows = pl.ds(pl.multiple_of(j * 256, 256), 256)
                part[c % 3, rows, :] = mm_tn(left[:, rows], right[:, first : first + WIDE]).astype(BF)
                return 0
            lax.fori_loop(0, width // 256, one, 0)
        else:
            part[c % 3, :, 0:128] = jnp.zeros((width, 128), BF)
            part[c % 3, :, 0:16] = misc_rows.T.astype(BF)
            part[c % 3, :, 16:24] = gain_rows.T.astype(BF)

    def finish(c):
        for copy in out_copy(c):
            copy.start()

    def out_copy(c):
        copy = lambda first, w, dst, at, k: pltpu.make_async_copy(
            res.at[c, :, pl.ds(first, w)], dst.at[:, pl.ds(at, w)], out_sem.at[c, k])
        if c < 3:
            return [copy(0, WIDE, og_out, c * WIDE, 0)]
        if c < 6:
            return [copy(0, WIDE, qg_out, (c - 3) * WIDE, 0)]
        if c == 6:
            return [copy(0, kv_width, kg_out, 0, 0), copy(kv_width, kv_width, vg_out, 0, 1)]
        return [copy(0, 128, mg_out, 0, 0)]

    def do(c, level):
        if level == 0:
            produce(c)
        for flow in flows(c):
            k, first, w, ways = flow
            cols = pl.ds(first, w)
            if level > 0:
                link(c, flow, level - 1).wait()
            if level == 1:
                plus(buf0.at[c], 0, cols, part.at[c % 3], ctx * half, half)
            elif 1 < level <= 4:
                before = buf0 if level == 2 else bufs[level - 3]
                plus(bufs[level - 2].at[c], 0, cols, before.at[c],
                     side[ways[level - 2]] * sizes[level - 2], sizes[level - 2])
            elif level == 5:
                rows = pl.ds(rows_at(ways, 4), sizes[3])
                keep = pl.ds(pl.multiple_of(side[ways[3]] * sizes[3], 16), sizes[3])
                res[c, rows, cols] = (buf4[c, :, cols].astype(F32)
                                      + buf3[c, keep, cols].astype(F32)).astype(BF)
            if level < LINKS:
                link(c, flow, level).start()
        if level == LINKS:
            finish(c)

    gain_rows = None
    misc_rows = misc_ref[...]
    for t in range(chunks + LINKS):
        for c in range(chunks):
            if 0 <= t - c <= LINKS:
                do(c, t - c)
        if t == 1:
            for copy in kv_copies:
                copy.wait()
            for h in range(kv_width // HEAD_SIZE):
                at = slice(h * HEAD_SIZE, (h + 1) * HEAD_SIZE)
                dk = dkp_ref[ours, at].astype(F32) + dkv_in[0, :, at].astype(F32)
                turned = pltpu.roll(dk, HEAD_SIZE // 2, 1)
                dkv_ref[:, at] = (dk * cos_ref[...] - turned * sin_ref[...]).astype(BF)
            dv = dvp_ref[ours, :].astype(F32) + dkv_in[1].astype(F32)
            dkv_ref[:, kv_width : 2 * kv_width] = dv.astype(BF)
        if t == 2:
            step = 64
            def strip(k, total):
                rows = pl.ds(pl.multiple_of(k * step, step), step)
                dxa = mm_nt(dq_ref[rows, :], wq_ref[...])
                dxa = dxa + mm_nt(dkv_ref[rows, 0:kv_width], wk_ref[...])
                dxa = dxa + mm_nt(dkv_ref[rows, kv_width : 2 * kv_width], wv_ref[...])
                v = x_ref[rows, :].astype(F32)
                root = inverse_root(v)
                back = dh_ref[rows, :] + norm_back(v, root, gain_ref[...], dxa)
                gt_ref[rows, :] = back.astype(BF)
                return total + fold_rows(dxa * v * root, jnp.sum)
            total = lax.fori_loop(0, tokens // step, strip, jnp.zeros((8, width), F32))
            gain_rows = jnp.broadcast_to(jnp.sum(total, axis=0, keepdims=True), (8, width))
    for c in range(chunks):
        for copy in out_copy(c):
            copy.wait()


def tail(ob, da, xa, dq, dk_part, dv_part, cos, sin, wq, wk, wv, dh, x, gain, misc):
    tokens, width = xa.shape
    kv_width = dk_part.shape[1]
    half = width // 2
    vmem = pl.BlockSpec(memory_space=pltpu.VMEM)
    anywhere = pl.BlockSpec(memory_space=pl.ANY)
    dma = pltpu.SemaphoreType.DMA
    shape = jax.ShapeDtypeStruct
    chunks = 8
    return pl.pallas_call(
        tail_kernel,
        out_shape=(
            shape((half, width), BF), shape((half, kv_width), BF), shape((half, kv_width), BF),
            shape((half, width), BF), shape((half, 128), BF), shape((tokens, width), BF),
        ),
        in_specs=[vmem] * 15,
        out_specs=[anywhere] * 5 + [vmem],
        scratch_shapes=[
            pltpu.VMEM((2, tokens, kv_width), BF), pltpu.VMEM((tokens, 2 * kv_width), BF),
            pltpu.VMEM((3, width, WIDE), BF),
            pltpu.VMEM((chunks, half, WIDE), BF), pltpu.VMEM((chunks, half // 2, WIDE), BF),
            pltpu.VMEM((chunks, half // 4, WIDE), BF), pltpu.VMEM((chunks, half // 8, WIDE), BF),
            pltpu.VMEM((chunks, half // 16, WIDE), BF), pltpu.VMEM((chunks, half, WIDE), BF),
            dma((2, 2)), dma((chunks, 2, LINKS)), dma((chunks, 2, LINKS)), dma((chunks, 2)),
        ],
        compiler_params=pltpu.CompilerParams(
            vmem_limit_bytes=MOE_VMEM, collective_id=2, has_side_effects=True
        ),
        cost_estimate=pl.CostEstimate(
            flops=2 * tokens * width * (2 * width + 4 * kv_width + width),
            transcendentals=0, bytes_accessed=16 * width * width,
        ),
        name="tail",
    )(ob, da, xa, dq, dk_part, dv_part, cos, sin, wq, wk, wv, dh, x, gain, misc)


def body(
    tokens, cotangent, segment_ids, routes, fill_rank, query_weight, key_projection_weight,
    value_projection_weight, output_weight, router_weight, gain_attention, gain_experts,
    gate_weight, up_weight, down_weight,
):
    context_index = lax.axis_index("context")
    context_size = lax.axis_size("context")
    expert_size = lax.axis_size("expert")
    rows = tokens.shape[1]
    length = segment_ids.shape[1]
    kv_width = KEY_VALUE_HEADS * HEAD_SIZE
    gather = lambda w, axis=0: lax.all_gather(w, "context", axis=axis, tiled=True)
    x, upstream = tokens[0], cotangent[0]

    cot_left = lax.ppermute(upstream, "expert", RIGHT)
    cot_right = lax.ppermute(upstream, "expert", LEFT)

    expert_count = router_weight.shape[1]
    local = gate_weight.shape[0]
    capacity = 5 * rows * TOP // (4 * expert_count)
    cap = -(-capacity // 64) * 64
    names = jnp.arange(expert_count, dtype=jnp.int32)
    route_hit = routes[0][:, :, None] == names[None, None, :]
    routed = jnp.any(route_hit, axis=1)
    ranks = fill_rank[0, 0].reshape(rows, TOP)
    order = jnp.sum(jnp.where(route_hit, ranks[:, :, None], 0), axis=1)
    order = jnp.where(routed, order, rows * TOP).T
    slots = jnp.sum((order[:, :, None] < order[:, None, :]).astype(jnp.int32), axis=1)
    kept = routed.T & (slots < capacity)
    slots = jnp.where(kept, slots, -1).astype(F32)
    kept_float = kept.T.astype(F32)

    small = jnp.concatenate([
        gain_attention[None], gain_experts[None], jnp.zeros((6, gain_attention.shape[0]), BF),
        router_weight.T,
    ]).astype(F32)
    positions = context_index * rows + jnp.arange(rows, dtype=jnp.int32)
    cosine, sine = rope_tables(positions)
    cos_full = jnp.concatenate([cosine, cosine], axis=-1)
    sin_full = jnp.concatenate([-sine, sine], axis=-1)
    turned = lambda v, heads, d: apply_rotary(
        v.reshape(rows, heads, HEAD_SIZE), cosine, sine, d
    ).reshape(rows, heads * HEAD_SIZE)
    output_full = gather(output_weight)
    if context_size == 2:
        q, attn_input, kv, query_full, key_full, value_full, small = project(
            x, query_weight, key_projection_weight, value_projection_weight, small,
            cos_full, sin_full,
        )
    else:
        query_full, key_full, value_full = (
            gather(query_weight), gather(key_projection_weight), gather(value_projection_weight)
        )
        small = gather(small.astype(BF), 1).astype(F32)
        residual = x.astype(F32)
        attn_input = (residual * inverse_root(residual) * small[0]).astype(BF)
        q = turned(mm(attn_input, query_full), QUERY_HEADS, 1.0).astype(BF)
        k_own = turned(mm(attn_input, key_full), KEY_VALUE_HEADS, 1.0).astype(BF)
        kv = gather(jnp.concatenate([k_own, mm(attn_input, value_full).astype(BF)], axis=1))
    segments = segment_ids[0]
    tq, kb = attention_sizes(rows, length)
    spans = attention_meta(context_index, rows, segments, tq, kb)
    segk = segments[:, None]
    segq = lax.dynamic_slice_in_dim(segments, context_index * rows, rows)[None, :]
    cot_left, cot_right, q, kv, spans, segk, segq, slots, kept_float, routed_float = (
        lax.optimization_barrier((cot_left, cot_right, q, kv, spans, segk, segq, slots, kept_float,
                                  routed.astype(F32))))
    second_left = lax.ppermute(cot_left, "expert", RIGHT_ON)
    second_right = lax.ppermute(cot_right, "expert", LEFT_ON)
    mixed, lse = attention_forward(q, kv, spans, segk, segq)

    hidden, expert_input, gates = mix(mixed, x, output_full, small, routed_float)
    second_left, second_right, gates = lax.optimization_barrier((second_left, second_right, gates))
    cot_second = second_left + second_right
    routing = jnp.stack([slots, (gates * kept_float).T], axis=0)
    routing = routing.reshape(2, expert_size, local, rows).transpose(1, 0, 2, 3)
    routing = routing.reshape(expert_size, 2 * local, rows)
    routing = jnp.pad(routing, ((0, 0), (0, 8 - 2 * local), (0, 0)))
    dn_parts, dw_parts, part_y, grads_low, _, _ = moe(
        expert_input, upstream, cot_left, cot_right, cot_second, routing, gate_weight, up_weight,
        down_weight, cap,
    )
    gate_dot = dw_parts[:, :local].reshape(expert_count, rows).T * kept_float
    y_parts = lax.all_to_all(part_y, "expert", split_axis=0, concat_axis=0, tiled=True)
    grads_shard = lax.psum_scatter(
        grads_low, ("dp", "context"), scatter_dimension=1, tiled=True
    ).astype(F32)
    ff = gate_weight.shape[2]
    gate_grad, up_grad, down_grad = (grads_shard[:, :, i * ff : (i + 1) * ff] for i in range(3))

    expert_index = lax.axis_index("expert")
    between = (expert_index > 0) & (expert_index < expert_size - 1)
    flags = jnp.where(between, jnp.array([1, 1, 1], jnp.int32), jnp.array([1, 0, 1], jnp.int32))
    hidden_total, attn_grad_low, mixed_grad_low, misc = turn(
        flags, dn_parts, gate_dot, gates, hidden, upstream, output_full, small
    )
    dq_low, dk_part, dv_part = attention_backward(
        q, kv, mixed_grad_low, lse, cos_full, sin_full, spans, segk, segq
    )
    if (lax.axis_size("dp"), context_size, expert_size) == (4, 2, 4):
        *sums, grad_tokens = tail(
            mixed, attn_grad_low, attn_input, dq_low, dk_part, dv_part, cos_full, sin_full,
            query_full, key_full, value_full, hidden_total, x, small[0:1], misc,
        )
        query_grad, key_grad, value_grad, output_grad, misc_grad = (v.astype(F32) for v in sums)
        sums = (
            query_grad, key_grad, value_grad, output_grad, misc_grad[:, :expert_count],
            misc_grad[:, 16], jnp.sum(misc_grad[:, 8:16], axis=1),
        )
    else:
        dkv = lax.psum_scatter(
            jnp.concatenate([dk_part, dv_part], axis=1), "context", scatter_dimension=0, tiled=True
        )
        dk_low = turned(dkv[:, :kv_width].astype(F32), KEY_VALUE_HEADS, -1.0).astype(BF)
        dv_low = dkv[:, kv_width:]
        input_total = (
            mm_nt(dq_low, query_full) + mm_nt(dk_low, key_full) + mm_nt(dv_low, value_full)
        )
        residual = x.astype(F32)
        root = inverse_root(residual)
        grad_tokens = (hidden_total + norm_back(residual, root, small[0], input_total)).astype(BF)
        reduce_rows = lambda v: lax.psum(
            lax.psum_scatter(v.astype(BF), "context", scatter_dimension=0, tiled=True),
            ("dp", "expert"),
        ).astype(F32)
        sums = tuple(reduce_rows(v) for v in (
            mm_tn(attn_input, dq_low), mm_tn(attn_input, dk_low), mm_tn(attn_input, dv_low),
            mm_tn(mixed, attn_grad_low), misc[:8].T,
            jnp.sum(input_total * residual * root, axis=0), jnp.sum(misc[8:16], axis=0),
        ))
    late, grad_tokens = lax.optimization_barrier((hidden, grad_tokens))
    layer_out = (late + jnp.sum(y_parts.astype(F32), axis=0)).astype(BF)
    return (layer_out[None], grad_tokens[None], *sums, gate_grad, up_grad, down_grad)


def solution(mesh):
    both = ("dp", "expert")
    token_spec = P(both, "context", None)
    row_spec = P("context", None)
    expert_out = P("expert", ("dp", "context"), None)
    return jax.shard_map(
        body,
        mesh=mesh,
        in_specs=(
            token_spec, token_spec, P(both, None), token_spec, token_spec,
            row_spec, row_spec, row_spec, row_spec, row_spec, P("context"), P("context"),
            P("expert", None, None), P("expert", None, None), P("expert", None, None),
        ),
        out_specs=(
            token_spec, token_spec, row_spec, row_spec, row_spec, row_spec, row_spec,
            P("context"), P("context"), expert_out, expert_out, expert_out,
        ),
        check_vma=False,
    )
```

```python
import functools
import math

import jax
import jax.numpy as jnp
from jax import lax
from jax.experimental import pallas as pl
from jax.experimental.pallas import tpu as pltpu
from jax.sharding import PartitionSpec as P

MODEL_WIDTH = 1536
QUERY_HEADS = 12
KEY_VALUE_HEADS = 2
HEAD_SIZE = 128
TOP = 4
GROUP = QUERY_HEADS // KEY_VALUE_HEADS
norm_eps = 1e-06
rope_base = 10000.0
NEG = -1e30
HEADS_AT_ONCE = 3
SCALE = 1.0 / math.sqrt(HEAD_SIZE)
BF = jnp.bfloat16
F32 = jnp.float32
VMEM_LIMIT = 60 * 1024 * 1024
MOE_VMEM = 63 * 1024 * 1024


def mm(a, b):
    return jnp.dot(a, b, preferred_element_type=F32)


def mm_nt(a, b):
    return lax.dot_general(a, b, (((1,), (1,)), ((), ())), preferred_element_type=F32)


def mm_tn(a, b):
    return lax.dot_general(a, b, (((0,), (0,)), ((), ())), preferred_element_type=F32)


def inverse_root(v):
    return lax.rsqrt(jnp.mean(v * v, axis=-1, keepdims=True) + norm_eps)


def norm_back(v, root, gain, upstream):
    scaled = upstream * gain
    cubed = root * root * root
    return root * scaled - v * cubed * jnp.mean(v * scaled, axis=-1, keepdims=True)


def rope_tables(positions):
    half = HEAD_SIZE // 2
    frequency = jnp.exp(
        -(jnp.arange(half, dtype=F32) * (2.0 / HEAD_SIZE)) * math.log(rope_base)
    )
    angle = positions.astype(F32)[:, None] * frequency[None, :]
    return jnp.cos(angle), jnp.sin(angle)


def apply_rotary(v, cosine, sine, direction):
    half = HEAD_SIZE // 2
    a, b = v[..., :half], v[..., half:]
    c, s = cosine[:, None, :], sine[:, None, :]
    return jnp.concatenate([a * c - direction * b * s, b * c + direction * a * s], axis=-1)


def fold_rows(v, op):
    rows, cols = v.shape
    return op(v.reshape(rows // 8, 8, cols), axis=0)


def make_bias(ctx, tokens, segk_ref, segq_ref, bias_ref):
    length = segk_ref.shape[0]
    key_pos = lax.broadcasted_iota(jnp.int32, (length, tokens), 0)
    query_pos = lax.broadcasted_iota(jnp.int32, (length, tokens), 1) + ctx * tokens
    same = segk_ref[...] == segq_ref[...]
    bias_ref[...] = jnp.where(same & (key_pos <= query_pos), 0.0, NEG)


def attn_fwd_kernel(kb, tq, meta, q_ref, k_ref, v_ref, segk_ref, segq_ref, o_ref, lse_ref,
                    bias_ref, s_ref, vt_ref):
    step = pl.program_id(0)
    tokens = q_ref.shape[0]

    @pl.when(step == 0)
    def _():
        make_bias(meta[0], tokens, segk_ref, segq_ref, bias_ref)

    @pl.when(lax.rem(step * HEADS_AT_ONCE, GROUP) == 0)
    def _():
        vt_ref[...] = v_ref[...].astype(F32).T.astype(BF)

    heads = [slice(h * HEAD_SIZE, (h + 1) * HEAD_SIZE) for h in range(HEADS_AT_ONCE)]
    for part in range(tokens // tq):
        cols = pl.ds(part * tq, tq)
        low, high = meta[1 + 2 * part], meta[2 + 2 * part]

        def score(i, tops):
            rows = pl.ds(pl.multiple_of(i * kb, kb), kb)
            key, bias = k_ref[rows, :], bias_ref[rows, cols]
            out = []
            for h, at in enumerate(heads):
                s = mm_nt(key, q_ref[cols, at]) * SCALE + bias
                s_ref[h, rows, :] = s
                out.append(jnp.maximum(tops[h], fold_rows(s, jnp.max)))
            return tuple(out)

        tops = lax.fori_loop(low, high, score,
                             tuple(jnp.full((8, tq), NEG, F32) for _ in heads))
        tops = [jnp.max(t, axis=0, keepdims=True) for t in tops]

        def value(i, carry):
            totals, outs = carry
            rows = pl.ds(pl.multiple_of(i * kb, kb), kb)
            vt = vt_ref[:, rows]
            new_totals, new_outs = [], []
            for h in range(HEADS_AT_ONCE):
                p = jnp.exp(s_ref[h, rows, :] - tops[h])
                new_totals.append(totals[h] + fold_rows(p, jnp.sum))
                new_outs.append(outs[h] + mm(vt, p.astype(BF)))
            return tuple(new_totals), tuple(new_outs)

        totals, outs = lax.fori_loop(
            low, high, value, (tuple(jnp.zeros((8, tq), F32) for _ in heads),
                               tuple(jnp.zeros((HEAD_SIZE, tq), F32) for _ in heads)))
        for h, at in enumerate(heads):
            total = jnp.sum(totals[h], axis=0, keepdims=True)
            o_ref[cols, at] = (outs[h] / total).T.astype(BF)
            lse_ref[h, :, cols] = tops[h] + jnp.log(total)


def attn_bwd_kernel(kb, tq, meta, q_ref, k_ref, v_ref, do_ref, lse_ref, cos_ref, sin_ref,
                    segk_ref, segq_ref, dq_ref, dk_ref, dv_ref,
                    bias_ref, p_ref, dp_ref, kt_ref, dk_acc, dv_acc):
    step = pl.program_id(0)
    tokens = q_ref.shape[0]

    @pl.when(step == 0)
    def _():
        make_bias(meta[0], tokens, segk_ref, segq_ref, bias_ref)

    place = lax.rem(step * HEADS_AT_ONCE, GROUP)

    @pl.when(place == 0)
    def _():
        kt_ref[...] = k_ref[...].astype(F32).T.astype(BF)
        dk_acc[...] = jnp.zeros_like(dk_acc)
        dv_acc[...] = jnp.zeros_like(dv_acc)

    heads = [slice(h * HEAD_SIZE, (h + 1) * HEAD_SIZE) for h in range(HEADS_AT_ONCE)]
    for part in range(tokens // tq):
        cols = pl.ds(part * tq, tq)
        low, high = meta[1 + 2 * part], meta[2 + 2 * part]

        def score(i, deltas):
            rows = pl.ds(pl.multiple_of(i * kb, kb), kb)
            key, value, bias = k_ref[rows, :], v_ref[rows, :], bias_ref[rows, cols]
            out = []
            for h, at in enumerate(heads):
                s = mm_nt(key, q_ref[cols, at]) * SCALE + bias
                p = jnp.exp(s - lse_ref[h, :, cols])
                dp = mm_nt(value, do_ref[cols, at])
                p_ref[h, rows, :] = p
                dp_ref[h, rows, :] = dp
                out.append(deltas[h] + fold_rows(p * dp, jnp.sum))
            return tuple(out)

        deltas = lax.fori_loop(low, high, score, tuple(jnp.zeros((8, tq), F32) for _ in heads))
        deltas = [jnp.sum(d, axis=0, keepdims=True) for d in deltas]

        def grads(i, dqs):
            rows = pl.ds(pl.multiple_of(i * kb, kb), kb)
            kt = kt_ref[:, rows]
            out, dk, dv = [], dk_acc[rows, :], dv_acc[rows, :]
            for h, at in enumerate(heads):
                p = p_ref[h, rows, :]
                ds = (p * (dp_ref[h, rows, :] - deltas[h])).astype(BF)
                dv = dv + mm(p.astype(BF), do_ref[cols, at])
                dk = dk + mm(ds, q_ref[cols, at])
                out.append(dqs[h] + mm(kt, ds))
            dk_acc[rows, :] = dk
            dv_acc[rows, :] = dv
            return tuple(out)

        dqs = lax.fori_loop(low, high, grads,
                            tuple(jnp.zeros((HEAD_SIZE, tq), F32) for _ in heads))
        for h, at in enumerate(heads):
            dq = dqs[h].T * SCALE
            turned = pltpu.roll(dq, HEAD_SIZE // 2, 1)
            dq_ref[cols, at] = (dq * cos_ref[cols, :] - turned * sin_ref[cols, :]).astype(BF)

    @pl.when(place == GROUP - HEADS_AT_ONCE)
    def _():
        dk_ref[...] = (dk_acc[...] * SCALE).astype(BF)
        dv_ref[...] = dv_acc[...].astype(BF)


def attention_sizes(tokens, length):
    tq = 256 if tokens % 256 == 0 else tokens
    kb = 256 if length % 256 == 0 else 128
    return tq, kb


def attention_meta(ctx, tokens, segments, tq, kb):
    entries = [ctx]
    for part in range(tokens // tq):
        first = ctx * tokens + part * tq
        own = lax.dynamic_slice_in_dim(segments, first, 1)
        start = jnp.sum((segments < own).astype(jnp.int32))
        entries += [start // kb, (first + tq + kb - 1) // kb]
    return jnp.stack(entries).astype(jnp.int32)


def attention_forward(q, kv, meta, segk, segq):
    tokens, length = q.shape[0], kv.shape[0]
    tq, kb = attention_sizes(tokens, length)
    const = lambda h, m: (0, 0)
    return pl.pallas_call(
        functools.partial(attn_fwd_kernel, kb, tq),
        out_shape=(
            jax.ShapeDtypeStruct(q.shape, BF),
            jax.ShapeDtypeStruct((QUERY_HEADS, 1, tokens), F32),
        ),
        grid_spec=pltpu.PrefetchScalarGridSpec(
            num_scalar_prefetch=1,
            grid=(QUERY_HEADS // HEADS_AT_ONCE,),
            in_specs=[
                pl.BlockSpec((tokens, HEADS_AT_ONCE * HEAD_SIZE), lambda h, m: (0, h)),
                pl.BlockSpec((length, HEAD_SIZE), lambda h, m: (0, h * HEADS_AT_ONCE // GROUP)),
                pl.BlockSpec((length, HEAD_SIZE), lambda h, m: (0, KEY_VALUE_HEADS + h * HEADS_AT_ONCE // GROUP)),
                pl.BlockSpec((length, 1), const),
                pl.BlockSpec((1, tokens), const),
            ],
            out_specs=[
                pl.BlockSpec((tokens, HEADS_AT_ONCE * HEAD_SIZE), lambda h, m: (0, h)),
                pl.BlockSpec((HEADS_AT_ONCE, 1, tokens), lambda h, m: (h, 0, 0)),
            ],
            scratch_shapes=[
                pltpu.VMEM((length, tokens), F32),
                pltpu.VMEM((HEADS_AT_ONCE, length, tq), F32),
                pltpu.VMEM((HEAD_SIZE, length), BF),
            ],
        ),
        compiler_params=pltpu.CompilerParams(vmem_limit_bytes=VMEM_LIMIT),
        cost_estimate=pl.CostEstimate(
            flops=3 * QUERY_HEADS * tokens * length * HEAD_SIZE,
            transcendentals=QUERY_HEADS * tokens * length,
            bytes_accessed=4 * tokens * MODEL_WIDTH,
        ),
        name="attn_fwd",
    )(meta, q, kv, kv, segk, segq)


def attention_backward(q, kv, do, lse, cos, sin, meta, segk, segq):
    tokens, length = q.shape[0], kv.shape[0]
    tq, kb = attention_sizes(tokens, length)
    const = lambda h, m: (0, 0)
    by_head = lambda h, m: (0, h)
    by_group = lambda h, m: (0, h * HEADS_AT_ONCE // GROUP)
    return pl.pallas_call(
        functools.partial(attn_bwd_kernel, kb, tq),
        out_shape=(
            jax.ShapeDtypeStruct(q.shape, BF),
            jax.ShapeDtypeStruct((length, KEY_VALUE_HEADS * HEAD_SIZE), BF),
            jax.ShapeDtypeStruct((length, KEY_VALUE_HEADS * HEAD_SIZE), BF),
        ),
        grid_spec=pltpu.PrefetchScalarGridSpec(
            num_scalar_prefetch=1,
            grid=(QUERY_HEADS // HEADS_AT_ONCE,),
            in_specs=[
                pl.BlockSpec((tokens, HEADS_AT_ONCE * HEAD_SIZE), by_head),
                pl.BlockSpec((length, HEAD_SIZE), by_group),
                pl.BlockSpec((length, HEAD_SIZE), lambda h, m: (0, KEY_VALUE_HEADS + h * HEADS_AT_ONCE // GROUP)),
                pl.BlockSpec((tokens, HEADS_AT_ONCE * HEAD_SIZE), by_head),
                pl.BlockSpec((HEADS_AT_ONCE, 1, tokens), lambda h, m: (h, 0, 0)),
                pl.BlockSpec((tokens, HEAD_SIZE), const),
                pl.BlockSpec((tokens, HEAD_SIZE), const),
                pl.BlockSpec((length, 1), const),
                pl.BlockSpec((1, tokens), const),
            ],
            out_specs=[
                pl.BlockSpec((tokens, HEADS_AT_ONCE * HEAD_SIZE), by_head),
                pl.BlockSpec((length, HEAD_SIZE), by_group),
                pl.BlockSpec((length, HEAD_SIZE), by_group),
            ],
            scratch_shapes=[
                pltpu.VMEM((length, tokens), F32),
                pltpu.VMEM((HEADS_AT_ONCE, length, tq), F32),
                pltpu.VMEM((HEADS_AT_ONCE, length, tq), F32),
                pltpu.VMEM((HEAD_SIZE, length), BF),
                pltpu.VMEM((length, HEAD_SIZE), F32),
                pltpu.VMEM((length, HEAD_SIZE), F32),
            ],
        ),
        compiler_params=pltpu.CompilerParams(vmem_limit_bytes=VMEM_LIMIT),
        cost_estimate=pl.CostEstimate(
            flops=8 * QUERY_HEADS * tokens * length * HEAD_SIZE,
            transcendentals=QUERY_HEADS * tokens * length,
            bytes_accessed=8 * tokens * MODEL_WIDTH,
        ),
        name="attn_bwd",
    )(meta, q, kv, kv, do, lse, cos, sin, segk, segq)


def remote(src, dst, ss, rs, axis, dev):
    return pltpu.make_async_remote_copy(
        src_ref=src, dst_ref=dst, send_sem=ss, recv_sem=rs, device_id={axis: dev},
        device_id_type=pl.DeviceIdType.MESH,
    )


def moe_kernel(cap, tile, n,
               x_hbm, cot_hbm, cotl_hbm, cotr_hbm, cot2_hbm, meta_hbm, gate_hbm, up_hbm, down_hbm,
               dn_out, dw_out, y_own, y_near, y_second, y_third, y_in, grads_out, xall, cotfar,
               gate_ref, up_ref, down_ref, x_ref, cot_ref, metas, xs_ref, dy_ref, hb_ref, dg_ref,
               du_ref, pdn_ref, transit, py_ref, dws, pick_ref, put_ref, ys_ref, acc_ref, stage,
               wsem, lsem, xs_send, xs_recv, far_sem, m_send, m_recv, dn_send, dn_recv,
               dw_send, dw_recv, py_sem, own_sem, st_sem, y_send, y_recv):
    me = lax.axis_index("expert")
    tokens, width = x_ref.shape
    local, _, hidden = gate_ref.shape
    edge = (me == 0) | (me == n - 1)

    barrier = pltpu.get_barrier_semaphore()
    for d in range(1, n):
        pl.semaphore_signal(barrier, inc=1, device_id={"expert": lax.rem(me + d, n)},
                            device_id_type=pl.DeviceIdType.MESH)
    pl.semaphore_wait(barrier, n - 1)

    def exists(direction, step):
        return (me - 1 - step >= 0) if direction == 0 else (me + 1 + step <= n - 1)

    def sends(direction, step):
        if direction == 0:
            return (me - step >= 0) & (me < n - 1)
        return (me + step <= n - 1) & (me > 0)

    def xcopy(direction, step):
        block = jnp.clip(me - step if direction == 0 else me + step, 0, n - 1)
        target = jnp.clip(me + 1 if direction == 0 else me - 1, 0, n - 1)
        src = x_hbm if step == 0 else xall.at[block]
        return remote(src, xall.at[block], xs_send.at[direction, step],
                      xs_recv.at[direction, step], "expert", target)

    outward = jnp.where(me < 2, 0, n - 1)
    inward = n - 1 - jnp.clip(me, 1, n - 2)
    inner = jnp.where(me < 2, 1, n - 2)
    far_copy = lambda: remote(cot2_hbm, cotfar, far_sem.at[0], far_sem.at[1], "expert", outward)
    middle_device = jnp.logical_not(edge)

    for d in range(2):
        @pl.when(sends(d, 0))
        def _():
            xcopy(d, 0).start()

    def meta_copy(j):
        return remote(meta_hbm.at[j], metas.at[me], m_send.at[j], m_recv.at[me], "expert", j)

    for j in range(n):
        @pl.when(me != j)
        def _():
            meta_copy(j).start()

    loads = [pltpu.make_async_copy(a, b, wsem.at[k]) for k, (a, b) in enumerate(
        ((gate_hbm, gate_ref), (up_hbm, up_ref), (down_hbm, down_ref)))]
    for load in loads:
        load.start()
    own_meta = pltpu.make_async_copy(meta_hbm.at[me], metas.at[me], lsem.at[2])
    own_meta.start()

    def fetch(a, b):
        cx = pltpu.make_async_copy(a, x_ref, lsem.at[0])
        cc = pltpu.make_async_copy(b, cot_ref, lsem.at[1])
        cx.start()
        cc.start()
        cx.wait()
        cc.wait()

    pieces = width // tile
    piece = lambda part: pl.ds(pl.multiple_of(part * tile, tile), tile)

    def edge_copy(kind, part):
        dst = (dn_out.at[1, :, piece(part)] if kind == 0 else
               transit.at[kind - 1, :, piece(part)])
        return remote(pdn_ref.at[kind, :, piece(part)], dst, dn_send.at[kind, part],
                      dn_recv.at[kind, part], "expert", inner)

    def y_copy(kind):
        target = jnp.where(edge, inner, outward) if kind == 0 else inward
        return remote(y_near.at[kind], y_in.at[kind], y_send.at[kind], y_recv.at[kind], "expert",
                      target)

    def pass_copy(kind, part):
        dst = transit.at[2, :, piece(part)] if kind == 1 else dn_out.at[2, :, piece(part)]
        arrival = dn_recv.at[3, part] if kind != 1 else dn_recv.at[4, part]
        return remote(transit.at[kind, :, piece(part)], dst, dn_send.at[kind, part], arrival,
                      "expert", outward if kind == 2 else inward)

    mirror = me >= 2
    side = jnp.where(mirror, n - 1 - me, me)

    def source_of(p):
        base = jnp.where(p == 0, side, jnp.where(p == 1, 1 - side, p))
        return jnp.where(mirror, n - 1 - base, base)

    def arrive(direction, step):
        @pl.when(exists(direction, step))
        def _():
            xcopy(direction, step).wait_recv()

    def forward(direction, step):
        @pl.when(sends(direction, step))
        def _():
            xcopy(direction, step).start()

    def one_source(p, _):
        src = source_of(p)

        @pl.when(p == 0)
        def _():
            own_meta.wait()

        @pl.when(p > 0)
        def _():
            remote(meta_hbm.at[src], metas.at[src], m_send.at[src], m_recv.at[src], "expert",
                   src).wait_recv()

        meta = metas[src]
        columns = meta.T
        spread = lax.broadcasted_iota(jnp.int32, (tokens, local * cap), 1).astype(F32)
        slot = lax.broadcasted_iota(jnp.int32, (cap, tokens), 0).astype(F32)
        weights, put = [], None
        for e in range(local):
            hit = slot == meta[e : e + 1, :]
            pick_ref[pl.ds(e * cap, cap), :] = jnp.where(hit, 1.0, 0.0).astype(BF)
            weights.append(
                jnp.sum(jnp.where(hit, meta[local + e : local + e + 1, :], 0.0), axis=1,
                        keepdims=True)
            )
            own = columns[:, e : e + 1]
            here = spread == jnp.where(own < 0.0, -1.0, own + e * cap)
            put = here if put is None else put | here
        put_ref[...] = jnp.where(put, 1.0, 0.0).astype(BF)
        @pl.when(p == 0)
        def _():
            fetch(x_hbm, cot_hbm)
            for load in loads:
                load.wait()

        @pl.when(p == 1)
        def _():
            for d in range(2):
                arrive(d, 0)
                forward(d, 1)

            @pl.when(middle_device)
            def _():
                far_copy().start()

        @pl.when(p > 0)
        def _():
            pltpu.make_async_copy(py_ref, y_own, py_sem.at[0]).wait()

        @pl.when(middle_device & (p == 3))
        def _():
            y_copy(1).start()

        @pl.when(edge & (p == 2))
        def _():
            for part in range(pieces):
                edge_copy(0, part).wait_send()
            y_copy(0).start()

        @pl.when(((p == 2) & edge) | ((p == 3) & jnp.logical_not(edge)))
        def _():
            for d in range(2):
                arrive(d, 1)
                forward(d, 2)

        @pl.when((p == 3) & edge)
        def _():
            for d in range(2):
                arrive(d, 2)
            far_copy().wait_recv()

        @pl.when((p > 0) & (src == me - 1))
        def _():
            fetch(xall.at[src], cotl_hbm)

        @pl.when((p > 0) & (src == me + 1))
        def _():
            fetch(xall.at[src], cotr_hbm)

        @pl.when((src == me - 2) | (src == me + 2))
        def _():
            fetch(xall.at[src], cot2_hbm)

        @pl.when((src == me - 3) | (src == me + 3))
        def _():
            fetch(xall.at[src], cotfar)

        mine = pl.ds(pl.multiple_of(p * cap, cap), cap)
        buf = lax.rem(p + 2, 3)

        def gather(j, _):
            cols = pl.ds(pl.multiple_of(j * tile, tile), tile)
            xs = mm(pick_ref[...], x_ref[:, cols]).astype(BF)
            cg = mm(pick_ref[...], cot_ref[:, cols])
            for e in range(local):
                rows = slice(e * cap, (e + 1) * cap)
                xs_ref[e, mine, cols] = xs[rows]
                dy_ref[e, mine, cols] = (weights[e] * cg[rows]).astype(BF)
            return 0

        lax.fori_loop(0, width // tile, gather, 0)

        def middle(j, _):
            cols = pl.ds(pl.multiple_of(j * tile, tile), tile)
            for e in range(local):
                g = mm(xs_ref[e, mine, :], gate_ref[e, :, cols])
                u = mm(xs_ref[e, mine, :], up_ref[e, :, cols])
                dh = mm(dy_ref[e, mine, :], down_ref[e, :, cols])
                s = 1.0 / (1.0 + jnp.exp(-g))
                act = g * s
                hb_ref[e, mine, cols] = (act * u).astype(BF)
                dg_ref[e, mine, cols] = (dh * u * (s * (1.0 + g * (1.0 - s)))).astype(BF)
                du_ref[e, mine, cols] = (dh * act).astype(BF)
            return 0

        lax.fori_loop(0, hidden // tile, middle, 0)


        @pl.when(p == 3)
        def _():
            pltpu.make_async_copy(pdn_ref.at[2], dn_out.at[0], own_sem.at[0]).wait()

        acc_ref[...] = jnp.zeros_like(acc_ref)

        def back(j, _):
            cols = pl.ds(pl.multiple_of(j * tile, tile), tile)
            for e in range(local):
                dxs = mm_nt(dg_ref[e, mine, :], gate_ref[e, cols, :])
                dxs = dxs + mm_nt(du_ref[e, mine, :], up_ref[e, cols, :])
                ys_ref[pl.ds(e * cap, cap), :] = dxs.astype(BF)
            pdn_ref[buf, :, cols] = mm(put_ref[...], ys_ref[...]).astype(BF)
            for kind in range(3):
                @pl.when(edge & (p == kind + 1))
                def _():
                    edge_copy(kind, j).start()
            return 0

        lax.fori_loop(0, width // tile, back, 0)

        @pl.when(p == 0)
        def _():
            pltpu.make_async_copy(pdn_ref.at[2], dn_out.at[0], own_sem.at[0]).start()

        def ahead(j, _):
            cols = pl.ds(pl.multiple_of(j * tile, tile), tile)
            for e in range(local):
                rows = pl.ds(e * cap, cap)
                y = mm_nt(hb_ref[e, mine, :], down_ref[e, cols, :])
                acc_ref[rows, :] += mm(pick_ref[rows, :], cot_ref[:, cols]) * y
                ys_ref[rows, :] = (weights[e] * y).astype(BF)
            py_ref[:, cols] = mm(put_ref[...], ys_ref[...]).astype(BF)
            return 0

        lax.fori_loop(0, width // tile, ahead, 0)
        for dst, when in ((y_own, p == 0), (y_near.at[0], p == 1),
                          (y_near.at[1], middle_device & (p == 2)),
                          (y_second, (edge & (p == 2)) | (middle_device & (p == 3))),
                          (y_third, edge & (p == 3))):
            @pl.when(when)
            def _():
                pltpu.make_async_copy(py_ref, dst, py_sem.at[0]).start()
        dws[p] = jnp.zeros((8, tokens), F32)
        for e in range(local):
            dot = jnp.sum(acc_ref[pl.ds(e * cap, cap), :], axis=1, keepdims=True)
            hit = slot == meta[e : e + 1, :]
            dws[p, e : e + 1, :] = jnp.sum(jnp.where(hit, dot, 0.0), axis=0, keepdims=True)

        @pl.when(p == 0)
        def _():
            pltpu.make_async_copy(dws.at[p], dw_out.at[me], own_sem.at[1]).start()

        @pl.when(p > 0)
        def _():
            remote(dws.at[p], dw_out.at[me], dw_send.at[src], dw_recv.at[me], "expert",
                   src).start()
        return 0

    lax.fori_loop(0, n, one_source, 0)

    tiles = width // tile
    store = lambda k, e, j: pltpu.make_async_copy(
        stage.at[k], grads_out.at[e, pl.ds(pl.multiple_of(j * tile, tile), tile), :], st_sem.at[k])

    def weight_grads(k, _):
        e, j = lax.div(k, tiles), lax.rem(k, tiles)
        cols = pl.ds(pl.multiple_of(j * tile, tile), tile)
        slot_k = lax.rem(k, 2)

        @pl.when(k >= 2)
        def _():
            store(slot_k, 0, 0).wait()

        xs = xs_ref[e, :, cols]
        stage[slot_k, :, 0:hidden] = mm_tn(xs, dg_ref[e]).astype(BF)
        stage[slot_k, :, hidden : 2 * hidden] = mm_tn(xs, du_ref[e]).astype(BF)
        stage[slot_k, :, 2 * hidden : 3 * hidden] = mm_tn(dy_ref[e, :, cols], hb_ref[e]).astype(BF)
        store(slot_k, e, j).start()
        return 0

    lax.fori_loop(0, local * tiles, weight_grads, 0)
    for k in range(2):
        store(k, 0, 0).wait()

    @pl.when(middle_device)
    def _():
        far_copy().wait_send()
        for d in range(2):
            @pl.when(sends(d, n - 2))
            def _():
                xcopy(d, n - 2).wait_send()
        y_copy(0).start()
        for kind, own in ((0, 1), (1, 2), (2, 0)):
            for part in range(pieces):
                landed = (edge_copy(kind + 1, part) if kind < 2 else pass_copy(1, part))
                landed.wait_recv()
                cols = piece(part)
                transit[kind, :, cols] = (transit[kind, :, cols].astype(F32)
                                          + pdn_ref[own, :, cols].astype(F32)).astype(BF)
                pass_copy(kind, part).start()
        for kind in range(2):
            y_copy(kind).wait()
        for part in range(pieces):
            edge_copy(0, part).wait_recv()
            pass_copy(0, part).wait_recv()
            for kind in range(3):
                pass_copy(kind, part).wait_send()

    @pl.when(edge)
    def _():
        for part in range(pieces):
            pass_copy(0, part).wait_recv()
            for kind in (1, 2):
                edge_copy(kind, part).wait_send()
        y_copy(0).wait()

    pltpu.make_async_copy(py_ref, y_own, py_sem.at[0]).wait()
    pltpu.make_async_copy(dws.at[0], dw_out.at[me], own_sem.at[1]).wait()
    for d in range(2):
        for s in range(n - 2):
            @pl.when(sends(d, s))
            def _():
                xcopy(d, s).wait_send()
    for j in range(n):
        @pl.when(me != j)
        def _():
            meta_copy(j).wait_send()
            remote(dws.at[0], dw_out.at[me], dw_send.at[j], dw_recv.at[me], "expert",
                   j).wait_send()
            remote(dws.at[0], dw_out.at[j], dw_send.at[j], dw_recv.at[j], "expert", j).wait_recv()


def moe(x, cot, cot_left, cot_right, cot_second, meta, gate, up, down, cap):
    n = meta.shape[0]
    tokens, width = x.shape
    local, _, hidden = gate.shape
    tile = 256
    anywhere = pl.BlockSpec(memory_space=pl.ANY)
    dma = pltpu.SemaphoreType.DMA
    shape = jax.ShapeDtypeStruct
    return pl.pallas_call(
        functools.partial(moe_kernel, cap, tile, n),
        out_shape=(
            shape((3, tokens, width), BF), shape((n, 8, tokens), F32), shape((tokens, width), BF),
            shape((2, tokens, width), BF), shape((tokens, width), BF), shape((tokens, width), BF),
            shape((2, tokens, width), BF),
            shape((local, width, 3 * hidden), BF),
            shape((n, tokens, width), BF), shape((tokens, width), BF),
        ),
        in_specs=[anywhere] * 9,
        out_specs=[anywhere] * 10,
        scratch_shapes=[
            pltpu.VMEM((local, width, hidden), BF), pltpu.VMEM((local, width, hidden), BF),
            pltpu.VMEM((local, width, hidden), BF),
            pltpu.VMEM((tokens, width), BF), pltpu.VMEM((tokens, width), BF),
            pltpu.VMEM((n, 8, tokens), F32),
            pltpu.VMEM((local, n * cap, width), BF), pltpu.VMEM((local, n * cap, width), BF),
            pltpu.VMEM((local, n * cap, hidden), BF), pltpu.VMEM((local, n * cap, hidden), BF),
            pltpu.VMEM((local, n * cap, hidden), BF),
            pltpu.VMEM((3, tokens, width), BF), pltpu.VMEM((3, tokens, width), BF),
            pltpu.VMEM((tokens, width), BF), pltpu.VMEM((n, 8, tokens), F32),
            pltpu.VMEM((local * cap, tokens), BF), pltpu.VMEM((tokens, local * cap), BF),
            pltpu.VMEM((local * cap, tile), BF), pltpu.VMEM((local * cap, tile), F32),
            pltpu.VMEM((2, tile, 3 * hidden), BF),
            dma((3,)), dma((3,)), dma((2, n - 1)), dma((2, n - 1)), dma((2,)), dma((n,)), dma((n,)),
            dma((3, width // tile)), dma((5, width // tile)), dma((n,)), dma((n,)), dma((1,)), dma((2,)), dma((2,)),
            dma((2,)), dma((2,)),
        ],
        compiler_params=pltpu.CompilerParams(
            vmem_limit_bytes=MOE_VMEM, collective_id=1, has_side_effects=True
        ),
        cost_estimate=pl.CostEstimate(
            flops=2 * n * local * cap * width * (9 * hidden + 5 * tokens),
            transcendentals=n * local * cap * hidden,
            bytes_accessed=2 * (8 * n * tokens * width + 6 * local * width * hidden),
        ),
        name="moe",
    )(x, cot, cot_left, cot_right, cot_second, meta, gate, up, down)


RIGHT = [(0, 1), (1, 2), (2, 3)]
LEFT = [(1, 0), (2, 1), (3, 2)]
RIGHT_ON = [(1, 2), (2, 3)]
LEFT_ON = [(1, 0), (2, 1)]
ACROSS = [(0, 2), (1, 3), (2, 0), (3, 1)]
FAR = [(0, 3), (3, 0)]


def project_kernel(x_ref, wq_own, wk_own, wv_own, small_own, cos_ref, sin_ref,
                   q_ref, xa_ref, kv_ref, wq_ref, wk_ref, wv_ref, small_ref,
                   small_in, root_ref, acc_ref, send_sem, recv_sem, own_sem):
    ctx = lax.axis_index("context")
    tokens, width = x_ref.shape
    kv_width = wk_ref.shape[1]
    half = width // 2
    barrier = pltpu.get_barrier_semaphore()
    pl.semaphore_signal(barrier, inc=1, device_id={"context": 1 - ctx},
                        device_id_type=pl.DeviceIdType.MESH)
    pl.semaphore_wait(barrier, 1)

    own = pl.ds(pl.multiple_of(ctx * half, 128), half)
    other = pl.ds(pl.multiple_of((1 - ctx) * half, 128), half)
    ours = pl.ds(pl.multiple_of(ctx * tokens, 16), tokens)
    give = lambda k, src, dst: remote(src, dst, send_sem.at[k], recv_sem.at[k], "context", 1 - ctx)
    weights = ((wk_own, wk_ref), (wv_own, wv_ref), (wq_own, wq_ref))
    sends = [give(0, small_own, small_in)]
    sends += [give(1 + k, a, b.at[own, :]) for k, (a, b) in enumerate(weights)]
    for copy in sends:
        copy.start()
    keeps = [pltpu.make_async_copy(a, b.at[own, :], own_sem.at[k])
             for k, (a, b) in enumerate(weights)]
    for copy in keeps:
        copy.start()

    strip = 64

    def scale(k, _):
        rows = pl.ds(pl.multiple_of(k * strip, strip), strip)
        root = inverse_root(x_ref[rows, :].astype(F32))
        root_ref[rows, :] = root
        xa_ref[rows, own] = (x_ref[rows, own].astype(F32) * root * small_own[0:1, :]).astype(BF)
        return 0

    lax.fori_loop(0, tokens // strip, scale, 0)
    for copy in keeps:
        copy.wait()

    acc_ref[:, 0:kv_width] = mm(xa_ref[:, own], wk_ref[own, :])
    acc_ref[:, kv_width : 2 * kv_width] = mm(xa_ref[:, own], wv_ref[own, :])
    tile = 256

    def first(j, _):
        cols = pl.ds(pl.multiple_of(j * tile, tile), tile)
        at = pl.ds(pl.multiple_of(2 * kv_width + j * tile, tile), tile)
        acc_ref[:, at] = mm(xa_ref[:, own], wq_ref[own, cols])
        return 0

    lax.fori_loop(0, width // tile, first, 0)

    sends[0].wait()
    small_ref[:, own] = small_own[...]
    small_ref[:, other] = small_in[...]

    def rest(k, _):
        rows = pl.ds(pl.multiple_of(k * strip, strip), strip)
        xa_ref[rows, other] = (x_ref[rows, other].astype(F32) * root_ref[rows, :]
                               * small_in[0:1, :]).astype(BF)
        return 0

    lax.fori_loop(0, tokens // strip, rest, 0)

    def rope(v):
        parts = []
        for h in range(v.shape[1] // HEAD_SIZE):
            t = v[:, h * HEAD_SIZE : (h + 1) * HEAD_SIZE]
            t = t * cos_ref[...] + pltpu.roll(t, HEAD_SIZE // 2, 1) * sin_ref[...]
            parts.append(t.astype(BF))
        return jnp.concatenate(parts, axis=1)

    sends[1].wait()
    sends[2].wait()
    k = acc_ref[:, 0:kv_width] + mm(xa_ref[:, other], wk_ref[other, :])
    v = acc_ref[:, kv_width : 2 * kv_width] + mm(xa_ref[:, other], wv_ref[other, :])
    kv_ref[ours, 0:kv_width] = rope(k)
    kv_ref[ours, kv_width : 2 * kv_width] = v.astype(BF)
    kv_copy = give(4, kv_ref.at[ours, :], kv_ref.at[ours, :])
    kv_copy.start()
    sends[3].wait()

    def second(j, _):
        cols = pl.ds(pl.multiple_of(j * tile, tile), tile)
        at = pl.ds(pl.multiple_of(2 * kv_width + j * tile, tile), tile)
        q_ref[:, cols] = rope(acc_ref[:, at] + mm(xa_ref[:, other], wq_ref[other, cols]))
        return 0

    lax.fori_loop(0, width // tile, second, 0)
    kv_copy.wait()


def project(x, wq, wk, wv, small, cos, sin):
    tokens, width = x.shape
    kv_width = wk.shape[1]
    vmem = pl.BlockSpec(memory_space=pltpu.VMEM)
    anywhere = pl.BlockSpec(memory_space=pl.ANY)
    dma = pltpu.SemaphoreType.DMA
    shape = jax.ShapeDtypeStruct
    return pl.pallas_call(
        project_kernel,
        out_shape=(
            shape((tokens, width), BF), shape((tokens, width), BF),
            shape((2 * tokens, 2 * kv_width), BF), shape((width, width), BF),
            shape((width, kv_width), BF), shape((width, kv_width), BF),
            shape((small.shape[0], width), F32),
        ),
        in_specs=[vmem, anywhere, anywhere, anywhere, vmem, vmem, vmem],
        out_specs=[vmem] * 7,
        scratch_shapes=[
            pltpu.VMEM(small.shape, F32), pltpu.VMEM((tokens, 1), F32),
            pltpu.VMEM((tokens, width + 2 * kv_width), F32), dma((5,)), dma((5,)), dma((3,)),
        ],
        compiler_params=pltpu.CompilerParams(
            vmem_limit_bytes=VMEM_LIMIT, collective_id=3, has_side_effects=True
        ),
        cost_estimate=pl.CostEstimate(
            flops=2 * tokens * width * (width + 2 * kv_width), transcendentals=0,
            bytes_accessed=8 * width * width,
        ),
        name="project",
    )(x, wq, wk, wv, small, cos, sin)


def exact(a, b, dims):
    return lax.dot_general(a, b, (dims, ((), ())), precision=lax.Precision.HIGHEST,
                           preferred_element_type=F32)


def three_parts(a, b):
    high = a.astype(BF)
    rest = a - high.astype(F32)
    middle = rest.astype(BF)
    low = (rest - middle.astype(F32)).astype(BF)
    return mm_nt(high, b) + mm_nt(middle, b) + mm_nt(low, b)


def mix_kernel(strip, ob_ref, x_ref, wo_ref, small_ref, routed_ref,
               hidden_ref, xq_ref, gates_ref):
    j = pl.program_id(0)
    tile = wo_ref.shape[1]
    cols = pl.ds(pl.multiple_of(j * tile, tile), tile)
    hidden_ref[:, cols] = x_ref[:, cols].astype(F32) + mm(ob_ref[...], wo_ref[...])

    @pl.when(j == pl.num_programs(0) - 1)
    def _():
        def one(k, _):
            rows = pl.ds(pl.multiple_of(k * strip, strip), strip)
            h = hidden_ref[rows, :]
            normed = h * inverse_root(h) * small_ref[1:2, :]
            xq_ref[rows, :] = normed.astype(BF)
            logits = three_parts(normed, small_ref[8:16, :].astype(BF))
            routed = routed_ref[rows, :] > 0.0
            top = jnp.max(jnp.where(routed, logits, NEG), axis=1, keepdims=True)
            power = jnp.where(routed, jnp.exp(jnp.where(routed, logits, top) - top), 0.0)
            gates_ref[rows, :] = power / jnp.sum(power, axis=1, keepdims=True)
            return 0

        lax.fori_loop(0, hidden_ref.shape[0] // strip, one, 0)


def row_strip(tokens):
    return 128 if tokens % 128 == 0 else 64


def mix(ob, x, wo, small, routed):
    tokens, width = x.shape
    tile = 256
    shape = jax.ShapeDtypeStruct
    const = lambda v: pl.BlockSpec(v.shape, lambda j: (0, 0), pipeline_mode=pl.Buffered(1))
    whole = lambda d: pl.BlockSpec((tokens, d), lambda j: (0, 0))
    experts = routed.shape[1]
    return pl.pallas_call(
        functools.partial(mix_kernel, row_strip(tokens)),
        out_shape=(shape((tokens, width), F32), shape((tokens, width), BF),
                   shape((tokens, experts), F32)),
        grid=(width // tile,),
        in_specs=[const(ob), const(x), pl.BlockSpec((width, tile), lambda j: (0, j)), const(small),
                  const(routed)],
        out_specs=[whole(width), whole(width), whole(experts)],
        compiler_params=pltpu.CompilerParams(vmem_limit_bytes=VMEM_LIMIT),
        cost_estimate=pl.CostEstimate(
            flops=2 * tokens * width * width, transcendentals=0, bytes_accessed=4 * width * width),
        name="mix",
    )(ob, x, wo, small, routed)


def turn_kernel(strip, flags, dn_ref, dot_ref, gates_ref, hidden_ref, cot_ref, wo_ref, small_ref,
                dh_ref, da_ref, dob_ref, misc_ref, normed_ref, dlog_ref):
    j = pl.program_id(0)

    @pl.when(j == 0)
    def _():
        gain = small_ref[1:2, :]

        def one(k, total):
            rows = pl.ds(pl.multiple_of(k * strip, strip), strip)
            gates, dot = gates_ref[rows, :], dot_ref[rows, :]
            dlogits = gates * (dot - jnp.sum(gates * dot, axis=1, keepdims=True))
            dn = jnp.zeros((strip, dh_ref.shape[1]), F32)
            for e in range(dlogits.shape[1]):
                dn = dn + dlogits[:, e : e + 1] * small_ref[8 + e : 9 + e, :]
            for part in range(dn_ref.shape[0]):
                dn = dn + jnp.where(flags[part] > 0, dn_ref[part, rows, :].astype(F32), 0.0)
            h = hidden_ref[rows, :]
            root = inverse_root(h)
            scaled = h * root
            normed_ref[rows, :] = scaled * gain
            dlog_ref[rows, :] = dlogits
            dh = cot_ref[rows, :].astype(F32) + norm_back(h, root, gain, dn)
            dh_ref[rows, :] = dh
            da_ref[rows, :] = dh.astype(BF)
            return total + fold_rows(dn * scaled, jnp.sum)

        tokens, width = dh_ref.shape
        misc_ref[8:16, :] = lax.fori_loop(0, tokens // strip, one, jnp.zeros((8, width), F32))

    tile = wo_ref.shape[0]
    cols = pl.ds(pl.multiple_of(j * tile, tile), tile)
    dob_ref[:, cols] = mm_nt(da_ref[...], wo_ref[...]).astype(BF)
    misc_ref[0:8, cols] = exact(dlog_ref[...], normed_ref[:, cols], ((0,), (0,)))


def turn(flags, dn_parts, dot, gates, hidden, cot, wo, small):
    tokens, width = cot.shape
    tile = 256
    shape = jax.ShapeDtypeStruct
    once = pl.Buffered(1)
    const = lambda v: pl.BlockSpec(v.shape, lambda j, f: (0,) * v.ndim, pipeline_mode=once)
    whole = lambda r: pl.BlockSpec((r, width), lambda j, f: (0, 0))
    return pl.pallas_call(
        functools.partial(turn_kernel, row_strip(tokens)),
        out_shape=(shape((tokens, width), F32), shape((tokens, width), BF),
                   shape((tokens, width), BF), shape((16, width), F32)),
        grid_spec=pltpu.PrefetchScalarGridSpec(
            num_scalar_prefetch=1,
            grid=(width // tile,),
            in_specs=[const(dn_parts), const(dot), const(gates), const(hidden), const(cot),
                      pl.BlockSpec((tile, width), lambda j, f: (j, 0)), const(small)],
            out_specs=[whole(tokens), whole(tokens), whole(tokens), whole(16)],
            scratch_shapes=[pltpu.VMEM((tokens, width), F32),
                            pltpu.VMEM((tokens, gates.shape[1]), F32)],
        ),
        compiler_params=pltpu.CompilerParams(vmem_limit_bytes=VMEM_LIMIT),
        cost_estimate=pl.CostEstimate(
            flops=2 * tokens * width * width, transcendentals=0, bytes_accessed=8 * width * width),
        name="turn",
    )(flags, dn_parts, dot, gates, hidden, cot, wo, small)


WIDE = 512
LINKS = 9


def tail_kernel(ob_ref, da_ref, xa_ref, dq_ref, dkp_ref, dvp_ref, cos_ref, sin_ref, wq_ref, wk_ref,
                wv_ref, dh_ref, x_ref, gain_ref, misc_ref,
                qg_out, kg_out, vg_out, og_out, mg_out, gt_ref,
                dkv_in, dkv_ref, part, buf0, buf1, buf2, buf3, buf4, res,
                kv_sem, send_sem, recv_sem, out_sem):
    ctx = lax.axis_index("context")
    dp = lax.axis_index("dp")
    z = lax.axis_index("expert")
    tokens, width = xa_ref.shape
    kv_width = dkp_ref.shape[1]
    half = width // 2
    chunks = 8
    bit = lambda v: lax.rem(v, 2)
    flip = lambda v: v + 1 - 2 * bit(v)
    far = lambda v: lax.rem(v + 2, 4)
    partner = {"c": ("context", 1 - ctx), "x": ("dp", flip(dp)), "y": ("dp", far(dp)),
               "n": ("expert", flip(z)), "f": ("expert", far(z))}
    side = {"c": ctx, "x": bit(dp), "y": lax.div(dp, 2), "n": bit(z), "f": lax.div(z, 2)}

    barrier = pltpu.get_barrier_semaphore()
    for axis, other in partner.values():
        pl.semaphore_signal(barrier, inc=1, device_id={axis: other},
                            device_id_type=pl.DeviceIdType.MESH)
    pl.semaphore_wait(barrier, len(partner))

    def exchange(src, dst, ss, rs, way):
        axis, other = partner[way]
        return remote(src, dst, ss, rs, axis, other)

    theirs = pl.ds(pl.multiple_of((1 - ctx) * tokens, 16), tokens)
    ours = pl.ds(pl.multiple_of(ctx * tokens, 16), tokens)
    kv_copies = [
        exchange(ref.at[theirs], dkv_in.at[k], kv_sem.at[0, k], kv_sem.at[1, k], "c")
        for k, ref in enumerate((dkp_ref, dvp_ref))
    ]
    for copy in kv_copies:
        copy.start()

    sizes = [half // 2, half // 4, half // 8, half // 16]
    bufs = [buf1, buf2, buf3, buf4]
    columns = [WIDE] * (chunks - 1) + [128]

    def flows(c):
        w = columns[c] // 2 if columns[c] >= 256 else columns[c]
        ways = [("x", "y", "n", "f"), ("y", "x", "n", "f")]
        return [(k, k * w, w, ways[(k + c) % 2]) for k in range(columns[c] // w)]

    def rows_at(ways, depth):
        first = 0
        for k in range(depth):
            first = first + side[ways[k]] * sizes[k]
        return pl.multiple_of(first, 16)

    def plus(dst, drows, dcols, a, arows, size):
        strip = 48
        def one(k, _):
            d = pl.ds(pl.multiple_of(drows + k * strip, 16), strip)
            s = pl.ds(pl.multiple_of(arows + k * strip, 16), strip)
            dst[d, dcols] = (dst[d, dcols].astype(F32) + a[s, dcols].astype(F32)).astype(BF)
            return 0
        lax.fori_loop(0, size // strip, one, 0)

    def link(c, flow, level):
        k, first, w, ways = flow
        cols = pl.ds(first, w)
        ss, rs = send_sem.at[c, k, level], recv_sem.at[c, k, level]
        if level == 0:
            src = part.at[c % 3, pl.ds(pl.multiple_of((1 - ctx) * half, 16), half), cols]
            return exchange(src, buf0.at[c, :, cols], ss, rs, "c")
        if level <= 4:
            way, size = ways[level - 1], sizes[level - 1]
            before = buf0 if level == 1 else bufs[level - 2]
            src = before.at[c, pl.ds(pl.multiple_of((1 - side[way]) * size, 16), size), cols]
            return exchange(src, bufs[level - 1].at[c, :, cols], ss, rs, way)
        depth = 8 - level + 1
        size = sizes[depth - 1]
        rows = pl.ds(rows_at(ways, depth), size)
        return exchange(res.at[c, rows, cols], res.at[c, rows, cols], ss, rs, ways[depth - 1])

    def produce(c):
        if c < 7:
            left, right, first = ((ob_ref, da_ref, c * WIDE) if c < 3 else
                                  (xa_ref, dq_ref, (c - 3) * WIDE) if c < 6 else
                                  (xa_ref, dkv_ref, 0))
            def one(j, _):
                rows = pl.ds(pl.multiple_of(j * 256, 256), 256)
                part[c % 3, rows, :] = mm_tn(left[:, rows], right[:, first : first + WIDE]).astype(BF)
                return 0
            lax.fori_loop(0, width // 256, one, 0)
        else:
            part[c % 3, :, 0:128] = jnp.zeros((width, 128), BF)
            part[c % 3, :, 0:16] = misc_rows.T.astype(BF)
            part[c % 3, :, 16:24] = gain_rows.T.astype(BF)

    def finish(c):
        for copy in out_copy(c):
            copy.start()

    def out_copy(c):
        copy = lambda first, w, dst, at, k: pltpu.make_async_copy(
            res.at[c, :, pl.ds(first, w)], dst.at[:, pl.ds(at, w)], out_sem.at[c, k])
        if c < 3:
            return [copy(0, WIDE, og_out, c * WIDE, 0)]
        if c < 6:
            return [copy(0, WIDE, qg_out, (c - 3) * WIDE, 0)]
        if c == 6:
            return [copy(0, kv_width, kg_out, 0, 0), copy(kv_width, kv_width, vg_out, 0, 1)]
        return [copy(0, 128, mg_out, 0, 0)]

    def do(c, level):
        if level == 0:
            produce(c)
        for flow in flows(c):
            k, first, w, ways = flow
            cols = pl.ds(first, w)
            if level > 0:
                link(c, flow, level - 1).wait()
            if level == 1:
                plus(buf0.at[c], 0, cols, part.at[c % 3], ctx * half, half)
            elif 1 < level <= 4:
                before = buf0 if level == 2 else bufs[level - 3]
                plus(bufs[level - 2].at[c], 0, cols, before.at[c],
                     side[ways[level - 2]] * sizes[level - 2], sizes[level - 2])
            elif level == 5:
                rows = pl.ds(rows_at(ways, 4), sizes[3])
                keep = pl.ds(pl.multiple_of(side[ways[3]] * sizes[3], 16), sizes[3])
                res[c, rows, cols] = (buf4[c, :, cols].astype(F32)
                                      + buf3[c, keep, cols].astype(F32)).astype(BF)
            if level < LINKS:
                link(c, flow, level).start()
        if level == LINKS:
            finish(c)

    gain_rows = None
    misc_rows = misc_ref[...]
    begin = [0, 0, 0, 1, 1, 1, 3, 3]
    for t in range(max(begin) + LINKS + 1):
        for c in range(chunks):
            if 0 <= t - begin[c] <= LINKS:
                do(c, t - begin[c])
        if t == 1:
            for copy in kv_copies:
                copy.wait()
            for h in range(kv_width // HEAD_SIZE):
                at = slice(h * HEAD_SIZE, (h + 1) * HEAD_SIZE)
                dk = dkp_ref[ours, at].astype(F32) + dkv_in[0, :, at].astype(F32)
                turned = pltpu.roll(dk, HEAD_SIZE // 2, 1)
                dkv_ref[:, at] = (dk * cos_ref[...] - turned * sin_ref[...]).astype(BF)
            dv = dvp_ref[ours, :].astype(F32) + dkv_in[1].astype(F32)
            dkv_ref[:, kv_width : 2 * kv_width] = dv.astype(BF)
        if t == 2:
            step = 64
            def strip(k, total):
                rows = pl.ds(pl.multiple_of(k * step, step), step)
                dxa = mm_nt(dq_ref[rows, :], wq_ref[...])
                dxa = dxa + mm_nt(dkv_ref[rows, 0:kv_width], wk_ref[...])
                dxa = dxa + mm_nt(dkv_ref[rows, kv_width : 2 * kv_width], wv_ref[...])
                v = x_ref[rows, :].astype(F32)
                root = inverse_root(v)
                back = dh_ref[rows, :] + norm_back(v, root, gain_ref[...], dxa)
                gt_ref[rows, :] = back.astype(BF)
                return total + fold_rows(dxa * v * root, jnp.sum)
            total = lax.fori_loop(0, tokens // step, strip, jnp.zeros((8, width), F32))
            gain_rows = jnp.broadcast_to(jnp.sum(total, axis=0, keepdims=True), (8, width))
    for c in range(chunks):
        for copy in out_copy(c):
            copy.wait()


def tail(ob, da, xa, dq, dk_part, dv_part, cos, sin, wq, wk, wv, dh, x, gain, misc):
    tokens, width = xa.shape
    kv_width = dk_part.shape[1]
    half = width // 2
    vmem = pl.BlockSpec(memory_space=pltpu.VMEM)
    anywhere = pl.BlockSpec(memory_space=pl.ANY)
    dma = pltpu.SemaphoreType.DMA
    shape = jax.ShapeDtypeStruct
    chunks = 8
    return pl.pallas_call(
        tail_kernel,
        out_shape=(
            shape((half, width), BF), shape((half, kv_width), BF), shape((half, kv_width), BF),
            shape((half, width), BF), shape((half, 128), BF), shape((tokens, width), BF),
        ),
        in_specs=[vmem] * 15,
        out_specs=[anywhere] * 5 + [vmem],
        scratch_shapes=[
            pltpu.VMEM((2, tokens, kv_width), BF), pltpu.VMEM((tokens, 2 * kv_width), BF),
            pltpu.VMEM((3, width, WIDE), BF),
            pltpu.VMEM((chunks, half, WIDE), BF), pltpu.VMEM((chunks, half // 2, WIDE), BF),
            pltpu.VMEM((chunks, half // 4, WIDE), BF), pltpu.VMEM((chunks, half // 8, WIDE), BF),
            pltpu.VMEM((chunks, half // 16, WIDE), BF), pltpu.VMEM((chunks, half, WIDE), BF),
            dma((2, 2)), dma((chunks, 2, LINKS)), dma((chunks, 2, LINKS)), dma((chunks, 2)),
        ],
        compiler_params=pltpu.CompilerParams(
            vmem_limit_bytes=MOE_VMEM, collective_id=2, has_side_effects=True
        ),
        cost_estimate=pl.CostEstimate(
            flops=2 * tokens * width * (2 * width + 4 * kv_width + width),
            transcendentals=0, bytes_accessed=16 * width * width,
        ),
        name="tail",
    )(ob, da, xa, dq, dk_part, dv_part, cos, sin, wq, wk, wv, dh, x, gain, misc)


def finish_kernel(flags, qg_ref, kg_ref, vg_ref, og_ref, misc_ref, y0_ref, y1_ref, y2_ref, y3_ref,
                  hidden_ref, shard_ref,
                  q_out, k_out, v_out, o_out, router_out, gains_out, layer_out,
                  gate_out, up_out, down_out):
    for src, dst in ((qg_ref, q_out), (kg_ref, k_out), (vg_ref, v_out), (og_ref, o_out)):
        dst[...] = src[...].astype(F32)
    out = hidden_ref[...]
    for ref in (y0_ref, y2_ref, y3_ref):
        out = out + ref[...].astype(F32)
    out = out + y1_ref[0].astype(F32)
    out = out + jnp.where(flags[1] > 0, y1_ref[1].astype(F32), 0.0)
    layer_out[...] = out.astype(BF)
    hidden = gate_out.shape[2]
    for k, dst in enumerate((gate_out, up_out, down_out)):
        dst[...] = shard_ref[:, :, k * hidden : (k + 1) * hidden].astype(F32)

    @pl.when(pl.program_id(0) == 0)
    def _():
        misc = misc_ref[...].astype(F32)
        router_out[...] = misc[:, 0 : router_out.shape[1]]
        rows = misc.T
        gains_out[0:1, :] = rows[16:17, :]
        gains_out[1:2, :] = jnp.sum(rows[8:16, :], axis=0, keepdims=True)


def finish(flags, qg, kg, vg, og, misc, y_own, y_in, y_far, hidden, shard, experts):
    half, width = qg.shape
    kv_width = kg.shape[1]
    tokens = hidden.shape[0]
    local, rows, three = shard.shape
    ff = three // 3
    grid = 4
    shape = jax.ShapeDtypeStruct
    cut = lambda r, d: pl.BlockSpec((r // grid, d), lambda i, f: (i, 0))
    const = lambda r, d: pl.BlockSpec((r, d), lambda i, f: (0, 0))
    grads = lambda d: pl.BlockSpec((local, rows // grid, d), lambda i, f: (0, i, 0))
    return pl.pallas_call(
        finish_kernel,
        out_shape=(
            shape((half, width), F32), shape((half, kv_width), F32), shape((half, kv_width), F32),
            shape((half, width), F32), shape((half, experts), F32), shape((2, half), F32),
            shape((tokens, width), BF), shape((local, rows, ff), F32),
            shape((local, rows, ff), F32), shape((local, rows, ff), F32),
        ),
        grid_spec=pltpu.PrefetchScalarGridSpec(
            num_scalar_prefetch=1,
            grid=(grid,),
            in_specs=[
                cut(half, width), cut(half, kv_width), cut(half, kv_width), cut(half, width),
                const(half, 128), cut(tokens, width),
                pl.BlockSpec((2, tokens // grid, width), lambda i, f: (0, i, 0)),
                cut(tokens, width), cut(tokens, width), cut(tokens, width), grads(three),
            ],
            out_specs=[
                cut(half, width), cut(half, kv_width), cut(half, kv_width), cut(half, width),
                const(half, experts), const(2, half), cut(tokens, width), grads(ff), grads(ff),
                grads(ff),
            ],
        ),
        compiler_params=pltpu.CompilerParams(vmem_limit_bytes=VMEM_LIMIT),
        cost_estimate=pl.CostEstimate(flops=0, transcendentals=0, bytes_accessed=16 * half * width),
        name="finish",
    )(flags, qg, kg, vg, og, misc, y_own, y_in, *y_far, hidden, shard)


def body(
    tokens, cotangent, segment_ids, routes, fill_rank, query_weight, key_projection_weight,
    value_projection_weight, output_weight, router_weight, gain_attention, gain_experts,
    gate_weight, up_weight, down_weight,
):
    context_index = lax.axis_index("context")
    context_size = lax.axis_size("context")
    expert_size = lax.axis_size("expert")
    rows = tokens.shape[1]
    length = segment_ids.shape[1]
    kv_width = KEY_VALUE_HEADS * HEAD_SIZE
    gather = lambda w, axis=0: lax.all_gather(w, "context", axis=axis, tiled=True)
    x, upstream = tokens[0], cotangent[0]

    cot_left = lax.ppermute(upstream, "expert", RIGHT)
    cot_right = lax.ppermute(upstream, "expert", LEFT)

    expert_count = router_weight.shape[1]
    local = gate_weight.shape[0]
    capacity = 5 * rows * TOP // (4 * expert_count)
    cap = -(-capacity // 64) * 64
    names = jnp.arange(expert_count, dtype=jnp.int32)
    route_hit = routes[0][:, :, None] == names[None, None, :]
    routed = jnp.any(route_hit, axis=1)
    ranks = fill_rank[0, 0].reshape(rows, TOP)
    order = jnp.sum(jnp.where(route_hit, ranks[:, :, None], 0), axis=1)
    order = jnp.where(routed, order, rows * TOP).T
    slots = jnp.sum((order[:, :, None] < order[:, None, :]).astype(jnp.int32), axis=1)
    kept = routed.T & (slots < capacity)
    slots = jnp.where(kept, slots, -1).astype(F32)
    kept_float = kept.T.astype(F32)

    small = jnp.concatenate([
        gain_attention[None], gain_experts[None], jnp.zeros((6, gain_attention.shape[0]), BF),
        router_weight.T,
    ]).astype(F32)
    positions = context_index * rows + jnp.arange(rows, dtype=jnp.int32)
    cosine, sine = rope_tables(positions)
    cos_full = jnp.concatenate([cosine, cosine], axis=-1)
    sin_full = jnp.concatenate([-sine, sine], axis=-1)
    turned = lambda v, heads, d: apply_rotary(
        v.reshape(rows, heads, HEAD_SIZE), cosine, sine, d
    ).reshape(rows, heads * HEAD_SIZE)
    output_full = gather(output_weight)
    if context_size == 2:
        q, attn_input, kv, query_full, key_full, value_full, small = project(
            x, query_weight, key_projection_weight, value_projection_weight, small,
            cos_full, sin_full,
        )
    else:
        query_full, key_full, value_full = (
            gather(query_weight), gather(key_projection_weight), gather(value_projection_weight)
        )
        small = gather(small.astype(BF), 1).astype(F32)
        residual = x.astype(F32)
        attn_input = (residual * inverse_root(residual) * small[0]).astype(BF)
        q = turned(mm(attn_input, query_full), QUERY_HEADS, 1.0).astype(BF)
        k_own = turned(mm(attn_input, key_full), KEY_VALUE_HEADS, 1.0).astype(BF)
        kv = gather(jnp.concatenate([k_own, mm(attn_input, value_full).astype(BF)], axis=1))
    segments = segment_ids[0]
    tq, kb = attention_sizes(rows, length)
    spans = attention_meta(context_index, rows, segments, tq, kb)
    segk = segments[:, None]
    segq = lax.dynamic_slice_in_dim(segments, context_index * rows, rows)[None, :]
    cot_left, cot_right, q, kv, spans, segk, segq, slots, kept_float, routed_float = (
        lax.optimization_barrier((cot_left, cot_right, q, kv, spans, segk, segq, slots, kept_float,
                                  routed.astype(F32))))
    second_left = lax.ppermute(cot_left, "expert", RIGHT_ON)
    second_right = lax.ppermute(cot_right, "expert", LEFT_ON)
    mixed, lse = attention_forward(q, kv, spans, segk, segq)

    hidden, expert_input, gates = mix(mixed, x, output_full, small, routed_float)
    second_left, second_right, gates = lax.optimization_barrier((second_left, second_right, gates))
    cot_second = second_left + second_right
    routing = jnp.stack([slots, (gates * kept_float).T], axis=0)
    routing = routing.reshape(2, expert_size, local, rows).transpose(1, 0, 2, 3)
    routing = routing.reshape(expert_size, 2 * local, rows)
    routing = jnp.pad(routing, ((0, 0), (0, 8 - 2 * local), (0, 0)))
    dn_parts, dw_parts, y_own, _, y_second, y_third, y_in, grads_low, _, _ = moe(
        expert_input, upstream, cot_left, cot_right, cot_second, routing, gate_weight, up_weight,
        down_weight, cap,
    )
    gate_dot = dw_parts[:, :local].reshape(expert_count, rows).T * kept_float
    y_far = (lax.ppermute(y_third, "expert", FAR), lax.ppermute(y_second, "expert", ACROSS))
    grads_shard = lax.psum_scatter(
        grads_low, ("dp", "context"), scatter_dimension=1, tiled=True
    )

    expert_index = lax.axis_index("expert")
    between = (expert_index > 0) & (expert_index < expert_size - 1)
    flags = jnp.where(between, jnp.array([1, 1, 1], jnp.int32), jnp.array([1, 0, 1], jnp.int32))
    hidden_total, attn_grad_low, mixed_grad_low, misc = turn(
        flags, dn_parts, gate_dot, gates, hidden, upstream, output_full, small
    )
    dq_low, dk_part, dv_part = attention_backward(
        q, kv, mixed_grad_low, lse, cos_full, sin_full, spans, segk, segq
    )
    if (lax.axis_size("dp"), context_size, expert_size) == (4, 2, 4):
        *sums, grad_tokens = tail(
            mixed, attn_grad_low, attn_input, dq_low, dk_part, dv_part, cos_full, sin_full,
            query_full, key_full, value_full, hidden_total, x, small[0:1], misc,
        )
        late, grad_tokens = lax.optimization_barrier((hidden, grad_tokens))
        (query_grad, key_grad, value_grad, output_grad, router_grad, gains, layer_out,
         *expert_sums) = finish(flags, *sums, y_own, y_in, y_far, late, grads_shard, expert_count)
        sums = (query_grad, key_grad, value_grad, output_grad, router_grad, gains[0], gains[1])
    else:
        dkv = lax.psum_scatter(
            jnp.concatenate([dk_part, dv_part], axis=1), "context", scatter_dimension=0, tiled=True
        )
        dk_low = turned(dkv[:, :kv_width].astype(F32), KEY_VALUE_HEADS, -1.0).astype(BF)
        dv_low = dkv[:, kv_width:]
        input_total = (
            mm_nt(dq_low, query_full) + mm_nt(dk_low, key_full) + mm_nt(dv_low, value_full)
        )
        residual = x.astype(F32)
        root = inverse_root(residual)
        grad_tokens = (hidden_total + norm_back(residual, root, small[0], input_total)).astype(BF)
        reduce_rows = lambda v: lax.psum(
            lax.psum_scatter(v.astype(BF), "context", scatter_dimension=0, tiled=True),
            ("dp", "expert"),
        ).astype(F32)
        sums = tuple(reduce_rows(v) for v in (
            mm_tn(attn_input, dq_low), mm_tn(attn_input, dk_low), mm_tn(attn_input, dv_low),
            mm_tn(mixed, attn_grad_low), misc[:8].T,
            jnp.sum(input_total * residual * root, axis=0), jnp.sum(misc[8:16], axis=0),
        ))
        mixture = sum(v.astype(F32) for v in (y_own, y_in[0], *y_far))
        mixture = mixture + jnp.where(between, y_in[1].astype(F32), 0.0)
        layer_out = (hidden + mixture).astype(BF)
        ff = gate_weight.shape[2]
        wide = grads_shard.astype(F32)
        expert_sums = [wide[:, :, i * ff : (i + 1) * ff] for i in range(3)]
    return (layer_out[None], grad_tokens[None], *sums, *expert_sums)


def solution(mesh):
    both = ("dp", "expert")
    token_spec = P(both, "context", None)
    row_spec = P("context", None)
    expert_out = P("expert", ("dp", "context"), None)
    return jax.shard_map(
        body,
        mesh=mesh,
        in_specs=(
            token_spec, token_spec, P(both, None), token_spec, token_spec,
            row_spec, row_spec, row_spec, row_spec, row_spec, P("context"), P("context"),
            P("expert", None, None), P("expert", None, None), P("expert", None, None),
        ),
        out_specs=(
            token_spec, token_spec, row_spec, row_spec, row_spec, row_spec, row_spec,
            P("context"), P("context"), expert_out, expert_out, expert_out,
        ),
        check_vma=False,
    )
```

```python
import functools
import math

import jax
import jax.numpy as jnp
from jax import lax
from jax.experimental import pallas as pl
from jax.experimental.pallas import tpu as pltpu
from jax.sharding import PartitionSpec as P

MODEL_WIDTH = 1536
QUERY_HEADS = 12
KEY_VALUE_HEADS = 2
HEAD_SIZE = 128
TOP = 4
GROUP = QUERY_HEADS // KEY_VALUE_HEADS
norm_eps = 1e-06
rope_base = 10000.0
NEG = -1e30
HEADS_AT_ONCE = 3
SCALE = 1.0 / math.sqrt(HEAD_SIZE)
BF = jnp.bfloat16
F32 = jnp.float32
VMEM_LIMIT = 60 * 1024 * 1024
MOE_VMEM = 63 * 1024 * 1024


def mm(a, b):
    return jnp.dot(a, b, preferred_element_type=F32)


def mm_nt(a, b):
    return lax.dot_general(a, b, (((1,), (1,)), ((), ())), preferred_element_type=F32)


def mm_tn(a, b):
    return lax.dot_general(a, b, (((0,), (0,)), ((), ())), preferred_element_type=F32)


def inverse_root(v):
    return lax.rsqrt(jnp.mean(v * v, axis=-1, keepdims=True) + norm_eps)


def norm_back(v, root, gain, upstream):
    scaled = upstream * gain
    cubed = root * root * root
    return root * scaled - v * cubed * jnp.mean(v * scaled, axis=-1, keepdims=True)


def rope_tables(positions):
    half = HEAD_SIZE // 2
    frequency = jnp.exp(
        -(jnp.arange(half, dtype=F32) * (2.0 / HEAD_SIZE)) * math.log(rope_base)
    )
    angle = positions.astype(F32)[:, None] * frequency[None, :]
    return jnp.cos(angle), jnp.sin(angle)


def apply_rotary(v, cosine, sine, direction):
    half = HEAD_SIZE // 2
    a, b = v[..., :half], v[..., half:]
    c, s = cosine[:, None, :], sine[:, None, :]
    return jnp.concatenate([a * c - direction * b * s, b * c + direction * a * s], axis=-1)


def fold_rows(v, op):
    rows, cols = v.shape
    return op(v.reshape(rows // 8, 8, cols), axis=0)


def make_bias(ctx, tokens, segk_ref, segq_ref, bias_ref):
    length = segk_ref.shape[0]
    key_pos = lax.broadcasted_iota(jnp.int32, (length, tokens), 0)
    query_pos = lax.broadcasted_iota(jnp.int32, (length, tokens), 1) + ctx * tokens
    same = segk_ref[...] == segq_ref[...]
    bias_ref[...] = jnp.where(same & (key_pos <= query_pos), 0.0, NEG)


def attn_fwd_kernel(kb, tq, meta, q_ref, k_ref, v_ref, segk_ref, segq_ref, o_ref, lse_ref,
                    bias_ref, s_ref, vt_ref):
    step = pl.program_id(0)
    tokens = q_ref.shape[0]

    @pl.when(step == 0)
    def _():
        make_bias(meta[0], tokens, segk_ref, segq_ref, bias_ref)

    @pl.when(lax.rem(step * HEADS_AT_ONCE, GROUP) == 0)
    def _():
        vt_ref[...] = v_ref[...].astype(F32).T.astype(BF)

    heads = [slice(h * HEAD_SIZE, (h + 1) * HEAD_SIZE) for h in range(HEADS_AT_ONCE)]
    for part in range(tokens // tq):
        cols = pl.ds(part * tq, tq)
        low, high = meta[1 + 2 * part], meta[2 + 2 * part]

        def score(i, tops):
            rows = pl.ds(pl.multiple_of(i * kb, kb), kb)
            key, bias = k_ref[rows, :], bias_ref[rows, cols]
            out = []
            for h, at in enumerate(heads):
                s = mm_nt(key, q_ref[cols, at]) * SCALE + bias
                s_ref[h, rows, :] = s
                out.append(jnp.maximum(tops[h], fold_rows(s, jnp.max)))
            return tuple(out)

        tops = lax.fori_loop(low, high, score,
                             tuple(jnp.full((8, tq), NEG, F32) for _ in heads))
        tops = [jnp.max(t, axis=0, keepdims=True) for t in tops]

        def value(i, carry):
            totals, outs = carry
            rows = pl.ds(pl.multiple_of(i * kb, kb), kb)
            vt = vt_ref[:, rows]
            new_totals, new_outs = [], []
            for h in range(HEADS_AT_ONCE):
                p = jnp.exp(s_ref[h, rows, :] - tops[h])
                new_totals.append(totals[h] + fold_rows(p, jnp.sum))
                new_outs.append(outs[h] + mm(vt, p.astype(BF)))
            return tuple(new_totals), tuple(new_outs)

        totals, outs = lax.fori_loop(
            low, high, value, (tuple(jnp.zeros((8, tq), F32) for _ in heads),
                               tuple(jnp.zeros((HEAD_SIZE, tq), F32) for _ in heads)))
        for h, at in enumerate(heads):
            total = jnp.sum(totals[h], axis=0, keepdims=True)
            o_ref[cols, at] = (outs[h] / total).T.astype(BF)
            lse_ref[h, :, cols] = tops[h] + jnp.log(total)


def attn_bwd_kernel(kb, tq, meta, q_ref, k_ref, v_ref, do_ref, lse_ref, cos_ref, sin_ref,
                    segk_ref, segq_ref, dq_ref, dk_ref, dv_ref,
                    bias_ref, p_ref, dp_ref, kt_ref, dk_acc, dv_acc):
    step = pl.program_id(0)
    tokens = q_ref.shape[0]

    @pl.when(step == 0)
    def _():
        make_bias(meta[0], tokens, segk_ref, segq_ref, bias_ref)

    place = lax.rem(step * HEADS_AT_ONCE, GROUP)

    @pl.when(place == 0)
    def _():
        kt_ref[...] = k_ref[...].astype(F32).T.astype(BF)
        dk_acc[...] = jnp.zeros_like(dk_acc)
        dv_acc[...] = jnp.zeros_like(dv_acc)

    heads = [slice(h * HEAD_SIZE, (h + 1) * HEAD_SIZE) for h in range(HEADS_AT_ONCE)]
    for part in range(tokens // tq):
        cols = pl.ds(part * tq, tq)
        low, high = meta[1 + 2 * part], meta[2 + 2 * part]

        def score(i, deltas):
            rows = pl.ds(pl.multiple_of(i * kb, kb), kb)
            key, value, bias = k_ref[rows, :], v_ref[rows, :], bias_ref[rows, cols]
            out = []
            for h, at in enumerate(heads):
                s = mm_nt(key, q_ref[cols, at]) * SCALE + bias
                p = jnp.exp(s - lse_ref[h, :, cols])
                dp = mm_nt(value, do_ref[cols, at])
                p_ref[h, rows, :] = p
                dp_ref[h, rows, :] = dp
                out.append(deltas[h] + fold_rows(p * dp, jnp.sum))
            return tuple(out)

        deltas = lax.fori_loop(low, high, score, tuple(jnp.zeros((8, tq), F32) for _ in heads))
        deltas = [jnp.sum(d, axis=0, keepdims=True) for d in deltas]

        def grads(i, dqs):
            rows = pl.ds(pl.multiple_of(i * kb, kb), kb)
            kt = kt_ref[:, rows]
            out, dk, dv = [], dk_acc[rows, :], dv_acc[rows, :]
            for h, at in enumerate(heads):
                p = p_ref[h, rows, :]
                ds = (p * (dp_ref[h, rows, :] - deltas[h])).astype(BF)
                dv = dv + mm(p.astype(BF), do_ref[cols, at])
                dk = dk + mm(ds, q_ref[cols, at])
                out.append(dqs[h] + mm(kt, ds))
            dk_acc[rows, :] = dk
            dv_acc[rows, :] = dv
            return tuple(out)

        dqs = lax.fori_loop(low, high, grads,
                            tuple(jnp.zeros((HEAD_SIZE, tq), F32) for _ in heads))
        for h, at in enumerate(heads):
            dq = dqs[h].T * SCALE
            turned = pltpu.roll(dq, HEAD_SIZE // 2, 1)
            dq_ref[cols, at] = (dq * cos_ref[cols, :] - turned * sin_ref[cols, :]).astype(BF)

    @pl.when(place == GROUP - HEADS_AT_ONCE)
    def _():
        dk_ref[...] = (dk_acc[...] * SCALE).astype(BF)
        dv_ref[...] = dv_acc[...].astype(BF)


def attention_sizes(tokens, length):
    tq = 256 if tokens % 256 == 0 else tokens
    kb = 256 if length % 256 == 0 else 128
    return tq, kb


def attention_meta(ctx, tokens, segments, tq, kb):
    entries = [ctx]
    for part in range(tokens // tq):
        first = ctx * tokens + part * tq
        own = lax.dynamic_slice_in_dim(segments, first, 1)
        start = jnp.sum((segments < own).astype(jnp.int32))
        entries += [start // kb, (first + tq + kb - 1) // kb]
    return jnp.stack(entries).astype(jnp.int32)


def attention_forward(q, kv, meta, segk, segq):
    tokens, length = q.shape[0], kv.shape[0]
    tq, kb = attention_sizes(tokens, length)
    const = lambda h, m: (0, 0)
    return pl.pallas_call(
        functools.partial(attn_fwd_kernel, kb, tq),
        out_shape=(
            jax.ShapeDtypeStruct(q.shape, BF),
            jax.ShapeDtypeStruct((QUERY_HEADS, 1, tokens), F32),
        ),
        grid_spec=pltpu.PrefetchScalarGridSpec(
            num_scalar_prefetch=1,
            grid=(QUERY_HEADS // HEADS_AT_ONCE,),
            in_specs=[
                pl.BlockSpec((tokens, HEADS_AT_ONCE * HEAD_SIZE), lambda h, m: (0, h)),
                pl.BlockSpec((length, HEAD_SIZE), lambda h, m: (0, h * HEADS_AT_ONCE // GROUP)),
                pl.BlockSpec((length, HEAD_SIZE), lambda h, m: (0, KEY_VALUE_HEADS + h * HEADS_AT_ONCE // GROUP)),
                pl.BlockSpec((length, 1), const),
                pl.BlockSpec((1, tokens), const),
            ],
            out_specs=[
                pl.BlockSpec((tokens, HEADS_AT_ONCE * HEAD_SIZE), lambda h, m: (0, h)),
                pl.BlockSpec((HEADS_AT_ONCE, 1, tokens), lambda h, m: (h, 0, 0)),
            ],
            scratch_shapes=[
                pltpu.VMEM((length, tokens), F32),
                pltpu.VMEM((HEADS_AT_ONCE, length, tq), F32),
                pltpu.VMEM((HEAD_SIZE, length), BF),
            ],
        ),
        compiler_params=pltpu.CompilerParams(vmem_limit_bytes=VMEM_LIMIT),
        cost_estimate=pl.CostEstimate(
            flops=3 * QUERY_HEADS * tokens * length * HEAD_SIZE,
            transcendentals=QUERY_HEADS * tokens * length,
            bytes_accessed=4 * tokens * MODEL_WIDTH,
        ),
        name="attn_fwd",
    )(meta, q, kv, kv, segk, segq)


def attention_backward(q, kv, do, lse, cos, sin, meta, segk, segq):
    tokens, length = q.shape[0], kv.shape[0]
    tq, kb = attention_sizes(tokens, length)
    const = lambda h, m: (0, 0)
    by_head = lambda h, m: (0, h)
    by_group = lambda h, m: (0, h * HEADS_AT_ONCE // GROUP)
    return pl.pallas_call(
        functools.partial(attn_bwd_kernel, kb, tq),
        out_shape=(
            jax.ShapeDtypeStruct(q.shape, BF),
            jax.ShapeDtypeStruct((length, KEY_VALUE_HEADS * HEAD_SIZE), BF),
            jax.ShapeDtypeStruct((length, KEY_VALUE_HEADS * HEAD_SIZE), BF),
        ),
        grid_spec=pltpu.PrefetchScalarGridSpec(
            num_scalar_prefetch=1,
            grid=(QUERY_HEADS // HEADS_AT_ONCE,),
            in_specs=[
                pl.BlockSpec((tokens, HEADS_AT_ONCE * HEAD_SIZE), by_head),
                pl.BlockSpec((length, HEAD_SIZE), by_group),
                pl.BlockSpec((length, HEAD_SIZE), lambda h, m: (0, KEY_VALUE_HEADS + h * HEADS_AT_ONCE // GROUP)),
                pl.BlockSpec((tokens, HEADS_AT_ONCE * HEAD_SIZE), by_head),
                pl.BlockSpec((HEADS_AT_ONCE, 1, tokens), lambda h, m: (h, 0, 0)),
                pl.BlockSpec((tokens, HEAD_SIZE), const),
                pl.BlockSpec((tokens, HEAD_SIZE), const),
                pl.BlockSpec((length, 1), const),
                pl.BlockSpec((1, tokens), const),
            ],
            out_specs=[
                pl.BlockSpec((tokens, HEADS_AT_ONCE * HEAD_SIZE), by_head),
                pl.BlockSpec((length, HEAD_SIZE), by_group),
                pl.BlockSpec((length, HEAD_SIZE), by_group),
            ],
            scratch_shapes=[
                pltpu.VMEM((length, tokens), F32),
                pltpu.VMEM((HEADS_AT_ONCE, length, tq), F32),
                pltpu.VMEM((HEADS_AT_ONCE, length, tq), F32),
                pltpu.VMEM((HEAD_SIZE, length), BF),
                pltpu.VMEM((length, HEAD_SIZE), F32),
                pltpu.VMEM((length, HEAD_SIZE), F32),
            ],
        ),
        compiler_params=pltpu.CompilerParams(vmem_limit_bytes=VMEM_LIMIT),
        cost_estimate=pl.CostEstimate(
            flops=8 * QUERY_HEADS * tokens * length * HEAD_SIZE,
            transcendentals=QUERY_HEADS * tokens * length,
            bytes_accessed=8 * tokens * MODEL_WIDTH,
        ),
        name="attn_bwd",
    )(meta, q, kv, kv, do, lse, cos, sin, segk, segq)


def remote(src, dst, ss, rs, axis, dev):
    return pltpu.make_async_remote_copy(
        src_ref=src, dst_ref=dst, send_sem=ss, recv_sem=rs, device_id={axis: dev},
        device_id_type=pl.DeviceIdType.MESH,
    )


def moe_kernel(cap, tile, n,
               x_hbm, cot_hbm, cotl_hbm, cotr_hbm, cotl2_hbm, cotr2_hbm, meta_hbm, gate_hbm, up_hbm, down_hbm,
               dn_out, dw_out, y_own, y_near, y_second, y_third, y_in, grads_out, xall, cotfar,
               gate_ref, up_ref, down_ref, x_ref, cot_ref, metas, xs_ref, dy_ref, hb_ref, dg_ref,
               du_ref, pdn_ref, transit, py_ref, dws, pick_ref, put_ref, ys_ref, acc_ref, stage,
               wsem, lsem, xs_send, xs_recv, far_sem, m_send, m_recv, dn_send, dn_recv,
               dw_send, dw_recv, py_sem, own_sem, st_sem, y_send, y_recv):
    me = lax.axis_index("expert")
    tokens, width = x_ref.shape
    local, _, hidden = gate_ref.shape
    edge = (me == 0) | (me == n - 1)

    barrier = pltpu.get_barrier_semaphore()
    for d in range(1, n):
        pl.semaphore_signal(barrier, inc=1, device_id={"expert": lax.rem(me + d, n)},
                            device_id_type=pl.DeviceIdType.MESH)
    pl.semaphore_wait(barrier, n - 1)

    def exists(direction, step):
        return (me - 1 - step >= 0) if direction == 0 else (me + 1 + step <= n - 1)

    def sends(direction, step):
        if direction == 0:
            return (me - step >= 0) & (me < n - 1)
        return (me + step <= n - 1) & (me > 0)

    def xcopy(direction, step):
        block = jnp.clip(me - step if direction == 0 else me + step, 0, n - 1)
        target = jnp.clip(me + 1 if direction == 0 else me - 1, 0, n - 1)
        src = x_hbm if step == 0 else xall.at[block]
        return remote(src, xall.at[block], xs_send.at[direction, step],
                      xs_recv.at[direction, step], "expert", target)

    outward = jnp.where(me < 2, 0, n - 1)
    inward = n - 1 - jnp.clip(me, 1, n - 2)
    inner = jnp.where(me < 2, 1, n - 2)
    far_copy = lambda ref=cotl2_hbm: remote(ref, cotfar, far_sem.at[0], far_sem.at[1], "expert",
                                            outward)
    middle_device = jnp.logical_not(edge)

    for d in range(2):
        @pl.when(sends(d, 0))
        def _():
            xcopy(d, 0).start()

    def meta_copy(j):
        return remote(meta_hbm.at[j], metas.at[me], m_send.at[j], m_recv.at[me], "expert", j)

    for j in range(n):
        @pl.when(me != j)
        def _():
            meta_copy(j).start()

    loads = [pltpu.make_async_copy(a, b, wsem.at[k]) for k, (a, b) in enumerate(
        ((gate_hbm, gate_ref), (up_hbm, up_ref), (down_hbm, down_ref)))]
    for load in loads:
        load.start()
    own_meta = pltpu.make_async_copy(meta_hbm.at[me], metas.at[me], lsem.at[2])
    own_meta.start()

    def fetch(a, b):
        cx = pltpu.make_async_copy(a, x_ref, lsem.at[0])
        cc = pltpu.make_async_copy(b, cot_ref, lsem.at[1])
        cx.start()
        cc.start()
        cx.wait()
        cc.wait()

    pieces = width // tile
    piece = lambda part: pl.ds(pl.multiple_of(part * tile, tile), tile)

    def edge_copy(kind, part):
        dst = (dn_out.at[1, :, piece(part)] if kind == 0 else
               transit.at[kind - 1, :, piece(part)])
        return remote(pdn_ref.at[kind, :, piece(part)], dst, dn_send.at[kind, part],
                      dn_recv.at[kind, part], "expert", inner)

    def y_copy(kind):
        target = jnp.where(edge, inner, outward) if kind == 0 else inward
        return remote(y_near.at[kind], y_in.at[kind], y_send.at[kind], y_recv.at[kind], "expert",
                      target)

    def pass_copy(kind, part):
        dst = transit.at[2, :, piece(part)] if kind == 1 else dn_out.at[2, :, piece(part)]
        arrival = dn_recv.at[3, part] if kind != 1 else dn_recv.at[4, part]
        return remote(transit.at[kind, :, piece(part)], dst, dn_send.at[kind, part], arrival,
                      "expert", outward if kind == 2 else inward)

    mirror = me >= 2
    side = jnp.where(mirror, n - 1 - me, me)

    def source_of(p):
        base = jnp.where(p == 0, side, jnp.where(p == 1, 1 - side, p))
        return jnp.where(mirror, n - 1 - base, base)

    def arrive(direction, step):
        @pl.when(exists(direction, step))
        def _():
            xcopy(direction, step).wait_recv()

    def forward(direction, step):
        @pl.when(sends(direction, step))
        def _():
            xcopy(direction, step).start()

    def one_source(p, _):
        src = source_of(p)

        @pl.when(p == 0)
        def _():
            own_meta.wait()

        @pl.when(p > 0)
        def _():
            remote(meta_hbm.at[src], metas.at[src], m_send.at[src], m_recv.at[src], "expert",
                   src).wait_recv()

        meta = metas[src]
        columns = meta.T
        spread = lax.broadcasted_iota(jnp.int32, (tokens, local * cap), 1).astype(F32)
        slot = lax.broadcasted_iota(jnp.int32, (cap, tokens), 0).astype(F32)
        weights, put = [], None
        for e in range(local):
            hit = slot == meta[e : e + 1, :]
            pick_ref[pl.ds(e * cap, cap), :] = jnp.where(hit, 1.0, 0.0).astype(BF)
            weights.append(
                jnp.sum(jnp.where(hit, meta[local + e : local + e + 1, :], 0.0), axis=1,
                        keepdims=True)
            )
            own = columns[:, e : e + 1]
            here = spread == jnp.where(own < 0.0, -1.0, own + e * cap)
            put = here if put is None else put | here
        put_ref[...] = jnp.where(put, 1.0, 0.0).astype(BF)
        @pl.when(p == 0)
        def _():
            fetch(x_hbm, cot_hbm)
            for load in loads:
                load.wait()

        @pl.when(p == 1)
        def _():
            for d in range(2):
                arrive(d, 0)
                forward(d, 1)

            for ref, when in ((cotl2_hbm, me >= 2), (cotr2_hbm, me < 2)):
                @pl.when(middle_device & when)
                def _():
                    far_copy(ref).start()

        @pl.when(p > 0)
        def _():
            pltpu.make_async_copy(py_ref, y_own, py_sem.at[0]).wait()

        @pl.when(middle_device & (p == 3))
        def _():
            y_copy(1).start()

        @pl.when(edge & (p == 2))
        def _():
            for part in range(pieces):
                edge_copy(0, part).wait_send()
            y_copy(0).start()

        @pl.when(((p == 2) & edge) | ((p == 3) & jnp.logical_not(edge)))
        def _():
            for d in range(2):
                arrive(d, 1)
                forward(d, 2)

        @pl.when((p == 3) & edge)
        def _():
            for d in range(2):
                arrive(d, 2)
            far_copy().wait_recv()

        @pl.when((p > 0) & (src == me - 1))
        def _():
            fetch(xall.at[src], cotl_hbm)

        @pl.when((p > 0) & (src == me + 1))
        def _():
            fetch(xall.at[src], cotr_hbm)

        @pl.when(src == me - 2)
        def _():
            fetch(xall.at[src], cotl2_hbm)

        @pl.when(src == me + 2)
        def _():
            fetch(xall.at[src], cotr2_hbm)

        @pl.when((src == me - 3) | (src == me + 3))
        def _():
            fetch(xall.at[src], cotfar)

        mine = pl.ds(pl.multiple_of(p * cap, cap), cap)
        buf = lax.rem(p + 2, 3)

        def gather(j, _):
            cols = pl.ds(pl.multiple_of(j * tile, tile), tile)
            xs = mm(pick_ref[...], x_ref[:, cols]).astype(BF)
            cg = mm(pick_ref[...], cot_ref[:, cols])
            for e in range(local):
                rows = slice(e * cap, (e + 1) * cap)
                xs_ref[e, mine, cols] = xs[rows]
                dy_ref[e, mine, cols] = (weights[e] * cg[rows]).astype(BF)
            return 0

        lax.fori_loop(0, width // tile, gather, 0)

        def middle(j, _):
            cols = pl.ds(pl.multiple_of(j * tile, tile), tile)
            for e in range(local):
                g = mm(xs_ref[e, mine, :], gate_ref[e, :, cols])
                u = mm(xs_ref[e, mine, :], up_ref[e, :, cols])
                dh = mm(dy_ref[e, mine, :], down_ref[e, :, cols])
                s = 1.0 / (1.0 + jnp.exp(-g))
                act = g * s
                hb_ref[e, mine, cols] = (act * u).astype(BF)
                dg_ref[e, mine, cols] = (dh * u * (s * (1.0 + g * (1.0 - s)))).astype(BF)
                du_ref[e, mine, cols] = (dh * act).astype(BF)
            return 0

        lax.fori_loop(0, hidden // tile, middle, 0)


        @pl.when(p == 3)
        def _():
            pltpu.make_async_copy(pdn_ref.at[2], dn_out.at[0], own_sem.at[0]).wait()

        acc_ref[...] = jnp.zeros_like(acc_ref)

        def back(j, _):
            cols = pl.ds(pl.multiple_of(j * tile, tile), tile)
            for e in range(local):
                dxs = mm_nt(dg_ref[e, mine, :], gate_ref[e, cols, :])
                dxs = dxs + mm_nt(du_ref[e, mine, :], up_ref[e, cols, :])
                ys_ref[pl.ds(e * cap, cap), :] = dxs.astype(BF)
            pdn_ref[buf, :, cols] = mm(put_ref[...], ys_ref[...]).astype(BF)
            for kind in range(3):
                @pl.when(edge & (p == kind + 1))
                def _():
                    edge_copy(kind, j).start()
            return 0

        lax.fori_loop(0, width // tile, back, 0)

        @pl.when(p == 0)
        def _():
            pltpu.make_async_copy(pdn_ref.at[2], dn_out.at[0], own_sem.at[0]).start()

        def ahead(j, _):
            cols = pl.ds(pl.multiple_of(j * tile, tile), tile)
            for e in range(local):
                rows = pl.ds(e * cap, cap)
                y = mm_nt(hb_ref[e, mine, :], down_ref[e, cols, :])
                acc_ref[rows, :] += mm(pick_ref[rows, :], cot_ref[:, cols]) * y
                ys_ref[rows, :] = (weights[e] * y).astype(BF)
            py_ref[:, cols] = mm(put_ref[...], ys_ref[...]).astype(BF)
            return 0

        lax.fori_loop(0, width // tile, ahead, 0)
        for dst, when in ((y_own, p == 0), (y_near.at[0], p == 1),
                          (y_near.at[1], middle_device & (p == 2)),
                          (y_second, (edge & (p == 2)) | (middle_device & (p == 3))),
                          (y_third, edge & (p == 3))):
            @pl.when(when)
            def _():
                pltpu.make_async_copy(py_ref, dst, py_sem.at[0]).start()
        dws[p] = jnp.zeros((8, tokens), F32)
        for e in range(local):
            dot = jnp.sum(acc_ref[pl.ds(e * cap, cap), :], axis=1, keepdims=True)
            hit = slot == meta[e : e + 1, :]
            dws[p, e : e + 1, :] = jnp.sum(jnp.where(hit, dot, 0.0), axis=0, keepdims=True)

        @pl.when(p == 0)
        def _():
            pltpu.make_async_copy(dws.at[p], dw_out.at[me], own_sem.at[1]).start()

        @pl.when(p > 0)
        def _():
            remote(dws.at[p], dw_out.at[me], dw_send.at[src], dw_recv.at[me], "expert",
                   src).start()
        return 0

    lax.fori_loop(0, n, one_source, 0)

    tiles = width // tile
    store = lambda k, e, j: pltpu.make_async_copy(
        stage.at[k], grads_out.at[e, pl.ds(pl.multiple_of(j * tile, tile), tile), :], st_sem.at[k])

    def weight_grads(k, _):
        e, j = lax.div(k, tiles), lax.rem(k, tiles)
        cols = pl.ds(pl.multiple_of(j * tile, tile), tile)
        slot_k = lax.rem(k, 2)

        @pl.when(k >= 2)
        def _():
            store(slot_k, 0, 0).wait()

        xs = xs_ref[e, :, cols]
        stage[slot_k, :, 0:hidden] = mm_tn(xs, dg_ref[e]).astype(BF)
        stage[slot_k, :, hidden : 2 * hidden] = mm_tn(xs, du_ref[e]).astype(BF)
        stage[slot_k, :, 2 * hidden : 3 * hidden] = mm_tn(dy_ref[e, :, cols], hb_ref[e]).astype(BF)
        store(slot_k, e, j).start()
        return 0

    lax.fori_loop(0, local * tiles, weight_grads, 0)
    for k in range(2):
        store(k, 0, 0).wait()

    @pl.when(middle_device)
    def _():
        far_copy().wait_send()
        for d in range(2):
            @pl.when(sends(d, n - 2))
            def _():
                xcopy(d, n - 2).wait_send()
        y_copy(0).start()
        for kind, own in ((0, 1), (1, 2), (2, 0)):
            for part in range(pieces):
                landed = (edge_copy(kind + 1, part) if kind < 2 else pass_copy(1, part))
                landed.wait_recv()
                cols = piece(part)
                transit[kind, :, cols] = (transit[kind, :, cols].astype(F32)
                                          + pdn_ref[own, :, cols].astype(F32)).astype(BF)
                pass_copy(kind, part).start()
        for kind in range(2):
            y_copy(kind).wait()
        for part in range(pieces):
            edge_copy(0, part).wait_recv()
            pass_copy(0, part).wait_recv()
            for kind in range(3):
                pass_copy(kind, part).wait_send()

    @pl.when(edge)
    def _():
        for part in range(pieces):
            pass_copy(0, part).wait_recv()
            for kind in (1, 2):
                edge_copy(kind, part).wait_send()
        y_copy(0).wait()

    pltpu.make_async_copy(py_ref, y_own, py_sem.at[0]).wait()
    pltpu.make_async_copy(dws.at[0], dw_out.at[me], own_sem.at[1]).wait()
    for d in range(2):
        for s in range(n - 2):
            @pl.when(sends(d, s))
            def _():
                xcopy(d, s).wait_send()
    for j in range(n):
        @pl.when(me != j)
        def _():
            meta_copy(j).wait_send()
            remote(dws.at[0], dw_out.at[me], dw_send.at[j], dw_recv.at[me], "expert",
                   j).wait_send()
            remote(dws.at[0], dw_out.at[j], dw_send.at[j], dw_recv.at[j], "expert", j).wait_recv()


def moe(x, cot, cot_left, cot_right, second_left, second_right, meta, gate, up, down, cap):
    n = meta.shape[0]
    tokens, width = x.shape
    local, _, hidden = gate.shape
    tile = 256
    anywhere = pl.BlockSpec(memory_space=pl.ANY)
    dma = pltpu.SemaphoreType.DMA
    shape = jax.ShapeDtypeStruct
    return pl.pallas_call(
        functools.partial(moe_kernel, cap, tile, n),
        out_shape=(
            shape((3, tokens, width), BF), shape((n, 8, tokens), F32), shape((tokens, width), BF),
            shape((2, tokens, width), BF), shape((tokens, width), BF), shape((tokens, width), BF),
            shape((2, tokens, width), BF),
            shape((local, width, 3 * hidden), BF),
            shape((n, tokens, width), BF), shape((tokens, width), BF),
        ),
        in_specs=[anywhere] * 10,
        out_specs=[anywhere] * 10,
        scratch_shapes=[
            pltpu.VMEM((local, width, hidden), BF), pltpu.VMEM((local, width, hidden), BF),
            pltpu.VMEM((local, width, hidden), BF),
            pltpu.VMEM((tokens, width), BF), pltpu.VMEM((tokens, width), BF),
            pltpu.VMEM((n, 8, tokens), F32),
            pltpu.VMEM((local, n * cap, width), BF), pltpu.VMEM((local, n * cap, width), BF),
            pltpu.VMEM((local, n * cap, hidden), BF), pltpu.VMEM((local, n * cap, hidden), BF),
            pltpu.VMEM((local, n * cap, hidden), BF),
            pltpu.VMEM((3, tokens, width), BF), pltpu.VMEM((3, tokens, width), BF),
            pltpu.VMEM((tokens, width), BF), pltpu.VMEM((n, 8, tokens), F32),
            pltpu.VMEM((local * cap, tokens), BF), pltpu.VMEM((tokens, local * cap), BF),
            pltpu.VMEM((local * cap, tile), BF), pltpu.VMEM((local * cap, tile), F32),
            pltpu.VMEM((2, tile, 3 * hidden), BF),
            dma((3,)), dma((3,)), dma((2, n - 1)), dma((2, n - 1)), dma((2,)), dma((n,)), dma((n,)),
            dma((3, width // tile)), dma((5, width // tile)), dma((n,)), dma((n,)), dma((1,)), dma((2,)), dma((2,)),
            dma((2,)), dma((2,)),
        ],
        compiler_params=pltpu.CompilerParams(
            vmem_limit_bytes=MOE_VMEM, collective_id=1, has_side_effects=True
        ),
        cost_estimate=pl.CostEstimate(
            flops=2 * n * local * cap * width * (9 * hidden + 5 * tokens),
            transcendentals=n * local * cap * hidden,
            bytes_accessed=2 * (8 * n * tokens * width + 6 * local * width * hidden),
        ),
        name="moe",
    )(x, cot, cot_left, cot_right, second_left, second_right, meta, gate, up, down)


RIGHT = [(0, 1), (1, 2), (2, 3)]
LEFT = [(1, 0), (2, 1), (3, 2)]
RIGHT_ON = [(1, 2), (2, 3)]
LEFT_ON = [(1, 0), (2, 1)]
ACROSS = [(0, 2), (1, 3), (2, 0), (3, 1)]
FAR = [(0, 3), (3, 0)]


def project_kernel(x_ref, wq_own, wk_own, wv_own, small_own, cos_ref, sin_ref,
                   q_ref, xa_ref, kv_ref, wq_ref, wk_ref, wv_ref, small_ref,
                   small_in, root_ref, acc_ref, send_sem, recv_sem, own_sem):
    ctx = lax.axis_index("context")
    tokens, width = x_ref.shape
    kv_width = wk_ref.shape[1]
    half = width // 2
    barrier = pltpu.get_barrier_semaphore()
    pl.semaphore_signal(barrier, inc=1, device_id={"context": 1 - ctx},
                        device_id_type=pl.DeviceIdType.MESH)
    pl.semaphore_wait(barrier, 1)

    own = pl.ds(pl.multiple_of(ctx * half, 128), half)
    other = pl.ds(pl.multiple_of((1 - ctx) * half, 128), half)
    ours = pl.ds(pl.multiple_of(ctx * tokens, 16), tokens)
    give = lambda k, src, dst: remote(src, dst, send_sem.at[k], recv_sem.at[k], "context", 1 - ctx)
    weights = ((wk_own, wk_ref), (wv_own, wv_ref), (wq_own, wq_ref))
    sends = [give(0, small_own, small_in)]
    sends += [give(1 + k, a, b.at[own, :]) for k, (a, b) in enumerate(weights)]
    for copy in sends:
        copy.start()
    keeps = [pltpu.make_async_copy(a, b.at[own, :], own_sem.at[k])
             for k, (a, b) in enumerate(weights)]
    for copy in keeps:
        copy.start()

    strip = 64

    def scale(k, _):
        rows = pl.ds(pl.multiple_of(k * strip, strip), strip)
        root = inverse_root(x_ref[rows, :].astype(F32))
        root_ref[rows, :] = root
        xa_ref[rows, own] = (x_ref[rows, own].astype(F32) * root * small_own[0:1, :]).astype(BF)
        return 0

    lax.fori_loop(0, tokens // strip, scale, 0)
    for copy in keeps:
        copy.wait()

    acc_ref[:, 0:kv_width] = mm(xa_ref[:, own], wk_ref[own, :])
    acc_ref[:, kv_width : 2 * kv_width] = mm(xa_ref[:, own], wv_ref[own, :])
    tile = 256

    def first(j, _):
        cols = pl.ds(pl.multiple_of(j * tile, tile), tile)
        at = pl.ds(pl.multiple_of(2 * kv_width + j * tile, tile), tile)
        acc_ref[:, at] = mm(xa_ref[:, own], wq_ref[own, cols])
        return 0

    lax.fori_loop(0, width // tile, first, 0)

    sends[0].wait()
    small_ref[:, own] = small_own[...]
    small_ref[:, other] = small_in[...]

    def rest(k, _):
        rows = pl.ds(pl.multiple_of(k * strip, strip), strip)
        xa_ref[rows, other] = (x_ref[rows, other].astype(F32) * root_ref[rows, :]
                               * small_in[0:1, :]).astype(BF)
        return 0

    lax.fori_loop(0, tokens // strip, rest, 0)

    def rope(v):
        parts = []
        for h in range(v.shape[1] // HEAD_SIZE):
            t = v[:, h * HEAD_SIZE : (h + 1) * HEAD_SIZE]
            t = t * cos_ref[...] + pltpu.roll(t, HEAD_SIZE // 2, 1) * sin_ref[...]
            parts.append(t.astype(BF))
        return jnp.concatenate(parts, axis=1)

    sends[1].wait()
    sends[2].wait()
    k = acc_ref[:, 0:kv_width] + mm(xa_ref[:, other], wk_ref[other, :])
    v = acc_ref[:, kv_width : 2 * kv_width] + mm(xa_ref[:, other], wv_ref[other, :])
    kv_ref[ours, 0:kv_width] = rope(k)
    kv_ref[ours, kv_width : 2 * kv_width] = v.astype(BF)
    kv_copy = give(4, kv_ref.at[ours, :], kv_ref.at[ours, :])
    kv_copy.start()
    sends[3].wait()

    def second(j, _):
        cols = pl.ds(pl.multiple_of(j * tile, tile), tile)
        at = pl.ds(pl.multiple_of(2 * kv_width + j * tile, tile), tile)
        q_ref[:, cols] = rope(acc_ref[:, at] + mm(xa_ref[:, other], wq_ref[other, cols]))
        return 0

    lax.fori_loop(0, width // tile, second, 0)
    kv_copy.wait()


def project(x, wq, wk, wv, small, cos, sin):
    tokens, width = x.shape
    kv_width = wk.shape[1]
    vmem = pl.BlockSpec(memory_space=pltpu.VMEM)
    anywhere = pl.BlockSpec(memory_space=pl.ANY)
    dma = pltpu.SemaphoreType.DMA
    shape = jax.ShapeDtypeStruct
    return pl.pallas_call(
        project_kernel,
        out_shape=(
            shape((tokens, width), BF), shape((tokens, width), BF),
            shape((2 * tokens, 2 * kv_width), BF), shape((width, width), BF),
            shape((width, kv_width), BF), shape((width, kv_width), BF),
            shape((small.shape[0], width), F32),
        ),
        in_specs=[vmem, anywhere, anywhere, anywhere, vmem, vmem, vmem],
        out_specs=[vmem] * 7,
        scratch_shapes=[
            pltpu.VMEM(small.shape, F32), pltpu.VMEM((tokens, 1), F32),
            pltpu.VMEM((tokens, width + 2 * kv_width), F32), dma((5,)), dma((5,)), dma((3,)),
        ],
        compiler_params=pltpu.CompilerParams(
            vmem_limit_bytes=VMEM_LIMIT, collective_id=3, has_side_effects=True
        ),
        cost_estimate=pl.CostEstimate(
            flops=2 * tokens * width * (width + 2 * kv_width), transcendentals=0,
            bytes_accessed=8 * width * width,
        ),
        name="project",
    )(x, wq, wk, wv, small, cos, sin)


def exact(a, b, dims):
    return lax.dot_general(a, b, (dims, ((), ())), precision=lax.Precision.HIGHEST,
                           preferred_element_type=F32)


def three_parts(a, b):
    high = a.astype(BF)
    rest = a - high.astype(F32)
    middle = rest.astype(BF)
    low = (rest - middle.astype(F32)).astype(BF)
    return mm_nt(high, b) + mm_nt(middle, b) + mm_nt(low, b)


def mix_kernel(strip, ob_ref, x_ref, wo_ref, small_ref, routed_ref,
               hidden_ref, xq_ref, gates_ref):
    j = pl.program_id(0)
    tile = wo_ref.shape[1]
    cols = pl.ds(pl.multiple_of(j * tile, tile), tile)
    hidden_ref[:, cols] = x_ref[:, cols].astype(F32) + mm(ob_ref[...], wo_ref[...])

    @pl.when(j == pl.num_programs(0) - 1)
    def _():
        def one(k, _):
            rows = pl.ds(pl.multiple_of(k * strip, strip), strip)
            h = hidden_ref[rows, :]
            normed = h * inverse_root(h) * small_ref[1:2, :]
            xq_ref[rows, :] = normed.astype(BF)
            logits = three_parts(normed, small_ref[8:16, :].astype(BF))
            routed = routed_ref[rows, :] > 0.0
            top = jnp.max(jnp.where(routed, logits, NEG), axis=1, keepdims=True)
            power = jnp.where(routed, jnp.exp(jnp.where(routed, logits, top) - top), 0.0)
            gates_ref[rows, :] = power / jnp.sum(power, axis=1, keepdims=True)
            return 0

        lax.fori_loop(0, hidden_ref.shape[0] // strip, one, 0)


def row_strip(tokens):
    return 128 if tokens % 128 == 0 else 64


def mix(ob, x, wo, small, routed):
    tokens, width = x.shape
    tile = 256
    shape = jax.ShapeDtypeStruct
    const = lambda v: pl.BlockSpec(v.shape, lambda j: (0, 0), pipeline_mode=pl.Buffered(1))
    whole = lambda d: pl.BlockSpec((tokens, d), lambda j: (0, 0))
    experts = routed.shape[1]
    return pl.pallas_call(
        functools.partial(mix_kernel, row_strip(tokens)),
        out_shape=(shape((tokens, width), F32), shape((tokens, width), BF),
                   shape((tokens, experts), F32)),
        grid=(width // tile,),
        in_specs=[const(ob), const(x), pl.BlockSpec((width, tile), lambda j: (0, j)), const(small),
                  const(routed)],
        out_specs=[whole(width), whole(width), whole(experts)],
        compiler_params=pltpu.CompilerParams(vmem_limit_bytes=VMEM_LIMIT),
        cost_estimate=pl.CostEstimate(
            flops=2 * tokens * width * width, transcendentals=0, bytes_accessed=4 * width * width),
        name="mix",
    )(ob, x, wo, small, routed)


def turn_kernel(strip, local, flags, dn_ref, dw_ref, kept_ref, gates_ref, hidden_ref, cot_ref,
                wo_ref, small_ref, dh_ref, da_ref, dob_ref, misc_ref,
                normed_ref, dlog_ref, da_all, row_ref, dot_ref):
    j = pl.program_id(0)
    strips = da_all.shape[0] // strip

    @pl.when(j == 0)
    def _():
        for d in range(dw_ref.shape[0]):
            row_ref[d * local : (d + 1) * local, :] = dw_ref[d, 0:local, :]
        dot_ref[...] = row_ref[...].T * kept_ref[...]
        misc_ref[...] = jnp.zeros_like(misc_ref)

    @pl.when(j < strips)
    def _():
        rows = pl.ds(pl.multiple_of(j * strip, strip), strip)
        gain = small_ref[1:2, :]
        gates, dot = gates_ref[rows, :], dot_ref[rows, :]
        dlogits = gates * (dot - jnp.sum(gates * dot, axis=1, keepdims=True))
        dn = jnp.zeros(dh_ref.shape, F32)
        for e in range(dlogits.shape[1]):
            dn = dn + dlogits[:, e : e + 1] * small_ref[8 + e : 9 + e, :]
        for part in range(dn_ref.shape[0]):
            dn = dn + jnp.where(flags[part] > 0, dn_ref[part].astype(F32), 0.0)
        h = hidden_ref[...]
        root = inverse_root(h)
        scaled = h * root
        normed_ref[rows, :] = scaled * gain
        dlog_ref[rows, :] = dlogits
        dh = cot_ref[...].astype(F32) + norm_back(h, root, gain, dn)
        dh_ref[...] = dh
        da = dh.astype(BF)
        da_ref[...] = da
        da_all[rows, :] = da
        misc_ref[8:16, :] += fold_rows(dn * scaled, jnp.sum)

    @pl.when(j >= strips)
    def _():
        tile = wo_ref.shape[0]
        cols = pl.ds(pl.multiple_of((j - strips) * tile, tile), tile)
        dob_ref[...] = mm_nt(da_all[...], wo_ref[...]).astype(BF)
        misc_ref[0:8, cols] = exact(dlog_ref[...], normed_ref[:, cols], ((0,), (0,)))


def turn(flags, dn_parts, dw_parts, kept, gates, hidden, cot, wo, small):
    tokens, width = cot.shape
    tile, strip = 256, row_strip(tokens)
    strips = tokens // strip
    experts = gates.shape[1]
    local = experts // dw_parts.shape[0]
    shape = jax.ShapeDtypeStruct
    once = pl.Buffered(1)
    const = lambda v: pl.BlockSpec(v.shape, lambda j, f: (0,) * v.ndim, pipeline_mode=once)
    early = lambda j: jnp.minimum(j, strips - 1)
    late = lambda j: jnp.maximum(j - strips, 0)
    rows = pl.BlockSpec((strip, width), lambda j, f: (early(j), 0))
    return pl.pallas_call(
        functools.partial(turn_kernel, strip, local),
        out_shape=(shape((tokens, width), F32), shape((tokens, width), BF),
                   shape((tokens, width), BF), shape((16, width), F32)),
        grid_spec=pltpu.PrefetchScalarGridSpec(
            num_scalar_prefetch=1,
            grid=(strips + width // tile,),
            in_specs=[pl.BlockSpec((dn_parts.shape[0], strip, width), lambda j, f: (0, early(j), 0)),
                      const(dw_parts), const(kept), const(gates), rows, rows,
                      pl.BlockSpec((tile, width), lambda j, f: (late(j), 0)), const(small)],
            out_specs=[rows, rows, pl.BlockSpec((tokens, tile), lambda j, f: (0, late(j))),
                       pl.BlockSpec((16, width), lambda j, f: (0, 0))],
            scratch_shapes=[pltpu.VMEM((tokens, width), F32), pltpu.VMEM((tokens, experts), F32),
                            pltpu.VMEM((tokens, width), BF), pltpu.VMEM((experts, tokens), F32),
                            pltpu.VMEM((tokens, experts), F32)],
        ),
        compiler_params=pltpu.CompilerParams(vmem_limit_bytes=VMEM_LIMIT),
        cost_estimate=pl.CostEstimate(
            flops=2 * tokens * width * width, transcendentals=0, bytes_accessed=8 * width * width),
        name="turn",
    )(flags, dn_parts, dw_parts, kept, gates, hidden, cot, wo, small)


WIDE = 512
LINKS = 9


def tail_kernel(ob_ref, da_ref, xa_hbm, q_ref, kv_ref, do_ref, lse_ref, segk_ref, segq_ref,
                cos_ref, sin_ref, wq_hbm, wk_hbm, wv_hbm, dh_hbm, x_hbm, gain_ref, misc_ref,
                qg_out, kg_out, vg_out, og_out, mg_out, gt_ref,
                dq_ref, dkp_ref, dvp_ref, bias_ref, p_ref, dp_ref, kt_ref, dk_acc, dv_acc,
                dkv_in, dkv_ref, part, buf0, buf1, buf2, buf3, buf4, res,
                xa_ref, wq_ref, wk_ref, wv_ref, dh_ref, x_ref,
                kv_sem, send_sem, recv_sem, out_sem, load_sem):
    loads = [pltpu.make_async_copy(a, b, load_sem.at[k]) for k, (a, b) in enumerate((
        (xa_hbm, xa_ref), (wq_hbm, wq_ref), (wk_hbm, wk_ref), (wv_hbm, wv_ref), (dh_hbm, dh_ref),
        (x_hbm, x_ref)))]
    for load in loads:
        load.start()
    ctx = lax.axis_index("context")
    dp = lax.axis_index("dp")
    z = lax.axis_index("expert")
    tokens, width = xa_ref.shape
    kv_width = dkp_ref.shape[1]
    half = width // 2
    chunks = 8
    bit = lambda v: lax.rem(v, 2)
    flip = lambda v: v + 1 - 2 * bit(v)
    far = lambda v: lax.rem(v + 2, 4)
    partner = {"c": ("context", 1 - ctx), "x": ("dp", flip(dp)), "y": ("dp", far(dp)),
               "n": ("expert", flip(z)), "f": ("expert", far(z))}
    side = {"c": ctx, "x": bit(dp), "y": lax.div(dp, 2), "n": bit(z), "f": lax.div(z, 2)}

    barrier = pltpu.get_barrier_semaphore()
    for axis, other in partner.values():
        pl.semaphore_signal(barrier, inc=1, device_id={axis: other},
                            device_id_type=pl.DeviceIdType.MESH)
    pl.semaphore_wait(barrier, len(partner))

    def exchange(src, dst, ss, rs, way):
        axis, other = partner[way]
        return remote(src, dst, ss, rs, axis, other)

    theirs = pl.ds(pl.multiple_of((1 - ctx) * tokens, 16), tokens)
    ours = pl.ds(pl.multiple_of(ctx * tokens, 16), tokens)
    kv_copies = [
        exchange(ref.at[theirs], dkv_in.at[k], kv_sem.at[0, k], kv_sem.at[1, k], "c")
        for k, ref in enumerate((dkp_ref, dvp_ref))
    ]
    sizes = [half // 2, half // 4, half // 8, half // 16]
    bufs = [buf1, buf2, buf3, buf4]
    columns = [WIDE] * (chunks - 1) + [128]

    def flows(c):
        w = columns[c] // 2 if columns[c] >= 256 else columns[c]
        ways = [("n", "x", "y", "f"), ("y", "x", "n", "f"), ("n", "y", "x", "f"), ("x", "y", "n", "f")]
        return [(k, k * w, w, ways[(k + 2 * c) % 4]) for k in range(columns[c] // w)]

    def rows_at(ways, depth):
        first = 0
        for k in range(depth):
            first = first + side[ways[k]] * sizes[k]
        return pl.multiple_of(first, 16)

    def plus(dst, drows, dcols, a, arows, size):
        strip = 48
        def one(k, _):
            d = pl.ds(pl.multiple_of(drows + k * strip, 16), strip)
            s = pl.ds(pl.multiple_of(arows + k * strip, 16), strip)
            dst[d, dcols] = (dst[d, dcols].astype(F32) + a[s, dcols].astype(F32)).astype(BF)
            return 0
        lax.fori_loop(0, size // strip, one, 0)

    def link(c, flow, level):
        k, first, w, ways = flow
        cols = pl.ds(first, w)
        ss, rs = send_sem.at[c, k, level], recv_sem.at[c, k, level]
        if level == 0:
            src = part.at[c % 4, pl.ds(pl.multiple_of((1 - ctx) * half, 16), half), cols]
            return exchange(src, buf0.at[c, :, cols], ss, rs, "c")
        if level <= 4:
            way, size = ways[level - 1], sizes[level - 1]
            before = buf0 if level == 1 else bufs[level - 2]
            src = before.at[c, pl.ds(pl.multiple_of((1 - side[way]) * size, 16), size), cols]
            return exchange(src, bufs[level - 1].at[c, :, cols], ss, rs, way)
        depth = 8 - level + 1
        size = sizes[depth - 1]
        rows = pl.ds(rows_at(ways, depth), size)
        return exchange(res.at[c, rows, cols], res.at[c, rows, cols], ss, rs, ways[depth - 1])

    def produce(c):
        if c < 7:
            left, right, first = ((ob_ref, da_ref, c * WIDE) if c < 3 else
                                  (xa_ref, dq_ref, (c - 3) * WIDE) if c < 6 else
                                  (xa_ref, dkv_ref, 0))
            if c == 3:
                loads[0].wait()
            tall = width // 2
            def one(j, _):
                rows = pl.ds(pl.multiple_of(j * tall, tall), tall)
                part[c % 4, rows, :] = mm_tn(left[:, rows], right[:, first : first + WIDE]).astype(BF)
                return 0
            lax.fori_loop(0, width // tall, one, 0)
        else:
            part[c % 4, :, 0:128] = jnp.zeros((width, 128), BF)
            part[c % 4, :, 0:16] = misc_rows.T.astype(BF)
            part[c % 4, :, 16:24] = gain_rows.T.astype(BF)

    def finish(c):
        for copy in out_copy(c):
            copy.start()

    def out_copy(c):
        copy = lambda first, w, dst, at, k: pltpu.make_async_copy(
            res.at[c, :, pl.ds(first, w)], dst.at[:, pl.ds(at, w)], out_sem.at[c, k])
        if c < 3:
            return [copy(0, WIDE, og_out, c * WIDE, 0)]
        if c < 6:
            return [copy(0, WIDE, qg_out, (c - 3) * WIDE, 0)]
        if c == 6:
            return [copy(0, kv_width, kg_out, 0, 0), copy(kv_width, kv_width, vg_out, 0, 1)]
        return [copy(0, 128, mg_out, 0, 0)]

    def do(c, level):
        if level == 0:
            produce(c)
        for flow in flows(c):
            k, first, w, ways = flow
            cols = pl.ds(first, w)
            if level > 0:
                link(c, flow, level - 1).wait()
            if level == 1:
                plus(buf0.at[c], 0, cols, part.at[c % 4], ctx * half, half)
            elif 1 < level <= 4:
                before = buf0 if level == 2 else bufs[level - 3]
                plus(bufs[level - 2].at[c], 0, cols, before.at[c],
                     side[ways[level - 2]] * sizes[level - 2], sizes[level - 2])
            elif level == 5:
                rows = pl.ds(rows_at(ways, 4), sizes[3])
                keep = pl.ds(pl.multiple_of(side[ways[3]] * sizes[3], 16), sizes[3])
                res[c, rows, cols] = (buf4[c, :, cols].astype(F32)
                                      + buf3[c, keep, cols].astype(F32)).astype(BF)
            if level < LINKS:
                link(c, flow, level).start()
        if level == LINKS:
            finish(c)

    length = kv_ref.shape[0]
    tq = tokens // 2
    kb = tq
    reach = length // 2
    make_bias(ctx, tokens, segk_ref, segq_ref, bias_ref)

    def attend(index):
        step, piece = index // 2, index % 2
        group, place = step * HEADS_AT_ONCE // GROUP, step * HEADS_AT_ONCE % GROUP
        k_at = slice(group * HEAD_SIZE, (group + 1) * HEAD_SIZE)
        v_at = slice(kv_width + group * HEAD_SIZE, kv_width + (group + 1) * HEAD_SIZE)
        if place == 0 and piece == 0:
            kt_ref[...] = kv_ref[:, k_at].astype(F32).T.astype(BF)
            dk_acc[...] = jnp.zeros_like(dk_acc)
            dv_acc[...] = jnp.zeros_like(dv_acc)
        cols = pl.ds(piece * tq, tq)
        high = ctx * 2 + piece + 1
        low = jnp.maximum(high - 1 - reach // kb, 0)
        heads = [step * HEADS_AT_ONCE + h for h in range(HEADS_AT_ONCE)]
        at = [slice(h * HEAD_SIZE, (h + 1) * HEAD_SIZE) for h in heads]

        def score(i, deltas):
            rows = pl.ds(pl.multiple_of(i * kb, kb), kb)
            key, value, bias = kv_ref[rows, k_at], kv_ref[rows, v_at], bias_ref[rows, cols]
            out = []
            for h in range(HEADS_AT_ONCE):
                s = mm_nt(key, q_ref[cols, at[h]]) * SCALE + bias
                p = jnp.exp(s - lse_ref[heads[h], :, cols])
                dp = mm_nt(value, do_ref[cols, at[h]])
                p_ref[h, rows, :] = p
                dp_ref[h, rows, :] = dp
                out.append(deltas[h] + fold_rows(p * dp, jnp.sum))
            return tuple(out)

        deltas = lax.fori_loop(low, high, score, tuple(jnp.zeros((8, tq), F32) for _ in heads))
        deltas = [jnp.sum(d, axis=0, keepdims=True) for d in deltas]

        def grads(i, dqs):
            rows = pl.ds(pl.multiple_of(i * kb, kb), kb)
            kt = kt_ref[:, rows]
            out, dk, dv = [], dk_acc[rows, :], dv_acc[rows, :]
            for h in range(HEADS_AT_ONCE):
                p = p_ref[h, rows, :]
                ds = (p * (dp_ref[h, rows, :] - deltas[h])).astype(BF)
                dv = dv + mm(p.astype(BF), do_ref[cols, at[h]])
                dk = dk + mm(ds, q_ref[cols, at[h]])
                out.append(dqs[h] + mm(kt, ds))
            dk_acc[rows, :] = dk
            dv_acc[rows, :] = dv
            return tuple(out)

        dqs = lax.fori_loop(low, high, grads,
                            tuple(jnp.zeros((HEAD_SIZE, tq), F32) for _ in heads))
        for h in range(HEADS_AT_ONCE):
            dq = dqs[h].T * SCALE
            turned = pltpu.roll(dq, HEAD_SIZE // 2, 1)
            dq_ref[cols, at[h]] = (dq * cos_ref[cols, :] - turned * sin_ref[cols, :]).astype(BF)
        if place == GROUP - HEADS_AT_ONCE and piece == 1:
            dkp_ref[:, k_at] = (dk_acc[...] * SCALE).astype(BF)
            dvp_ref[:, k_at] = dv_acc[...].astype(BF)

    gain_rows = None
    misc_rows = misc_ref[...]
    steps = 2 * QUERY_HEADS // HEADS_AT_ONCE
    begin = [0, 0, 0, 3, 3, 3, 3, 5]
    paces = begin[3]
    for t in range(begin[-1] + LINKS + 1):
        if t == begin[6]:
            for copy in kv_copies:
                copy.wait()
            for h in range(kv_width // HEAD_SIZE):
                at = slice(h * HEAD_SIZE, (h + 1) * HEAD_SIZE)
                dk = dkp_ref[ours, at].astype(F32) + dkv_in[0, :, at].astype(F32)
                turned = pltpu.roll(dk, HEAD_SIZE // 2, 1)
                dkv_ref[:, at] = (dk * cos_ref[...] - turned * sin_ref[...]).astype(BF)
            dv = dvp_ref[ours, :].astype(F32) + dkv_in[1].astype(F32)
            dkv_ref[:, kv_width : 2 * kv_width] = dv.astype(BF)
        for c in range(chunks):
            if 0 <= t - begin[c] <= LINKS:
                do(c, t - begin[c])
        if t < paces:
            for k in (range(2), range(2, 6), range(6, steps))[t]:
                attend(k)
        if t == paces - 1:
            for copy in kv_copies:
                copy.start()
        if t == begin[7] - 1:
            for load in loads[1:]:
                load.wait()

            def column(j, _):
                cols = pl.ds(pl.multiple_of(j * tq, tq), tq)
                tile = mm_nt(dq_ref[...], wq_ref[cols, :])
                tile = tile + mm_nt(dkv_ref[:, 0:kv_width], wk_ref[cols, :])
                tile = tile + mm_nt(dkv_ref[:, kv_width : 2 * kv_width], wv_ref[cols, :])
                at = pl.ds(pl.multiple_of(lax.rem(j, 2) * tokens, 16), tokens)
                p_ref[lax.div(j, 2), at, :] = tile
                return 0

            lax.fori_loop(0, width // tq, column, 0)
            step = 128

            def strip(k, total):
                rows = pl.ds(pl.multiple_of(k * step, step), step)
                dxa = jnp.concatenate([
                    p_ref[j // 2, pl.ds(pl.multiple_of(j % 2 * tokens + k * step, step), step), :]
                    for j in range(width // tq)], axis=1)
                v = x_ref[rows, :].astype(F32)
                root = inverse_root(v)
                back = dh_ref[rows, :] + norm_back(v, root, gain_ref[0:1, :], dxa)
                gt_ref[rows, :] = back.astype(BF)
                return total + fold_rows(dxa * v * root, jnp.sum)

            total = lax.fori_loop(0, tokens // step, strip, jnp.zeros((8, width), F32))
            gain_rows = jnp.broadcast_to(jnp.sum(total, axis=0, keepdims=True), (8, width))
    for c in range(chunks):
        for copy in out_copy(c):
            copy.wait()


def tail(ob, da, xa, q, kv, do, lse, segk, segq, cos, sin, wq, wk, wv, dh, x, gain, misc):
    tokens, width = xa.shape
    length, kv_width = kv.shape[0], kv.shape[1] // 2
    tq = tokens // 2
    half = width // 2
    vmem = pl.BlockSpec(memory_space=pltpu.VMEM)
    anywhere = pl.BlockSpec(memory_space=pl.ANY)
    dma = pltpu.SemaphoreType.DMA
    shape = jax.ShapeDtypeStruct
    chunks = 8
    return pl.pallas_call(
        tail_kernel,
        out_shape=(
            shape((half, width), BF), shape((half, kv_width), BF), shape((half, kv_width), BF),
            shape((half, width), BF), shape((half, 128), BF), shape((tokens, width), BF),
        ),
        in_specs=[vmem, vmem, anywhere] + [vmem] * 8 + [anywhere] * 5 + [vmem] * 2,
        out_specs=[anywhere] * 5 + [vmem],
        scratch_shapes=[
            pltpu.VMEM((tokens, width), BF), pltpu.VMEM((length, kv_width), BF),
            pltpu.VMEM((length, kv_width), BF), pltpu.VMEM((length, tokens), F32),
            pltpu.VMEM((HEADS_AT_ONCE, length, tq), F32),
            pltpu.VMEM((HEADS_AT_ONCE, length, tq), F32),
            pltpu.VMEM((HEAD_SIZE, length), BF), pltpu.VMEM((length, HEAD_SIZE), F32),
            pltpu.VMEM((length, HEAD_SIZE), F32),
            pltpu.VMEM((2, tokens, kv_width), BF), pltpu.VMEM((tokens, 2 * kv_width), BF),
            pltpu.VMEM((4, width, WIDE), BF),
            pltpu.VMEM((chunks, half, WIDE), BF), pltpu.VMEM((chunks, half // 2, WIDE), BF),
            pltpu.VMEM((chunks, half // 4, WIDE), BF), pltpu.VMEM((chunks, half // 8, WIDE), BF),
            pltpu.VMEM((chunks, half // 16, WIDE), BF), pltpu.VMEM((chunks, half, WIDE), BF),
            pltpu.VMEM((tokens, width), BF), pltpu.VMEM((width, width), BF),
            pltpu.VMEM((width, kv_width), BF), pltpu.VMEM((width, kv_width), BF),
            pltpu.VMEM((tokens, width), F32), pltpu.VMEM((tokens, width), BF),
            dma((2, 2)), dma((chunks, 2, LINKS)), dma((chunks, 2, LINKS)), dma((chunks, 2)), dma((6,)),
        ],
        compiler_params=pltpu.CompilerParams(
            vmem_limit_bytes=MOE_VMEM, collective_id=2, has_side_effects=True
        ),
        cost_estimate=pl.CostEstimate(
            flops=2 * tokens * width * (2 * width + 4 * kv_width + width),
            transcendentals=0, bytes_accessed=16 * width * width,
        ),
        name="tail",
    )(ob, da, xa, q, kv, do, lse, segk, segq, cos, sin, wq, wk, wv, dh, x, gain, misc)


def finish_kernel(flags, qg_ref, kg_ref, vg_ref, og_ref, misc_ref, y0_ref, y1_ref, y2_ref, y3_ref,
                  hidden_ref, shard_ref,
                  q_out, k_out, v_out, o_out, router_out, first_out, second_out, layer_out,
                  gate_out, up_out, down_out):
    for src, dst in ((qg_ref, q_out), (kg_ref, k_out), (vg_ref, v_out), (og_ref, o_out)):
        dst[...] = src[...].astype(F32)
    out = hidden_ref[...]
    for ref in (y0_ref, y2_ref, y3_ref):
        out = out + ref[...].astype(F32)
    out = out + y1_ref[0].astype(F32)
    out = out + jnp.where(flags[1] > 0, y1_ref[1].astype(F32), 0.0)
    layer_out[...] = out.astype(BF)
    hidden = gate_out.shape[2]
    for k, dst in enumerate((gate_out, up_out, down_out)):
        dst[...] = shard_ref[:, :, k * hidden : (k + 1) * hidden].astype(F32)

    @pl.when(pl.program_id(0) == 0)
    def _():
        misc = misc_ref[...].astype(F32)
        rows = misc.T
        router_out[...] = rows[0 : router_out.shape[0], :]
        first_out[...] = rows[16:17, :]
        second_out[...] = jnp.sum(rows[8:16, :], axis=0, keepdims=True)


def finish(flags, qg, kg, vg, og, misc, y_own, y_in, y_far, hidden, shard, experts):
    half, width = qg.shape
    kv_width = kg.shape[1]
    tokens = hidden.shape[0]
    local, rows, three = shard.shape
    ff = three // 3
    grid = 4
    shape = jax.ShapeDtypeStruct
    cut = lambda r, d: pl.BlockSpec((r // grid, d), lambda i, f: (i, 0))
    const = lambda r, d: pl.BlockSpec((r, d), lambda i, f: (0, 0))
    grads = lambda d: pl.BlockSpec((local, rows // grid, d), lambda i, f: (0, i, 0))
    return pl.pallas_call(
        finish_kernel,
        out_shape=(
            shape((half, width), F32), shape((half, kv_width), F32), shape((half, kv_width), F32),
            shape((half, width), F32), shape((experts, half), F32), shape((1, half), F32),
            shape((1, half), F32),
            shape((tokens, width), BF), shape((local, rows, ff), F32),
            shape((local, rows, ff), F32), shape((local, rows, ff), F32),
        ),
        grid_spec=pltpu.PrefetchScalarGridSpec(
            num_scalar_prefetch=1,
            grid=(grid,),
            in_specs=[
                cut(half, width), cut(half, kv_width), cut(half, kv_width), cut(half, width),
                const(half, 128), cut(tokens, width),
                pl.BlockSpec((2, tokens // grid, width), lambda i, f: (0, i, 0)),
                cut(tokens, width), cut(tokens, width), cut(tokens, width), grads(three),
            ],
            out_specs=[
                cut(half, width), cut(half, kv_width), cut(half, kv_width), cut(half, width),
                const(experts, half), const(1, half), const(1, half), cut(tokens, width), grads(ff), grads(ff),
                grads(ff),
            ],
        ),
        compiler_params=pltpu.CompilerParams(vmem_limit_bytes=VMEM_LIMIT),
        cost_estimate=pl.CostEstimate(flops=0, transcendentals=0, bytes_accessed=16 * half * width),
        name="finish",
    )(flags, qg, kg, vg, og, misc, y_own, y_in, *y_far, hidden, shard)


def body(
    tokens, cotangent, segment_ids, routes, fill_rank, query_weight, key_projection_weight,
    value_projection_weight, output_weight, router_weight, gain_attention, gain_experts,
    gate_weight, up_weight, down_weight,
):
    context_index = lax.axis_index("context")
    context_size = lax.axis_size("context")
    expert_size = lax.axis_size("expert")
    rows = tokens.shape[1]
    length = segment_ids.shape[1]
    kv_width = KEY_VALUE_HEADS * HEAD_SIZE
    gather = lambda w, axis=0: lax.all_gather(w, "context", axis=axis, tiled=True)
    x, upstream = tokens[0], cotangent[0]

    cot_left = lax.ppermute(upstream, "expert", RIGHT)
    cot_right = lax.ppermute(upstream, "expert", LEFT)

    expert_count = router_weight.shape[1]
    local = gate_weight.shape[0]
    capacity = 5 * rows * TOP // (4 * expert_count)
    cap = -(-capacity // 64) * 64
    names = jnp.arange(expert_count, dtype=jnp.int32)
    route_hit = routes[0][:, :, None] == names[None, None, :]
    routed = jnp.any(route_hit, axis=1)
    ranks = fill_rank[0, 0].reshape(rows, TOP)
    order = jnp.sum(jnp.where(route_hit, ranks[:, :, None], 0), axis=1)
    order = jnp.where(routed, order, rows * TOP).T
    slots = jnp.sum((order[:, :, None] < order[:, None, :]).astype(jnp.int32), axis=1)
    kept = routed.T & (slots < capacity)
    slots = jnp.where(kept, slots, -1).astype(F32)
    kept_float = kept.T.astype(F32)

    small = jnp.concatenate([
        gain_attention[None], gain_experts[None], jnp.zeros((6, gain_attention.shape[0]), BF),
        router_weight.T,
    ]).astype(F32)
    positions = context_index * rows + jnp.arange(rows, dtype=jnp.int32)
    cosine, sine = rope_tables(positions)
    cos_full = jnp.concatenate([cosine, cosine], axis=-1)
    sin_full = jnp.concatenate([-sine, sine], axis=-1)
    turned = lambda v, heads, d: apply_rotary(
        v.reshape(rows, heads, HEAD_SIZE), cosine, sine, d
    ).reshape(rows, heads * HEAD_SIZE)
    output_full = gather(output_weight)
    if context_size == 2:
        q, attn_input, kv, query_full, key_full, value_full, small = project(
            x, query_weight, key_projection_weight, value_projection_weight, small,
            cos_full, sin_full,
        )
    else:
        query_full, key_full, value_full = (
            gather(query_weight), gather(key_projection_weight), gather(value_projection_weight)
        )
        small = gather(small.astype(BF), 1).astype(F32)
        residual = x.astype(F32)
        attn_input = (residual * inverse_root(residual) * small[0]).astype(BF)
        q = turned(mm(attn_input, query_full), QUERY_HEADS, 1.0).astype(BF)
        k_own = turned(mm(attn_input, key_full), KEY_VALUE_HEADS, 1.0).astype(BF)
        kv = gather(jnp.concatenate([k_own, mm(attn_input, value_full).astype(BF)], axis=1))
    segments = segment_ids[0]
    tq, kb = attention_sizes(rows, length)
    spans = attention_meta(context_index, rows, segments, tq, kb)
    segk = segments[:, None]
    segq = lax.dynamic_slice_in_dim(segments, context_index * rows, rows)[None, :]
    cot_left, cot_right, q, kv, spans, segk, segq, slots, kept_float, routed_float = (
        lax.optimization_barrier((cot_left, cot_right, q, kv, spans, segk, segq, slots, kept_float,
                                  routed.astype(F32))))
    second_left = lax.ppermute(cot_left, "expert", RIGHT_ON)
    second_right = lax.ppermute(cot_right, "expert", LEFT_ON)
    mixed, lse = attention_forward(q, kv, spans, segk, segq)

    hidden, expert_input, gates = mix(mixed, x, output_full, small, routed_float)
    expert_index = lax.axis_index("expert")
    between = (expert_index > 0) & (expert_index < expert_size - 1)
    flags = jnp.stack([expert_size > 0, between, expert_size > 0]).astype(jnp.int32)
    second_left, second_right, expert_input, flags = lax.optimization_barrier(
        (second_left, second_right, expert_input, flags))
    routing = jnp.stack([slots, (gates * kept_float).T], axis=0)
    routing = routing.reshape(2, expert_size, local, rows).transpose(1, 0, 2, 3)
    routing = routing.reshape(expert_size, 2 * local, rows)
    routing = jnp.pad(routing, ((0, 0), (0, 8 - 2 * local), (0, 0)))
    dn_parts, dw_parts, y_own, _, y_second, y_third, y_in, grads_low, _, _ = moe(
        expert_input, upstream, cot_left, cot_right, second_left, second_right, routing, gate_weight, up_weight,
        down_weight, cap,
    )
    y_far = (lax.ppermute(y_third, "expert", FAR), lax.ppermute(y_second, "expert", ACROSS))
    grads_shard = lax.psum_scatter(
        grads_low, ("dp", "context"), scatter_dimension=1, tiled=True
    )

    hidden_total, attn_grad_low, mixed_grad_low, misc = turn(
        flags, dn_parts, dw_parts, kept_float, gates, hidden, upstream, output_full, small
    )
    if (lax.axis_size("dp"), context_size, expert_size) == (4, 2, 4):
        *sums, grad_tokens = tail(
            mixed, attn_grad_low, attn_input, q, kv, mixed_grad_low, lse, segk, segq,
            cos_full, sin_full, query_full, key_full, value_full, hidden_total, x, small, misc,
        )
        late, grad_tokens = lax.optimization_barrier((hidden, grad_tokens))
        (query_grad, key_grad, value_grad, output_grad, router_grad, first, second, layer_out,
         *expert_sums) = finish(flags, *sums, y_own, y_in, y_far, late, grads_shard, expert_count)
        sums = (query_grad, key_grad, value_grad, output_grad, router_grad.T, first[0], second[0])
    else:
        dq_low, dk_part, dv_part = attention_backward(
            q, kv, mixed_grad_low, lse, cos_full, sin_full, spans, segk, segq
        )
        dkv = lax.psum_scatter(
            jnp.concatenate([dk_part, dv_part], axis=1), "context", scatter_dimension=0, tiled=True
        )
        dk_low = turned(dkv[:, :kv_width].astype(F32), KEY_VALUE_HEADS, -1.0).astype(BF)
        dv_low = dkv[:, kv_width:]
        input_total = (
            mm_nt(dq_low, query_full) + mm_nt(dk_low, key_full) + mm_nt(dv_low, value_full)
        )
        residual = x.astype(F32)
        root = inverse_root(residual)
        grad_tokens = (hidden_total + norm_back(residual, root, small[0], input_total)).astype(BF)
        reduce_rows = lambda v: lax.psum(
            lax.psum_scatter(v.astype(BF), "context", scatter_dimension=0, tiled=True),
            ("dp", "expert"),
        ).astype(F32)
        sums = tuple(reduce_rows(v) for v in (
            mm_tn(attn_input, dq_low), mm_tn(attn_input, dk_low), mm_tn(attn_input, dv_low),
            mm_tn(mixed, attn_grad_low), misc[:8].T,
            jnp.sum(input_total * residual * root, axis=0), jnp.sum(misc[8:16], axis=0),
        ))
        mixture = sum(v.astype(F32) for v in (y_own, y_in[0], *y_far))
        mixture = mixture + jnp.where(between, y_in[1].astype(F32), 0.0)
        layer_out = (hidden + mixture).astype(BF)
        ff = gate_weight.shape[2]
        wide = grads_shard.astype(F32)
        expert_sums = [wide[:, :, i * ff : (i + 1) * ff] for i in range(3)]
    return (layer_out[None], grad_tokens[None], *sums, *expert_sums)


def solution(mesh):
    both = ("dp", "expert")
    token_spec = P(both, "context", None)
    row_spec = P("context", None)
    expert_out = P("expert", ("dp", "context"), None)
    return jax.shard_map(
        body,
        mesh=mesh,
        in_specs=(
            token_spec, token_spec, P(both, None), token_spec, token_spec,
            row_spec, row_spec, row_spec, row_spec, row_spec, P("context"), P("context"),
            P("expert", None, None), P("expert", None, None), P("expert", None, None),
        ),
        out_specs=(
            token_spec, token_spec, row_spec, row_spec, row_spec, row_spec, row_spec,
            P("context"), P("context"), expert_out, expert_out, expert_out,
        ),
        check_vma=False,
    )
```

```python
import functools
import math

import jax
import jax.numpy as jnp
from jax import lax
from jax.experimental import pallas as pl
from jax.experimental.pallas import tpu as pltpu
from jax.sharding import PartitionSpec as P

MODEL_WIDTH = 1536
QUERY_HEADS = 12
KEY_VALUE_HEADS = 2
HEAD_SIZE = 128
TOP = 4
GROUP = QUERY_HEADS // KEY_VALUE_HEADS
norm_eps = 1e-06
rope_base = 10000.0
NEG = -1e30
HEADS_AT_ONCE = 3
SCALE = 1.0 / math.sqrt(HEAD_SIZE)
BF = jnp.bfloat16
F32 = jnp.float32
VMEM_LIMIT = 60 * 1024 * 1024
MOE_VMEM = 63 * 1024 * 1024


def mm(a, b):
    return jnp.dot(a, b, preferred_element_type=F32)


def mm_nt(a, b):
    return lax.dot_general(a, b, (((1,), (1,)), ((), ())), preferred_element_type=F32)


def mm_tn(a, b):
    return lax.dot_general(a, b, (((0,), (0,)), ((), ())), preferred_element_type=F32)


def inverse_root(v):
    return lax.rsqrt(jnp.mean(v * v, axis=-1, keepdims=True) + norm_eps)


def norm_back(v, root, gain, upstream):
    scaled = upstream * gain
    cubed = root * root * root
    return root * scaled - v * cubed * jnp.mean(v * scaled, axis=-1, keepdims=True)


def rope_tables(positions):
    half = HEAD_SIZE // 2
    frequency = jnp.exp(
        -(jnp.arange(half, dtype=F32) * (2.0 / HEAD_SIZE)) * math.log(rope_base)
    )
    angle = positions.astype(F32)[:, None] * frequency[None, :]
    return jnp.cos(angle), jnp.sin(angle)


def apply_rotary(v, cosine, sine, direction):
    half = HEAD_SIZE // 2
    a, b = v[..., :half], v[..., half:]
    c, s = cosine[:, None, :], sine[:, None, :]
    return jnp.concatenate([a * c - direction * b * s, b * c + direction * a * s], axis=-1)


def fold_rows(v, op):
    rows, cols = v.shape
    return op(v.reshape(rows // 8, 8, cols), axis=0)


def make_bias(ctx, tokens, segk_ref, segq_ref, bias_ref):
    length = segk_ref.shape[0]
    key_pos = lax.broadcasted_iota(jnp.int32, (length, tokens), 0)
    query_pos = lax.broadcasted_iota(jnp.int32, (length, tokens), 1) + ctx * tokens
    same = segk_ref[...] == segq_ref[...]
    bias_ref[...] = jnp.where(same & (key_pos <= query_pos), 0.0, NEG)


def attn_fwd_kernel(kb, tq, meta, q_ref, k_ref, v_ref, segk_ref, segq_ref, o_ref, lse_ref,
                    bias_ref, s_ref, vt_ref):
    step = pl.program_id(0)
    tokens = q_ref.shape[0]

    @pl.when(step == 0)
    def _():
        make_bias(meta[0], tokens, segk_ref, segq_ref, bias_ref)

    @pl.when(lax.rem(step * HEADS_AT_ONCE, GROUP) == 0)
    def _():
        vt_ref[...] = v_ref[...].astype(F32).T.astype(BF)

    heads = [slice(h * HEAD_SIZE, (h + 1) * HEAD_SIZE) for h in range(HEADS_AT_ONCE)]
    for part in range(tokens // tq):
        cols = pl.ds(part * tq, tq)
        low, high = meta[1 + 2 * part], meta[2 + 2 * part]

        def score(i, tops):
            rows = pl.ds(pl.multiple_of(i * kb, kb), kb)
            key, bias = k_ref[rows, :], bias_ref[rows, cols]
            out = []
            for h, at in enumerate(heads):
                s = mm_nt(key, q_ref[cols, at]) * SCALE + bias
                s_ref[h, rows, :] = s
                out.append(jnp.maximum(tops[h], fold_rows(s, jnp.max)))
            return tuple(out)

        tops = lax.fori_loop(low, high, score,
                             tuple(jnp.full((8, tq), NEG, F32) for _ in heads))
        tops = [jnp.max(t, axis=0, keepdims=True) for t in tops]

        def value(i, carry):
            totals, outs = carry
            rows = pl.ds(pl.multiple_of(i * kb, kb), kb)
            vt = vt_ref[:, rows]
            new_totals, new_outs = [], []
            for h in range(HEADS_AT_ONCE):
                p = jnp.exp(s_ref[h, rows, :] - tops[h])
                new_totals.append(totals[h] + fold_rows(p, jnp.sum))
                new_outs.append(outs[h] + mm(vt, p.astype(BF)))
            return tuple(new_totals), tuple(new_outs)

        totals, outs = lax.fori_loop(
            low, high, value, (tuple(jnp.zeros((8, tq), F32) for _ in heads),
                               tuple(jnp.zeros((HEAD_SIZE, tq), F32) for _ in heads)))
        for h, at in enumerate(heads):
            total = jnp.sum(totals[h], axis=0, keepdims=True)
            o_ref[cols, at] = (outs[h] / total).T.astype(BF)
            lse_ref[h, :, cols] = tops[h] + jnp.log(total)


def attn_bwd_kernel(kb, tq, meta, q_ref, k_ref, v_ref, do_ref, lse_ref, cos_ref, sin_ref,
                    segk_ref, segq_ref, dq_ref, dk_ref, dv_ref,
                    bias_ref, p_ref, dp_ref, kt_ref, dk_acc, dv_acc):
    step = pl.program_id(0)
    tokens = q_ref.shape[0]

    @pl.when(step == 0)
    def _():
        make_bias(meta[0], tokens, segk_ref, segq_ref, bias_ref)

    place = lax.rem(step * HEADS_AT_ONCE, GROUP)

    @pl.when(place == 0)
    def _():
        kt_ref[...] = k_ref[...].astype(F32).T.astype(BF)
        dk_acc[...] = jnp.zeros_like(dk_acc)
        dv_acc[...] = jnp.zeros_like(dv_acc)

    heads = [slice(h * HEAD_SIZE, (h + 1) * HEAD_SIZE) for h in range(HEADS_AT_ONCE)]
    for part in range(tokens // tq):
        cols = pl.ds(part * tq, tq)
        low, high = meta[1 + 2 * part], meta[2 + 2 * part]

        def score(i, deltas):
            rows = pl.ds(pl.multiple_of(i * kb, kb), kb)
            key, value, bias = k_ref[rows, :], v_ref[rows, :], bias_ref[rows, cols]
            out = []
            for h, at in enumerate(heads):
                s = mm_nt(key, q_ref[cols, at]) * SCALE + bias
                p = jnp.exp(s - lse_ref[h, :, cols])
                dp = mm_nt(value, do_ref[cols, at])
                p_ref[h, rows, :] = p
                dp_ref[h, rows, :] = dp
                out.append(deltas[h] + fold_rows(p * dp, jnp.sum))
            return tuple(out)

        deltas = lax.fori_loop(low, high, score, tuple(jnp.zeros((8, tq), F32) for _ in heads))
        deltas = [jnp.sum(d, axis=0, keepdims=True) for d in deltas]

        def grads(i, dqs):
            rows = pl.ds(pl.multiple_of(i * kb, kb), kb)
            kt = kt_ref[:, rows]
            out, dk, dv = [], dk_acc[rows, :], dv_acc[rows, :]
            for h, at in enumerate(heads):
                p = p_ref[h, rows, :]
                ds = (p * (dp_ref[h, rows, :] - deltas[h])).astype(BF)
                dv = dv + mm(p.astype(BF), do_ref[cols, at])
                dk = dk + mm(ds, q_ref[cols, at])
                out.append(dqs[h] + mm(kt, ds))
            dk_acc[rows, :] = dk
            dv_acc[rows, :] = dv
            return tuple(out)

        dqs = lax.fori_loop(low, high, grads,
                            tuple(jnp.zeros((HEAD_SIZE, tq), F32) for _ in heads))
        for h, at in enumerate(heads):
            dq = dqs[h].T * SCALE
            turned = pltpu.roll(dq, HEAD_SIZE // 2, 1)
            dq_ref[cols, at] = (dq * cos_ref[cols, :] - turned * sin_ref[cols, :]).astype(BF)

    @pl.when(place == GROUP - HEADS_AT_ONCE)
    def _():
        dk_ref[...] = (dk_acc[...] * SCALE).astype(BF)
        dv_ref[...] = dv_acc[...].astype(BF)


def attention_sizes(tokens, length):
    tq = 256 if tokens % 256 == 0 else tokens
    kb = 256 if length % 256 == 0 else 128
    return tq, kb


def attention_meta(ctx, tokens, segments, tq, kb):
    entries = [ctx]
    for part in range(tokens // tq):
        first = ctx * tokens + part * tq
        own = lax.dynamic_slice_in_dim(segments, first, 1)
        start = jnp.sum((segments < own).astype(jnp.int32))
        entries += [start // kb, (first + tq + kb - 1) // kb]
    return jnp.stack(entries).astype(jnp.int32)


def attention_forward(q, kv, meta, segk, segq):
    tokens, length = q.shape[0], kv.shape[0]
    tq, kb = attention_sizes(tokens, length)
    const = lambda h, m: (0, 0)
    return pl.pallas_call(
        functools.partial(attn_fwd_kernel, kb, tq),
        out_shape=(
            jax.ShapeDtypeStruct(q.shape, BF),
            jax.ShapeDtypeStruct((QUERY_HEADS, 1, tokens), F32),
        ),
        grid_spec=pltpu.PrefetchScalarGridSpec(
            num_scalar_prefetch=1,
            grid=(QUERY_HEADS // HEADS_AT_ONCE,),
            in_specs=[
                pl.BlockSpec((tokens, HEADS_AT_ONCE * HEAD_SIZE), lambda h, m: (0, h)),
                pl.BlockSpec((length, HEAD_SIZE), lambda h, m: (0, h * HEADS_AT_ONCE // GROUP)),
                pl.BlockSpec((length, HEAD_SIZE), lambda h, m: (0, KEY_VALUE_HEADS + h * HEADS_AT_ONCE // GROUP)),
                pl.BlockSpec((length, 1), const),
                pl.BlockSpec((1, tokens), const),
            ],
            out_specs=[
                pl.BlockSpec((tokens, HEADS_AT_ONCE * HEAD_SIZE), lambda h, m: (0, h)),
                pl.BlockSpec((HEADS_AT_ONCE, 1, tokens), lambda h, m: (h, 0, 0)),
            ],
            scratch_shapes=[
                pltpu.VMEM((length, tokens), F32),
                pltpu.VMEM((HEADS_AT_ONCE, length, tq), F32),
                pltpu.VMEM((HEAD_SIZE, length), BF),
            ],
        ),
        compiler_params=pltpu.CompilerParams(vmem_limit_bytes=VMEM_LIMIT),
        cost_estimate=pl.CostEstimate(
            flops=3 * QUERY_HEADS * tokens * length * HEAD_SIZE,
            transcendentals=QUERY_HEADS * tokens * length,
            bytes_accessed=4 * tokens * MODEL_WIDTH,
        ),
        name="attn_fwd",
    )(meta, q, kv, kv, segk, segq)


def attention_backward(q, kv, do, lse, cos, sin, meta, segk, segq):
    tokens, length = q.shape[0], kv.shape[0]
    tq, kb = attention_sizes(tokens, length)
    const = lambda h, m: (0, 0)
    by_head = lambda h, m: (0, h)
    by_group = lambda h, m: (0, h * HEADS_AT_ONCE // GROUP)
    return pl.pallas_call(
        functools.partial(attn_bwd_kernel, kb, tq),
        out_shape=(
            jax.ShapeDtypeStruct(q.shape, BF),
            jax.ShapeDtypeStruct((length, KEY_VALUE_HEADS * HEAD_SIZE), BF),
            jax.ShapeDtypeStruct((length, KEY_VALUE_HEADS * HEAD_SIZE), BF),
        ),
        grid_spec=pltpu.PrefetchScalarGridSpec(
            num_scalar_prefetch=1,
            grid=(QUERY_HEADS // HEADS_AT_ONCE,),
            in_specs=[
                pl.BlockSpec((tokens, HEADS_AT_ONCE * HEAD_SIZE), by_head),
                pl.BlockSpec((length, HEAD_SIZE), by_group),
                pl.BlockSpec((length, HEAD_SIZE), lambda h, m: (0, KEY_VALUE_HEADS + h * HEADS_AT_ONCE // GROUP)),
                pl.BlockSpec((tokens, HEADS_AT_ONCE * HEAD_SIZE), by_head),
                pl.BlockSpec((HEADS_AT_ONCE, 1, tokens), lambda h, m: (h, 0, 0)),
                pl.BlockSpec((tokens, HEAD_SIZE), const),
                pl.BlockSpec((tokens, HEAD_SIZE), const),
                pl.BlockSpec((length, 1), const),
                pl.BlockSpec((1, tokens), const),
            ],
            out_specs=[
                pl.BlockSpec((tokens, HEADS_AT_ONCE * HEAD_SIZE), by_head),
                pl.BlockSpec((length, HEAD_SIZE), by_group),
                pl.BlockSpec((length, HEAD_SIZE), by_group),
            ],
            scratch_shapes=[
                pltpu.VMEM((length, tokens), F32),
                pltpu.VMEM((HEADS_AT_ONCE, length, tq), F32),
                pltpu.VMEM((HEADS_AT_ONCE, length, tq), F32),
                pltpu.VMEM((HEAD_SIZE, length), BF),
                pltpu.VMEM((length, HEAD_SIZE), F32),
                pltpu.VMEM((length, HEAD_SIZE), F32),
            ],
        ),
        compiler_params=pltpu.CompilerParams(vmem_limit_bytes=VMEM_LIMIT),
        cost_estimate=pl.CostEstimate(
            flops=8 * QUERY_HEADS * tokens * length * HEAD_SIZE,
            transcendentals=QUERY_HEADS * tokens * length,
            bytes_accessed=8 * tokens * MODEL_WIDTH,
        ),
        name="attn_bwd",
    )(meta, q, kv, kv, do, lse, cos, sin, segk, segq)


def remote(src, dst, ss, rs, axis, dev):
    return pltpu.make_async_remote_copy(
        src_ref=src, dst_ref=dst, send_sem=ss, recv_sem=rs, device_id={axis: dev},
        device_id_type=pl.DeviceIdType.MESH,
    )


def moe_kernel(cap, tile, n,
               x_hbm, cot_hbm, cotl_hbm, cotr_hbm, cotl2_hbm, cotr2_hbm, meta_hbm, gate_hbm, up_hbm, down_hbm,
               dn_out, dw_out, y_own, y_near, y_second, y_third, y_in, grads_out, xall, cotfar,
               gate_ref, up_ref, down_ref, x_ref, cot_ref, metas, xs_ref, dy_ref, hb_ref, dg_ref,
               du_ref, pdn_ref, transit, py_ref, dws, pick_ref, put_ref, ys_ref, acc_ref, stage,
               wsem, lsem, xs_send, xs_recv, far_sem, m_send, m_recv, dn_send, dn_recv,
               dw_send, dw_recv, py_sem, own_sem, st_sem, y_send, y_recv):
    me = lax.axis_index("expert")
    tokens, width = x_ref.shape
    local, _, hidden = gate_ref.shape
    edge = (me == 0) | (me == n - 1)

    barrier = pltpu.get_barrier_semaphore()
    for d in range(1, n):
        pl.semaphore_signal(barrier, inc=1, device_id={"expert": lax.rem(me + d, n)},
                            device_id_type=pl.DeviceIdType.MESH)
    pl.semaphore_wait(barrier, n - 1)

    def exists(direction, step):
        return (me - 1 - step >= 0) if direction == 0 else (me + 1 + step <= n - 1)

    def sends(direction, step):
        if direction == 0:
            return (me - step >= 0) & (me < n - 1)
        return (me + step <= n - 1) & (me > 0)

    def xcopy(direction, step):
        block = jnp.clip(me - step if direction == 0 else me + step, 0, n - 1)
        target = jnp.clip(me + 1 if direction == 0 else me - 1, 0, n - 1)
        src = x_hbm if step == 0 else xall.at[block]
        return remote(src, xall.at[block], xs_send.at[direction, step],
                      xs_recv.at[direction, step], "expert", target)

    outward = jnp.where(me < 2, 0, n - 1)
    inward = n - 1 - jnp.clip(me, 1, n - 2)
    inner = jnp.where(me < 2, 1, n - 2)
    far_copy = lambda ref=cotl2_hbm: remote(ref, cotfar, far_sem.at[0], far_sem.at[1], "expert",
                                            outward)
    middle_device = jnp.logical_not(edge)

    for d in range(2):
        @pl.when(sends(d, 0))
        def _():
            xcopy(d, 0).start()

    def meta_copy(j):
        return remote(meta_hbm.at[j], metas.at[me], m_send.at[j], m_recv.at[me], "expert", j)

    for j in range(n):
        @pl.when(me != j)
        def _():
            meta_copy(j).start()

    loads = [pltpu.make_async_copy(a, b, wsem.at[k]) for k, (a, b) in enumerate(
        ((gate_hbm, gate_ref), (up_hbm, up_ref), (down_hbm, down_ref)))]
    for load in loads:
        load.start()
    own_meta = pltpu.make_async_copy(meta_hbm.at[me], metas.at[me], lsem.at[2])
    own_meta.start()

    def fetch(a, b):
        cx = pltpu.make_async_copy(a, x_ref, lsem.at[0])
        cc = pltpu.make_async_copy(b, cot_ref, lsem.at[1])
        cx.start()
        cc.start()
        cx.wait()
        cc.wait()

    pieces = width // tile
    piece = lambda part: pl.ds(pl.multiple_of(part * tile, tile), tile)

    def edge_copy(kind, part):
        dst = (dn_out.at[1, :, piece(part)] if kind == 0 else
               transit.at[kind - 1, :, piece(part)])
        return remote(pdn_ref.at[kind, :, piece(part)], dst, dn_send.at[kind, part],
                      dn_recv.at[kind, part], "expert", inner)

    def y_copy(kind):
        target = jnp.where(edge, inner, outward) if kind == 0 else inward
        return remote(y_near.at[kind], y_in.at[kind], y_send.at[kind], y_recv.at[kind], "expert",
                      target)

    def pass_copy(kind, part):
        dst = transit.at[2, :, piece(part)] if kind == 1 else dn_out.at[2, :, piece(part)]
        arrival = dn_recv.at[3, part] if kind != 1 else dn_recv.at[4, part]
        return remote(transit.at[kind, :, piece(part)], dst, dn_send.at[kind, part], arrival,
                      "expert", outward if kind == 2 else inward)

    mirror = me >= 2
    side = jnp.where(mirror, n - 1 - me, me)

    def source_of(p):
        base = jnp.where(p == 0, side, jnp.where(p == 1, 1 - side, p))
        return jnp.where(mirror, n - 1 - base, base)

    def arrive(direction, step):
        @pl.when(exists(direction, step))
        def _():
            xcopy(direction, step).wait_recv()

    def forward(direction, step):
        @pl.when(sends(direction, step))
        def _():
            xcopy(direction, step).start()

    def one_source(p, _):
        src = source_of(p)

        @pl.when(p == 0)
        def _():
            own_meta.wait()

        @pl.when(p > 0)
        def _():
            remote(meta_hbm.at[src], metas.at[src], m_send.at[src], m_recv.at[src], "expert",
                   src).wait_recv()

        meta = metas[src]
        columns = meta.T
        spread = lax.broadcasted_iota(jnp.int32, (tokens, local * cap), 1).astype(F32)
        slot = lax.broadcasted_iota(jnp.int32, (cap, tokens), 0).astype(F32)
        weights, put = [], None
        for e in range(local):
            hit = slot == meta[e : e + 1, :]
            pick_ref[pl.ds(e * cap, cap), :] = jnp.where(hit, 1.0, 0.0).astype(BF)
            weights.append(
                jnp.sum(jnp.where(hit, meta[local + e : local + e + 1, :], 0.0), axis=1,
                        keepdims=True)
            )
            own = columns[:, e : e + 1]
            here = spread == jnp.where(own < 0.0, -1.0, own + e * cap)
            put = here if put is None else put | here
        put_ref[...] = jnp.where(put, 1.0, 0.0).astype(BF)
        @pl.when(p == 0)
        def _():
            fetch(x_hbm, cot_hbm)
            for load in loads:
                load.wait()

        @pl.when(p == 1)
        def _():
            for d in range(2):
                arrive(d, 0)
                forward(d, 1)

            for ref, when in ((cotl2_hbm, me >= 2), (cotr2_hbm, me < 2)):
                @pl.when(middle_device & when)
                def _():
                    far_copy(ref).start()

        @pl.when(p > 0)
        def _():
            pltpu.make_async_copy(py_ref, y_own, py_sem.at[0]).wait()

        @pl.when(middle_device & (p == 3))
        def _():
            y_copy(1).start()

        @pl.when(edge & (p == 2))
        def _():
            for part in range(pieces):
                edge_copy(0, part).wait_send()
            y_copy(0).start()

        @pl.when(((p == 2) & edge) | ((p == 3) & jnp.logical_not(edge)))
        def _():
            for d in range(2):
                arrive(d, 1)
                forward(d, 2)

        @pl.when((p == 3) & edge)
        def _():
            for d in range(2):
                arrive(d, 2)
            far_copy().wait_recv()

        @pl.when((p > 0) & (src == me - 1))
        def _():
            fetch(xall.at[src], cotl_hbm)

        @pl.when((p > 0) & (src == me + 1))
        def _():
            fetch(xall.at[src], cotr_hbm)

        @pl.when(src == me - 2)
        def _():
            fetch(xall.at[src], cotl2_hbm)

        @pl.when(src == me + 2)
        def _():
            fetch(xall.at[src], cotr2_hbm)

        @pl.when((src == me - 3) | (src == me + 3))
        def _():
            fetch(xall.at[src], cotfar)

        mine = pl.ds(pl.multiple_of(p * cap, cap), cap)
        buf = lax.rem(p + 2, 3)

        def gather(j, _):
            cols = pl.ds(pl.multiple_of(j * tile, tile), tile)
            xs = mm(pick_ref[...], x_ref[:, cols]).astype(BF)
            cg = mm(pick_ref[...], cot_ref[:, cols])
            for e in range(local):
                rows = slice(e * cap, (e + 1) * cap)
                xs_ref[e, mine, cols] = xs[rows]
                dy_ref[e, mine, cols] = (weights[e] * cg[rows]).astype(BF)
            return 0

        lax.fori_loop(0, width // tile, gather, 0)

        def middle(j, _):
            cols = pl.ds(pl.multiple_of(j * tile, tile), tile)
            for e in range(local):
                g = mm(xs_ref[e, mine, :], gate_ref[e, :, cols])
                u = mm(xs_ref[e, mine, :], up_ref[e, :, cols])
                dh = mm(dy_ref[e, mine, :], down_ref[e, :, cols])
                s = 1.0 / (1.0 + jnp.exp(-g))
                act = g * s
                hb_ref[e, mine, cols] = (act * u).astype(BF)
                dg_ref[e, mine, cols] = (dh * u * (s * (1.0 + g * (1.0 - s)))).astype(BF)
                du_ref[e, mine, cols] = (dh * act).astype(BF)
            return 0

        lax.fori_loop(0, hidden // tile, middle, 0)


        @pl.when(p == 3)
        def _():
            pltpu.make_async_copy(pdn_ref.at[2], dn_out.at[0], own_sem.at[0]).wait()

        acc_ref[...] = jnp.zeros_like(acc_ref)

        def back(j, _):
            cols = pl.ds(pl.multiple_of(j * tile, tile), tile)
            for e in range(local):
                dxs = mm_nt(dg_ref[e, mine, :], gate_ref[e, cols, :])
                dxs = dxs + mm_nt(du_ref[e, mine, :], up_ref[e, cols, :])
                ys_ref[pl.ds(e * cap, cap), :] = dxs.astype(BF)
            pdn_ref[buf, :, cols] = mm(put_ref[...], ys_ref[...]).astype(BF)
            for kind in range(3):
                @pl.when(edge & (p == kind + 1))
                def _():
                    edge_copy(kind, j).start()
            return 0

        lax.fori_loop(0, width // tile, back, 0)

        @pl.when(p == 0)
        def _():
            pltpu.make_async_copy(pdn_ref.at[2], dn_out.at[0], own_sem.at[0]).start()

        def ahead(j, _):
            cols = pl.ds(pl.multiple_of(j * tile, tile), tile)
            for e in range(local):
                rows = pl.ds(e * cap, cap)
                y = mm_nt(hb_ref[e, mine, :], down_ref[e, cols, :])
                acc_ref[rows, :] += mm(pick_ref[rows, :], cot_ref[:, cols]) * y
                ys_ref[rows, :] = (weights[e] * y).astype(BF)
            py_ref[:, cols] = mm(put_ref[...], ys_ref[...]).astype(BF)
            return 0

        lax.fori_loop(0, width // tile, ahead, 0)
        for dst, when in ((y_own, p == 0), (y_near.at[0], p == 1),
                          (y_near.at[1], middle_device & (p == 2)),
                          (y_second, (edge & (p == 2)) | (middle_device & (p == 3))),
                          (y_third, edge & (p == 3))):
            @pl.when(when)
            def _():
                pltpu.make_async_copy(py_ref, dst, py_sem.at[0]).start()
        dws[p] = jnp.zeros((8, tokens), F32)
        for e in range(local):
            dot = jnp.sum(acc_ref[pl.ds(e * cap, cap), :], axis=1, keepdims=True)
            hit = slot == meta[e : e + 1, :]
            dws[p, e : e + 1, :] = jnp.sum(jnp.where(hit, dot, 0.0), axis=0, keepdims=True)

        @pl.when(p == 0)
        def _():
            pltpu.make_async_copy(dws.at[p], dw_out.at[me], own_sem.at[1]).start()

        @pl.when(p > 0)
        def _():
            remote(dws.at[p], dw_out.at[me], dw_send.at[src], dw_recv.at[me], "expert",
                   src).start()
        return 0

    lax.fori_loop(0, n, one_source, 0)

    tiles = width // tile
    store = lambda k, e, j: pltpu.make_async_copy(
        stage.at[k], grads_out.at[e, pl.ds(pl.multiple_of(j * tile, tile), tile), :], st_sem.at[k])

    def weight_grads(k, _):
        e, j = lax.div(k, tiles), lax.rem(k, tiles)
        cols = pl.ds(pl.multiple_of(j * tile, tile), tile)
        slot_k = lax.rem(k, 2)

        @pl.when(k >= 2)
        def _():
            store(slot_k, 0, 0).wait()

        xs = xs_ref[e, :, cols]
        stage[slot_k, :, 0:hidden] = mm_tn(xs, dg_ref[e]).astype(BF)
        stage[slot_k, :, hidden : 2 * hidden] = mm_tn(xs, du_ref[e]).astype(BF)
        stage[slot_k, :, 2 * hidden : 3 * hidden] = mm_tn(dy_ref[e, :, cols], hb_ref[e]).astype(BF)
        store(slot_k, e, j).start()
        return 0

    lax.fori_loop(0, local * tiles, weight_grads, 0)
    for k in range(2):
        store(k, 0, 0).wait()

    @pl.when(middle_device)
    def _():
        far_copy().wait_send()
        for d in range(2):
            @pl.when(sends(d, n - 2))
            def _():
                xcopy(d, n - 2).wait_send()
        y_copy(0).start()
        for kind, own in ((0, 1), (1, 2), (2, 0)):
            for part in range(pieces):
                landed = (edge_copy(kind + 1, part) if kind < 2 else pass_copy(1, part))
                landed.wait_recv()
                cols = piece(part)
                transit[kind, :, cols] = (transit[kind, :, cols].astype(F32)
                                          + pdn_ref[own, :, cols].astype(F32)).astype(BF)
                pass_copy(kind, part).start()
        for kind in range(2):
            y_copy(kind).wait()
        for part in range(pieces):
            edge_copy(0, part).wait_recv()
            pass_copy(0, part).wait_recv()
            for kind in range(3):
                pass_copy(kind, part).wait_send()

    @pl.when(edge)
    def _():
        for part in range(pieces):
            pass_copy(0, part).wait_recv()
            for kind in (1, 2):
                edge_copy(kind, part).wait_send()
        y_copy(0).wait()

    pltpu.make_async_copy(py_ref, y_own, py_sem.at[0]).wait()
    pltpu.make_async_copy(dws.at[0], dw_out.at[me], own_sem.at[1]).wait()
    for d in range(2):
        for s in range(n - 2):
            @pl.when(sends(d, s))
            def _():
                xcopy(d, s).wait_send()
    for j in range(n):
        @pl.when(me != j)
        def _():
            meta_copy(j).wait_send()
            remote(dws.at[0], dw_out.at[me], dw_send.at[j], dw_recv.at[me], "expert",
                   j).wait_send()
            remote(dws.at[0], dw_out.at[j], dw_send.at[j], dw_recv.at[j], "expert", j).wait_recv()


def moe(x, cot, cot_left, cot_right, second_left, second_right, meta, gate, up, down, cap):
    n = meta.shape[0]
    tokens, width = x.shape
    local, _, hidden = gate.shape
    tile = 256
    anywhere = pl.BlockSpec(memory_space=pl.ANY)
    dma = pltpu.SemaphoreType.DMA
    shape = jax.ShapeDtypeStruct
    return pl.pallas_call(
        functools.partial(moe_kernel, cap, tile, n),
        out_shape=(
            shape((3, tokens, width), BF), shape((n, 8, tokens), F32), shape((tokens, width), BF),
            shape((2, tokens, width), BF), shape((tokens, width), BF), shape((tokens, width), BF),
            shape((2, tokens, width), BF),
            shape((local, width, 3 * hidden), BF),
            shape((n, tokens, width), BF), shape((tokens, width), BF),
        ),
        in_specs=[anywhere] * 10,
        out_specs=[anywhere] * 10,
        scratch_shapes=[
            pltpu.VMEM((local, width, hidden), BF), pltpu.VMEM((local, width, hidden), BF),
            pltpu.VMEM((local, width, hidden), BF),
            pltpu.VMEM((tokens, width), BF), pltpu.VMEM((tokens, width), BF),
            pltpu.VMEM((n, 8, tokens), F32),
            pltpu.VMEM((local, n * cap, width), BF), pltpu.VMEM((local, n * cap, width), BF),
            pltpu.VMEM((local, n * cap, hidden), BF), pltpu.VMEM((local, n * cap, hidden), BF),
            pltpu.VMEM((local, n * cap, hidden), BF),
            pltpu.VMEM((3, tokens, width), BF), pltpu.VMEM((3, tokens, width), BF),
            pltpu.VMEM((tokens, width), BF), pltpu.VMEM((n, 8, tokens), F32),
            pltpu.VMEM((local * cap, tokens), BF), pltpu.VMEM((tokens, local * cap), BF),
            pltpu.VMEM((local * cap, tile), BF), pltpu.VMEM((local * cap, tile), F32),
            pltpu.VMEM((2, tile, 3 * hidden), BF),
            dma((3,)), dma((3,)), dma((2, n - 1)), dma((2, n - 1)), dma((2,)), dma((n,)), dma((n,)),
            dma((3, width // tile)), dma((5, width // tile)), dma((n,)), dma((n,)), dma((1,)), dma((2,)), dma((2,)),
            dma((2,)), dma((2,)),
        ],
        compiler_params=pltpu.CompilerParams(
            vmem_limit_bytes=MOE_VMEM, collective_id=1, has_side_effects=True
        ),
        cost_estimate=pl.CostEstimate(
            flops=2 * n * local * cap * width * (9 * hidden + 5 * tokens),
            transcendentals=n * local * cap * hidden,
            bytes_accessed=2 * (8 * n * tokens * width + 6 * local * width * hidden),
        ),
        name="moe",
    )(x, cot, cot_left, cot_right, second_left, second_right, meta, gate, up, down)


RIGHT = [(0, 1), (1, 2), (2, 3)]
LEFT = [(1, 0), (2, 1), (3, 2)]
RIGHT_ON = [(1, 2), (2, 3)]
LEFT_ON = [(1, 0), (2, 1)]
ACROSS = [(0, 2), (1, 3), (2, 0), (3, 1)]
FAR = [(0, 3), (3, 0)]


def project_kernel(x_ref, wq_own, wk_own, wv_own, small_own, cos_ref, sin_ref,
                   q_ref, xa_ref, kv_ref, wq_ref, wk_ref, wv_ref, small_ref,
                   small_in, root_ref, acc_ref, send_sem, recv_sem, own_sem):
    ctx = lax.axis_index("context")
    tokens, width = x_ref.shape
    kv_width = wk_ref.shape[1]
    half = width // 2
    barrier = pltpu.get_barrier_semaphore()
    pl.semaphore_signal(barrier, inc=1, device_id={"context": 1 - ctx},
                        device_id_type=pl.DeviceIdType.MESH)
    pl.semaphore_wait(barrier, 1)

    own = pl.ds(pl.multiple_of(ctx * half, 128), half)
    other = pl.ds(pl.multiple_of((1 - ctx) * half, 128), half)
    ours = pl.ds(pl.multiple_of(ctx * tokens, 16), tokens)
    give = lambda k, src, dst: remote(src, dst, send_sem.at[k], recv_sem.at[k], "context", 1 - ctx)
    weights = ((wk_own, wk_ref), (wv_own, wv_ref), (wq_own, wq_ref))
    sends = [give(0, small_own, small_in)]
    sends += [give(1 + k, a, b.at[own, :]) for k, (a, b) in enumerate(weights)]
    for copy in sends:
        copy.start()
    keeps = [pltpu.make_async_copy(a, b.at[own, :], own_sem.at[k])
             for k, (a, b) in enumerate(weights)]
    for copy in keeps:
        copy.start()

    strip = 64

    def scale(k, _):
        rows = pl.ds(pl.multiple_of(k * strip, strip), strip)
        root = inverse_root(x_ref[rows, :].astype(F32))
        root_ref[rows, :] = root
        xa_ref[rows, own] = (x_ref[rows, own].astype(F32) * root * small_own[0:1, :]).astype(BF)
        return 0

    lax.fori_loop(0, tokens // strip, scale, 0)
    for copy in keeps:
        copy.wait()

    acc_ref[:, 0:kv_width] = mm(xa_ref[:, own], wk_ref[own, :])
    acc_ref[:, kv_width : 2 * kv_width] = mm(xa_ref[:, own], wv_ref[own, :])
    tile = 256

    def first(j, _):
        cols = pl.ds(pl.multiple_of(j * tile, tile), tile)
        at = pl.ds(pl.multiple_of(2 * kv_width + j * tile, tile), tile)
        acc_ref[:, at] = mm(xa_ref[:, own], wq_ref[own, cols])
        return 0

    lax.fori_loop(0, width // tile, first, 0)

    sends[0].wait()
    small_ref[:, own] = small_own[...]
    small_ref[:, other] = small_in[...]

    def rest(k, _):
        rows = pl.ds(pl.multiple_of(k * strip, strip), strip)
        xa_ref[rows, other] = (x_ref[rows, other].astype(F32) * root_ref[rows, :]
                               * small_in[0:1, :]).astype(BF)
        return 0

    lax.fori_loop(0, tokens // strip, rest, 0)

    def rope(v):
        parts = []
        for h in range(v.shape[1] // HEAD_SIZE):
            t = v[:, h * HEAD_SIZE : (h + 1) * HEAD_SIZE]
            t = t * cos_ref[...] + pltpu.roll(t, HEAD_SIZE // 2, 1) * sin_ref[...]
            parts.append(t.astype(BF))
        return jnp.concatenate(parts, axis=1)

    sends[1].wait()
    sends[2].wait()
    k = acc_ref[:, 0:kv_width] + mm(xa_ref[:, other], wk_ref[other, :])
    v = acc_ref[:, kv_width : 2 * kv_width] + mm(xa_ref[:, other], wv_ref[other, :])
    kv_ref[ours, 0:kv_width] = rope(k)
    kv_ref[ours, kv_width : 2 * kv_width] = v.astype(BF)
    kv_copy = give(4, kv_ref.at[ours, :], kv_ref.at[ours, :])
    kv_copy.start()
    sends[3].wait()

    def second(j, _):
        cols = pl.ds(pl.multiple_of(j * tile, tile), tile)
        at = pl.ds(pl.multiple_of(2 * kv_width + j * tile, tile), tile)
        q_ref[:, cols] = rope(acc_ref[:, at] + mm(xa_ref[:, other], wq_ref[other, cols]))
        return 0

    lax.fori_loop(0, width // tile, second, 0)
    kv_copy.wait()


def project(x, wq, wk, wv, small, cos, sin):
    tokens, width = x.shape
    kv_width = wk.shape[1]
    vmem = pl.BlockSpec(memory_space=pltpu.VMEM)
    anywhere = pl.BlockSpec(memory_space=pl.ANY)
    dma = pltpu.SemaphoreType.DMA
    shape = jax.ShapeDtypeStruct
    return pl.pallas_call(
        project_kernel,
        out_shape=(
            shape((tokens, width), BF), shape((tokens, width), BF),
            shape((2 * tokens, 2 * kv_width), BF), shape((width, width), BF),
            shape((width, kv_width), BF), shape((width, kv_width), BF),
            shape((small.shape[0], width), F32),
        ),
        in_specs=[vmem, anywhere, anywhere, anywhere, vmem, vmem, vmem],
        out_specs=[vmem] * 7,
        scratch_shapes=[
            pltpu.VMEM(small.shape, F32), pltpu.VMEM((tokens, 1), F32),
            pltpu.VMEM((tokens, width + 2 * kv_width), F32), dma((5,)), dma((5,)), dma((3,)),
        ],
        compiler_params=pltpu.CompilerParams(
            vmem_limit_bytes=VMEM_LIMIT, collective_id=3, has_side_effects=True
        ),
        cost_estimate=pl.CostEstimate(
            flops=2 * tokens * width * (width + 2 * kv_width), transcendentals=0,
            bytes_accessed=8 * width * width,
        ),
        name="project",
    )(x, wq, wk, wv, small, cos, sin)


def exact(a, b, dims):
    return lax.dot_general(a, b, (dims, ((), ())), precision=lax.Precision.HIGHEST,
                           preferred_element_type=F32)


def three_parts(a, b):
    high = a.astype(BF)
    rest = a - high.astype(F32)
    middle = rest.astype(BF)
    low = (rest - middle.astype(F32)).astype(BF)
    return mm_nt(high, b) + mm_nt(middle, b) + mm_nt(low, b)


def mix_kernel(strip, ob_ref, x_ref, wo_ref, small_ref, routed_ref,
               hidden_ref, xq_ref, gates_ref):
    j = pl.program_id(0)
    tile = wo_ref.shape[1]
    cols = pl.ds(pl.multiple_of(j * tile, tile), tile)
    hidden_ref[:, cols] = x_ref[:, cols].astype(F32) + mm(ob_ref[...], wo_ref[...])

    @pl.when(j == pl.num_programs(0) - 1)
    def _():
        def one(k, _):
            rows = pl.ds(pl.multiple_of(k * strip, strip), strip)
            h = hidden_ref[rows, :]
            normed = h * inverse_root(h) * small_ref[1:2, :]
            xq_ref[rows, :] = normed.astype(BF)
            logits = three_parts(normed, small_ref[8:16, :].astype(BF))
            routed = routed_ref[rows, :] > 0.0
            top = jnp.max(jnp.where(routed, logits, NEG), axis=1, keepdims=True)
            power = jnp.where(routed, jnp.exp(jnp.where(routed, logits, top) - top), 0.0)
            gates_ref[rows, :] = power / jnp.sum(power, axis=1, keepdims=True)
            return 0

        lax.fori_loop(0, hidden_ref.shape[0] // strip, one, 0)


def row_strip(tokens):
    return 128 if tokens % 128 == 0 else 64


def mix(ob, x, wo, small, routed):
    tokens, width = x.shape
    tile = 256
    shape = jax.ShapeDtypeStruct
    const = lambda v: pl.BlockSpec(v.shape, lambda j: (0, 0), pipeline_mode=pl.Buffered(1))
    whole = lambda d: pl.BlockSpec((tokens, d), lambda j: (0, 0))
    experts = routed.shape[1]
    return pl.pallas_call(
        functools.partial(mix_kernel, row_strip(tokens)),
        out_shape=(shape((tokens, width), F32), shape((tokens, width), BF),
                   shape((tokens, experts), F32)),
        grid=(width // tile,),
        in_specs=[const(ob), const(x), pl.BlockSpec((width, tile), lambda j: (0, j)), const(small),
                  const(routed)],
        out_specs=[whole(width), whole(width), whole(experts)],
        compiler_params=pltpu.CompilerParams(vmem_limit_bytes=VMEM_LIMIT),
        cost_estimate=pl.CostEstimate(
            flops=2 * tokens * width * width, transcendentals=0, bytes_accessed=4 * width * width),
        name="mix",
    )(ob, x, wo, small, routed)


def turn_kernel(strip, local, flags, dn_ref, dw_ref, kept_ref, gates_ref, hidden_ref, cot_ref,
                wo_ref, small_ref, dh_ref, da_ref, dob_ref, misc_ref,
                normed_ref, dlog_ref, da_all, row_ref, dot_ref):
    j = pl.program_id(0)
    strips = da_all.shape[0] // strip

    @pl.when(j == 0)
    def _():
        for d in range(dw_ref.shape[0]):
            row_ref[d * local : (d + 1) * local, :] = dw_ref[d, 0:local, :]
        dot_ref[...] = row_ref[...].T * kept_ref[...]
        misc_ref[...] = jnp.zeros_like(misc_ref)

    @pl.when(j < strips)
    def _():
        rows = pl.ds(pl.multiple_of(j * strip, strip), strip)
        gain = small_ref[1:2, :]
        gates, dot = gates_ref[rows, :], dot_ref[rows, :]
        dlogits = gates * (dot - jnp.sum(gates * dot, axis=1, keepdims=True))
        dn = jnp.zeros(dh_ref.shape, F32)
        for e in range(dlogits.shape[1]):
            dn = dn + dlogits[:, e : e + 1] * small_ref[8 + e : 9 + e, :]
        for part in range(dn_ref.shape[0]):
            dn = dn + jnp.where(flags[part] > 0, dn_ref[part].astype(F32), 0.0)
        h = hidden_ref[...]
        root = inverse_root(h)
        scaled = h * root
        normed_ref[rows, :] = scaled * gain
        dlog_ref[rows, :] = dlogits
        dh = cot_ref[...].astype(F32) + norm_back(h, root, gain, dn)
        dh_ref[...] = dh
        da = dh.astype(BF)
        da_ref[...] = da
        da_all[rows, :] = da
        misc_ref[8:16, :] += fold_rows(dn * scaled, jnp.sum)

    @pl.when(j >= strips)
    def _():
        tile = wo_ref.shape[0]
        cols = pl.ds(pl.multiple_of((j - strips) * tile, tile), tile)
        dob_ref[...] = mm_nt(da_all[...], wo_ref[...]).astype(BF)
        misc_ref[0:8, cols] = exact(dlog_ref[...], normed_ref[:, cols], ((0,), (0,)))


def turn(flags, dn_parts, dw_parts, kept, gates, hidden, cot, wo, small):
    tokens, width = cot.shape
    tile, strip = 256, row_strip(tokens)
    strips = tokens // strip
    experts = gates.shape[1]
    local = experts // dw_parts.shape[0]
    shape = jax.ShapeDtypeStruct
    once = pl.Buffered(1)
    const = lambda v: pl.BlockSpec(v.shape, lambda j, f: (0,) * v.ndim, pipeline_mode=once)
    early = lambda j: jnp.minimum(j, strips - 1)
    late = lambda j: jnp.maximum(j - strips, 0)
    rows = pl.BlockSpec((strip, width), lambda j, f: (early(j), 0))
    return pl.pallas_call(
        functools.partial(turn_kernel, strip, local),
        out_shape=(shape((tokens, width), F32), shape((tokens, width), BF),
                   shape((tokens, width), BF), shape((16, width), F32)),
        grid_spec=pltpu.PrefetchScalarGridSpec(
            num_scalar_prefetch=1,
            grid=(strips + width // tile,),
            in_specs=[pl.BlockSpec((dn_parts.shape[0], strip, width), lambda j, f: (0, early(j), 0)),
                      const(dw_parts), const(kept), const(gates), rows, rows,
                      pl.BlockSpec((tile, width), lambda j, f: (late(j), 0)), const(small)],
            out_specs=[rows, rows, pl.BlockSpec((tokens, tile), lambda j, f: (0, late(j))),
                       pl.BlockSpec((16, width), lambda j, f: (0, 0))],
            scratch_shapes=[pltpu.VMEM((tokens, width), F32), pltpu.VMEM((tokens, experts), F32),
                            pltpu.VMEM((tokens, width), BF), pltpu.VMEM((experts, tokens), F32),
                            pltpu.VMEM((tokens, experts), F32)],
        ),
        compiler_params=pltpu.CompilerParams(vmem_limit_bytes=VMEM_LIMIT),
        cost_estimate=pl.CostEstimate(
            flops=2 * tokens * width * width, transcendentals=0, bytes_accessed=8 * width * width),
        name="turn",
    )(flags, dn_parts, dw_parts, kept, gates, hidden, cot, wo, small)


WIDE = 512
LINKS = 9


def tail_kernel(ob_ref, da_ref, xa_hbm, q_ref, kv_ref, do_ref, lse_ref, segk_ref, segq_ref,
                cos_ref, sin_ref, wq_hbm, wk_hbm, wv_hbm, dh_hbm, x_hbm, gain_ref, misc_ref,
                qg_out, kg_out, vg_out, og_out, mg_out, gt_ref,
                dq_ref, dkp_ref, dvp_ref, bias_ref, p_ref, dp_ref, kt_ref, dk_acc, dv_acc,
                dkv_in, dkv_ref, part, buf0, buf1, buf2, buf3, buf4, res,
                xa_ref, wq_ref, wk_ref, wv_ref, dh_ref, x_ref,
                kv_sem, send_sem, recv_sem, out_sem, load_sem):
    loads = [pltpu.make_async_copy(a, b, load_sem.at[k]) for k, (a, b) in enumerate((
        (xa_hbm, xa_ref), (wq_hbm, wq_ref), (wk_hbm, wk_ref), (wv_hbm, wv_ref), (dh_hbm, dh_ref),
        (x_hbm, x_ref)))]
    for load in loads:
        load.start()
    ctx = lax.axis_index("context")
    dp = lax.axis_index("dp")
    z = lax.axis_index("expert")
    tokens, width = xa_ref.shape
    kv_width = dkp_ref.shape[1]
    half = width // 2
    chunks = 8
    bit = lambda v: lax.rem(v, 2)
    flip = lambda v: v + 1 - 2 * bit(v)
    far = lambda v: lax.rem(v + 2, 4)
    partner = {"c": ("context", 1 - ctx), "x": ("dp", flip(dp)), "y": ("dp", far(dp)),
               "n": ("expert", flip(z)), "f": ("expert", far(z))}
    side = {"c": ctx, "x": bit(dp), "y": lax.div(dp, 2), "n": bit(z), "f": lax.div(z, 2)}

    barrier = pltpu.get_barrier_semaphore()
    for axis, other in partner.values():
        pl.semaphore_signal(barrier, inc=1, device_id={axis: other},
                            device_id_type=pl.DeviceIdType.MESH)
    pl.semaphore_wait(barrier, len(partner))

    def exchange(src, dst, ss, rs, way):
        axis, other = partner[way]
        return remote(src, dst, ss, rs, axis, other)

    theirs = pl.ds(pl.multiple_of((1 - ctx) * tokens, 16), tokens)
    ours = pl.ds(pl.multiple_of(ctx * tokens, 16), tokens)
    kv_copies = [
        exchange(ref.at[theirs], dkv_in.at[k], kv_sem.at[0, k], kv_sem.at[1, k], "c")
        for k, ref in enumerate((dkp_ref, dvp_ref))
    ]
    sizes = [half // 2, half // 4, half // 8, half // 16]
    bufs = [buf1, buf2, buf3, buf4]
    columns = [WIDE] * (chunks - 1) + [128]

    def flows(c):
        w = columns[c] // 2 if columns[c] >= 256 else columns[c]
        ways = [("n", "x", "y", "f"), ("y", "x", "n", "f"), ("n", "y", "x", "f"), ("x", "y", "n", "f")]
        return [(k, k * w, w, ways[(k + 2 * c) % 4]) for k in range(columns[c] // w)]

    def rows_at(ways, depth):
        first = 0
        for k in range(depth):
            first = first + side[ways[k]] * sizes[k]
        return pl.multiple_of(first, 16)

    def plus(dst, drows, dcols, a, arows, size):
        strip = 48
        def one(k, _):
            d = pl.ds(pl.multiple_of(drows + k * strip, 16), strip)
            s = pl.ds(pl.multiple_of(arows + k * strip, 16), strip)
            dst[d, dcols] = (dst[d, dcols].astype(F32) + a[s, dcols].astype(F32)).astype(BF)
            return 0
        lax.fori_loop(0, size // strip, one, 0)

    def link(c, flow, level):
        k, first, w, ways = flow
        cols = pl.ds(first, w)
        ss, rs = send_sem.at[c, k, level], recv_sem.at[c, k, level]
        if level == 0:
            src = part.at[c % 4, pl.ds(pl.multiple_of((1 - ctx) * half, 16), half), cols]
            return exchange(src, buf0.at[c, :, cols], ss, rs, "c")
        if level <= 4:
            way, size = ways[level - 1], sizes[level - 1]
            before = buf0 if level == 1 else bufs[level - 2]
            src = before.at[c, pl.ds(pl.multiple_of((1 - side[way]) * size, 16), size), cols]
            return exchange(src, bufs[level - 1].at[c, :, cols], ss, rs, way)
        depth = 8 - level + 1
        size = sizes[depth - 1]
        rows = pl.ds(rows_at(ways, depth), size)
        return exchange(res.at[c, rows, cols], res.at[c, rows, cols], ss, rs, ways[depth - 1])

    def produce(c):
        if c < 7:
            left, right, first = ((ob_ref, da_ref, c * WIDE) if c < 3 else
                                  (xa_ref, dq_ref, (c - 3) * WIDE) if c < 6 else
                                  (xa_ref, dkv_ref, 0))
            if c == 3:
                loads[0].wait()
            tall = width // 2
            def one(j, _):
                rows = pl.ds(pl.multiple_of(j * tall, tall), tall)
                part[c % 4, rows, :] = mm_tn(left[:, rows], right[:, first : first + WIDE]).astype(BF)
                return 0
            lax.fori_loop(0, width // tall, one, 0)
        else:
            part[c % 4, :, 0:128] = jnp.zeros((width, 128), BF)
            part[c % 4, :, 0:16] = misc_rows.T.astype(BF)
            part[c % 4, :, 16:24] = gain_rows.T.astype(BF)

    def finish(c):
        for copy in out_copy(c):
            copy.start()

    def out_copy(c):
        copy = lambda first, w, dst, at, k: pltpu.make_async_copy(
            res.at[c, :, pl.ds(first, w)], dst.at[:, pl.ds(at, w)], out_sem.at[c, k])
        if c < 3:
            return [copy(0, WIDE, og_out, c * WIDE, 0)]
        if c < 6:
            return [copy(0, WIDE, qg_out, (c - 3) * WIDE, 0)]
        if c == 6:
            return [copy(0, kv_width, kg_out, 0, 0), copy(kv_width, kv_width, vg_out, 0, 1)]
        return [copy(0, 128, mg_out, 0, 0)]

    def do(c, level):
        if level == 0:
            produce(c)
        for flow in flows(c):
            k, first, w, ways = flow
            cols = pl.ds(first, w)
            if level > 0:
                link(c, flow, level - 1).wait()
            if level == 1:
                plus(buf0.at[c], 0, cols, part.at[c % 4], ctx * half, half)
            elif 1 < level <= 4:
                before = buf0 if level == 2 else bufs[level - 3]
                plus(bufs[level - 2].at[c], 0, cols, before.at[c],
                     side[ways[level - 2]] * sizes[level - 2], sizes[level - 2])
            elif level == 5:
                rows = pl.ds(rows_at(ways, 4), sizes[3])
                keep = pl.ds(pl.multiple_of(side[ways[3]] * sizes[3], 16), sizes[3])
                res[c, rows, cols] = (buf4[c, :, cols].astype(F32)
                                      + buf3[c, keep, cols].astype(F32)).astype(BF)
            if level < LINKS:
                link(c, flow, level).start()
        if level == LINKS:
            finish(c)

    length = kv_ref.shape[0]
    tq = tokens // 2
    kb = tq
    reach = length // 2
    make_bias(ctx, tokens, segk_ref, segq_ref, bias_ref)

    def attend(step):
        group, place = step * HEADS_AT_ONCE // GROUP, step * HEADS_AT_ONCE % GROUP
        k_at = slice(group * HEAD_SIZE, (group + 1) * HEAD_SIZE)
        v_at = slice(kv_width + group * HEAD_SIZE, kv_width + (group + 1) * HEAD_SIZE)
        heads = [step * HEADS_AT_ONCE + h for h in range(HEADS_AT_ONCE)]
        at = [slice(h * HEAD_SIZE, (h + 1) * HEAD_SIZE) for h in heads]
        if place == 0:
            kt_ref[...] = kv_ref[:, k_at].astype(F32).T.astype(BF)
            dk_acc[...] = jnp.zeros_like(dk_acc)
            dv_acc[...] = jnp.zeros_like(dv_acc)

        def half_of_queries(piece, _):
            cols = pl.ds(pl.multiple_of(piece * tq, tq), tq)
            high = ctx * 2 + piece + 1
            low = jnp.maximum(high - 1 - reach // kb, 0)

            def score(i, deltas):
                rows = pl.ds(pl.multiple_of(i * kb, kb), kb)
                key, value, bias = kv_ref[rows, k_at], kv_ref[rows, v_at], bias_ref[rows, cols]
                out = []
                for h in range(HEADS_AT_ONCE):
                    s = mm_nt(key, q_ref[cols, at[h]]) * SCALE + bias
                    p = jnp.exp(s - lse_ref[heads[h], :, cols])
                    dp = mm_nt(value, do_ref[cols, at[h]])
                    p_ref[h, rows, :] = p
                    dp_ref[h, rows, :] = dp
                    out.append(deltas[h] + fold_rows(p * dp, jnp.sum))
                return tuple(out)

            deltas = lax.fori_loop(low, high, score, tuple(jnp.zeros((8, tq), F32) for _ in heads))
            deltas = [jnp.sum(d, axis=0, keepdims=True) for d in deltas]

            def grads(i, dqs):
                rows = pl.ds(pl.multiple_of(i * kb, kb), kb)
                kt = kt_ref[:, rows]
                out, dk, dv = [], dk_acc[rows, :], dv_acc[rows, :]
                for h in range(HEADS_AT_ONCE):
                    p = p_ref[h, rows, :]
                    ds = (p * (dp_ref[h, rows, :] - deltas[h])).astype(BF)
                    dv = dv + mm(p.astype(BF), do_ref[cols, at[h]])
                    dk = dk + mm(ds, q_ref[cols, at[h]])
                    out.append(dqs[h] + mm(kt, ds))
                dk_acc[rows, :] = dk
                dv_acc[rows, :] = dv
                return tuple(out)

            dqs = lax.fori_loop(low, high, grads,
                                tuple(jnp.zeros((HEAD_SIZE, tq), F32) for _ in heads))
            for h in range(HEADS_AT_ONCE):
                dq = dqs[h].T * SCALE
                turned = pltpu.roll(dq, HEAD_SIZE // 2, 1)
                dq_ref[cols, at[h]] = (dq * cos_ref[cols, :] - turned * sin_ref[cols, :]).astype(BF)
            return 0

        lax.fori_loop(0, 2, half_of_queries, 0)
        if place == GROUP - HEADS_AT_ONCE:
            dkp_ref[:, k_at] = (dk_acc[...] * SCALE).astype(BF)
            dvp_ref[:, k_at] = dv_acc[...].astype(BF)

    gain_rows = None
    misc_rows = misc_ref[...]
    steps = QUERY_HEADS // HEADS_AT_ONCE
    begin = [0, 0, 0, 3, 3, 3, 3, 5]
    paces = begin[3]
    for t in range(begin[-1] + LINKS + 1):
        if t == begin[6]:
            for copy in kv_copies:
                copy.wait()
            for h in range(kv_width // HEAD_SIZE):
                at = slice(h * HEAD_SIZE, (h + 1) * HEAD_SIZE)
                dk = dkp_ref[ours, at].astype(F32) + dkv_in[0, :, at].astype(F32)
                turned = pltpu.roll(dk, HEAD_SIZE // 2, 1)
                dkv_ref[:, at] = (dk * cos_ref[...] - turned * sin_ref[...]).astype(BF)
            dv = dvp_ref[ours, :].astype(F32) + dkv_in[1].astype(F32)
            dkv_ref[:, kv_width : 2 * kv_width] = dv.astype(BF)
        for c in range(chunks):
            if 0 <= t - begin[c] <= LINKS:
                do(c, t - begin[c])
        if t < paces:
            for k in (range(1), range(1, 3), range(3, steps))[t]:
                attend(k)
        if t == paces - 1:
            for copy in kv_copies:
                copy.start()
        if t == begin[7] - 1:
            for load in loads[1:]:
                load.wait()

            def column(j, _):
                cols = pl.ds(pl.multiple_of(j * tq, tq), tq)
                tile = mm_nt(dq_ref[...], wq_ref[cols, :])
                tile = tile + mm_nt(dkv_ref[:, 0:kv_width], wk_ref[cols, :])
                tile = tile + mm_nt(dkv_ref[:, kv_width : 2 * kv_width], wv_ref[cols, :])
                at = pl.ds(pl.multiple_of(lax.rem(j, 2) * tokens, 16), tokens)
                p_ref[lax.div(j, 2), at, :] = tile
                return 0

            lax.fori_loop(0, width // tq, column, 0)
            step = 128

            def strip(k, total):
                rows = pl.ds(pl.multiple_of(k * step, step), step)
                dxa = jnp.concatenate([
                    p_ref[j // 2, pl.ds(pl.multiple_of(j % 2 * tokens + k * step, step), step), :]
                    for j in range(width // tq)], axis=1)
                v = x_ref[rows, :].astype(F32)
                root = inverse_root(v)
                back = dh_ref[rows, :] + norm_back(v, root, gain_ref[0:1, :], dxa)
                gt_ref[rows, :] = back.astype(BF)
                return total + fold_rows(dxa * v * root, jnp.sum)

            total = lax.fori_loop(0, tokens // step, strip, jnp.zeros((8, width), F32))
            gain_rows = jnp.broadcast_to(jnp.sum(total, axis=0, keepdims=True), (8, width))
    for c in range(chunks):
        for copy in out_copy(c):
            copy.wait()


def tail(ob, da, xa, q, kv, do, lse, segk, segq, cos, sin, wq, wk, wv, dh, x, gain, misc):
    tokens, width = xa.shape
    length, kv_width = kv.shape[0], kv.shape[1] // 2
    tq = tokens // 2
    half = width // 2
    vmem = pl.BlockSpec(memory_space=pltpu.VMEM)
    anywhere = pl.BlockSpec(memory_space=pl.ANY)
    dma = pltpu.SemaphoreType.DMA
    shape = jax.ShapeDtypeStruct
    chunks = 8
    return pl.pallas_call(
        tail_kernel,
        out_shape=(
            shape((half, width), BF), shape((half, kv_width), BF), shape((half, kv_width), BF),
            shape((half, width), BF), shape((half, 128), BF), shape((tokens, width), BF),
        ),
        in_specs=[vmem, vmem, anywhere] + [vmem] * 8 + [anywhere] * 5 + [vmem] * 2,
        out_specs=[anywhere] * 5 + [vmem],
        scratch_shapes=[
            pltpu.VMEM((tokens, width), BF), pltpu.VMEM((length, kv_width), BF),
            pltpu.VMEM((length, kv_width), BF), pltpu.VMEM((length, tokens), F32),
            pltpu.VMEM((HEADS_AT_ONCE, length, tq), F32),
            pltpu.VMEM((HEADS_AT_ONCE, length, tq), F32),
            pltpu.VMEM((HEAD_SIZE, length), BF), pltpu.VMEM((length, HEAD_SIZE), F32),
            pltpu.VMEM((length, HEAD_SIZE), F32),
            pltpu.VMEM((2, tokens, kv_width), BF), pltpu.VMEM((tokens, 2 * kv_width), BF),
            pltpu.VMEM((4, width, WIDE), BF),
            pltpu.VMEM((chunks, half, WIDE), BF), pltpu.VMEM((chunks, half // 2, WIDE), BF),
            pltpu.VMEM((chunks, half // 4, WIDE), BF), pltpu.VMEM((chunks, half // 8, WIDE), BF),
            pltpu.VMEM((chunks, half // 16, WIDE), BF), pltpu.VMEM((chunks, half, WIDE), BF),
            pltpu.VMEM((tokens, width), BF), pltpu.VMEM((width, width), BF),
            pltpu.VMEM((width, kv_width), BF), pltpu.VMEM((width, kv_width), BF),
            pltpu.VMEM((tokens, width), F32), pltpu.VMEM((tokens, width), BF),
            dma((2, 2)), dma((chunks, 2, LINKS)), dma((chunks, 2, LINKS)), dma((chunks, 2)), dma((6,)),
        ],
        compiler_params=pltpu.CompilerParams(
            vmem_limit_bytes=MOE_VMEM, collective_id=2, has_side_effects=True
        ),
        cost_estimate=pl.CostEstimate(
            flops=2 * tokens * width * (2 * width + 4 * kv_width + width),
            transcendentals=0, bytes_accessed=16 * width * width,
        ),
        name="tail",
    )(ob, da, xa, q, kv, do, lse, segk, segq, cos, sin, wq, wk, wv, dh, x, gain, misc)


def finish_kernel(qg_ref, kg_ref, vg_ref, og_ref, misc_ref, y2_ref, y3_ref, hidden_ref, shard_ref,
                  q_out, k_out, v_out, o_out, router_out, first_out, second_out, layer_out,
                  gate_out, up_out, down_out):
    for src, dst in ((qg_ref, q_out), (kg_ref, k_out), (vg_ref, v_out), (og_ref, o_out)):
        dst[...] = src[...].astype(F32)
    out = hidden_ref[...]
    for ref in (y2_ref, y3_ref):
        out = out + ref[...].astype(F32)
    layer_out[...] = out.astype(BF)
    hidden = gate_out.shape[2]
    for k, dst in enumerate((gate_out, up_out, down_out)):
        dst[...] = shard_ref[:, :, k * hidden : (k + 1) * hidden].astype(F32)

    @pl.when(pl.program_id(0) == 0)
    def _():
        misc = misc_ref[...].astype(F32)
        rows = misc.T
        router_out[...] = rows[0 : router_out.shape[0], :]
        first_out[...] = rows[16:17, :]
        second_out[...] = jnp.sum(rows[8:16, :], axis=0, keepdims=True)


def finish(qg, kg, vg, og, misc, y_far, hidden, shard, experts):
    half, width = qg.shape
    kv_width = kg.shape[1]
    tokens = hidden.shape[0]
    local, rows, three = shard.shape
    ff = three // 3
    grid = 4
    shape = jax.ShapeDtypeStruct
    cut = lambda r, d: pl.BlockSpec((r // grid, d), lambda i: (i, 0))
    const = lambda r, d: pl.BlockSpec((r, d), lambda i: (0, 0))
    grads = lambda d: pl.BlockSpec((local, rows // grid, d), lambda i: (0, i, 0))
    return pl.pallas_call(
        finish_kernel,
        out_shape=(
            shape((half, width), F32), shape((half, kv_width), F32), shape((half, kv_width), F32),
            shape((half, width), F32), shape((experts, half), F32), shape((1, half), F32),
            shape((1, half), F32),
            shape((tokens, width), BF), shape((local, rows, ff), F32),
            shape((local, rows, ff), F32), shape((local, rows, ff), F32),
        ),
            grid=(grid,),
            in_specs=[
                cut(half, width), cut(half, kv_width), cut(half, kv_width), cut(half, width),
                const(half, 128),
                cut(tokens, width), cut(tokens, width), cut(tokens, width), grads(three),
            ],
            out_specs=[
                cut(half, width), cut(half, kv_width), cut(half, kv_width), cut(half, width),
                const(experts, half), const(1, half), const(1, half), cut(tokens, width), grads(ff), grads(ff),
                grads(ff),
            ],
        compiler_params=pltpu.CompilerParams(vmem_limit_bytes=VMEM_LIMIT),
        cost_estimate=pl.CostEstimate(flops=0, transcendentals=0, bytes_accessed=16 * half * width),
        name="finish",
    )(qg, kg, vg, og, misc, *y_far, hidden, shard)


def body(
    tokens, cotangent, segment_ids, routes, fill_rank, query_weight, key_projection_weight,
    value_projection_weight, output_weight, router_weight, gain_attention, gain_experts,
    gate_weight, up_weight, down_weight,
):
    context_index = lax.axis_index("context")
    context_size = lax.axis_size("context")
    expert_size = lax.axis_size("expert")
    rows = tokens.shape[1]
    length = segment_ids.shape[1]
    kv_width = KEY_VALUE_HEADS * HEAD_SIZE
    gather = lambda w, axis=0: lax.all_gather(w, "context", axis=axis, tiled=True)
    x, upstream = tokens[0], cotangent[0]

    cot_left = lax.ppermute(upstream, "expert", RIGHT)
    cot_right = lax.ppermute(upstream, "expert", LEFT)

    expert_count = router_weight.shape[1]
    local = gate_weight.shape[0]
    capacity = 5 * rows * TOP // (4 * expert_count)
    cap = -(-capacity // 64) * 64
    names = jnp.arange(expert_count, dtype=jnp.int32)
    route_hit = routes[0][:, :, None] == names[None, None, :]
    routed = jnp.any(route_hit, axis=1)
    ranks = fill_rank[0, 0].reshape(rows, TOP)
    order = jnp.sum(jnp.where(route_hit, ranks[:, :, None], 0), axis=1)
    order = jnp.where(routed, order, rows * TOP).T
    slots = jnp.sum((order[:, :, None] < order[:, None, :]).astype(jnp.int32), axis=1)
    kept = routed.T & (slots < capacity)
    slots = jnp.where(kept, slots, -1).astype(F32)
    kept_float = kept.T.astype(F32)

    small = jnp.concatenate([
        gain_attention[None], gain_experts[None], jnp.zeros((6, gain_attention.shape[0]), BF),
        router_weight.T,
    ]).astype(F32)
    positions = context_index * rows + jnp.arange(rows, dtype=jnp.int32)
    cosine, sine = rope_tables(positions)
    cos_full = jnp.concatenate([cosine, cosine], axis=-1)
    sin_full = jnp.concatenate([-sine, sine], axis=-1)
    turned = lambda v, heads, d: apply_rotary(
        v.reshape(rows, heads, HEAD_SIZE), cosine, sine, d
    ).reshape(rows, heads * HEAD_SIZE)
    output_full = gather(output_weight)
    if context_size == 2:
        q, attn_input, kv, query_full, key_full, value_full, small = project(
            x, query_weight, key_projection_weight, value_projection_weight, small,
            cos_full, sin_full,
        )
    else:
        query_full, key_full, value_full = (
            gather(query_weight), gather(key_projection_weight), gather(value_projection_weight)
        )
        small = gather(small.astype(BF), 1).astype(F32)
        residual = x.astype(F32)
        attn_input = (residual * inverse_root(residual) * small[0]).astype(BF)
        q = turned(mm(attn_input, query_full), QUERY_HEADS, 1.0).astype(BF)
        k_own = turned(mm(attn_input, key_full), KEY_VALUE_HEADS, 1.0).astype(BF)
        kv = gather(jnp.concatenate([k_own, mm(attn_input, value_full).astype(BF)], axis=1))
    segments = segment_ids[0]
    tq, kb = attention_sizes(rows, length)
    spans = attention_meta(context_index, rows, segments, tq, kb)
    segk = segments[:, None]
    segq = lax.dynamic_slice_in_dim(segments, context_index * rows, rows)[None, :]
    cot_left, cot_right, q, kv, spans, segk, segq, slots, kept_float, routed_float = (
        lax.optimization_barrier((cot_left, cot_right, q, kv, spans, segk, segq, slots, kept_float,
                                  routed.astype(F32))))
    second_left = lax.ppermute(cot_left, "expert", RIGHT_ON)
    second_right = lax.ppermute(cot_right, "expert", LEFT_ON)
    mixed, lse = attention_forward(q, kv, spans, segk, segq)

    hidden, expert_input, gates = mix(mixed, x, output_full, small, routed_float)
    expert_index = lax.axis_index("expert")
    between = (expert_index > 0) & (expert_index < expert_size - 1)
    flags = jnp.stack([expert_size > 0, between, expert_size > 0]).astype(jnp.int32)
    second_left, second_right, expert_input, flags = lax.optimization_barrier(
        (second_left, second_right, expert_input, flags))
    routing = jnp.stack([slots, (gates * kept_float).T], axis=0)
    routing = routing.reshape(2, expert_size, local, rows).transpose(1, 0, 2, 3)
    routing = routing.reshape(expert_size, 2 * local, rows)
    routing = jnp.pad(routing, ((0, 0), (0, 8 - 2 * local), (0, 0)))
    dn_parts, dw_parts, y_own, _, y_second, y_third, y_in, grads_low, _, _ = moe(
        expert_input, upstream, cot_left, cot_right, second_left, second_right, routing, gate_weight, up_weight,
        down_weight, cap,
    )
    y_far = (lax.ppermute(y_third, "expert", FAR), lax.ppermute(y_second, "expert", ACROSS))
    grads_shard = lax.psum_scatter(
        grads_low, ("dp", "context"), scatter_dimension=1, tiled=True
    )

    hidden_total, attn_grad_low, mixed_grad_low, misc = turn(
        flags, dn_parts, dw_parts, kept_float, gates, hidden, upstream, output_full, small
    )
    if (lax.axis_size("dp"), context_size, expert_size) == (4, 2, 4):
        near = hidden + y_own.astype(F32) + y_in[0].astype(F32)
        near = near + jnp.where(between, y_in[1].astype(F32), 0.0)
        near, mixed_grad_low = lax.optimization_barrier((near, mixed_grad_low))
        *sums, grad_tokens = tail(
            mixed, attn_grad_low, attn_input, q, kv, mixed_grad_low, lse, segk, segq,
            cos_full, sin_full, query_full, key_full, value_full, hidden_total, x, small, misc,
        )
        late, grad_tokens = lax.optimization_barrier((near, grad_tokens))
        (query_grad, key_grad, value_grad, output_grad, router_grad, first, second, layer_out,
         *expert_sums) = finish(*sums, y_far, late, grads_shard, expert_count)
        sums = (query_grad, key_grad, value_grad, output_grad, router_grad.T, first[0], second[0])
    else:
        dq_low, dk_part, dv_part = attention_backward(
            q, kv, mixed_grad_low, lse, cos_full, sin_full, spans, segk, segq
        )
        dkv = lax.psum_scatter(
            jnp.concatenate([dk_part, dv_part], axis=1), "context", scatter_dimension=0, tiled=True
        )
        dk_low = turned(dkv[:, :kv_width].astype(F32), KEY_VALUE_HEADS, -1.0).astype(BF)
        dv_low = dkv[:, kv_width:]
        input_total = (
            mm_nt(dq_low, query_full) + mm_nt(dk_low, key_full) + mm_nt(dv_low, value_full)
        )
        residual = x.astype(F32)
        root = inverse_root(residual)
        grad_tokens = (hidden_total + norm_back(residual, root, small[0], input_total)).astype(BF)
        reduce_rows = lambda v: lax.psum(
            lax.psum_scatter(v.astype(BF), "context", scatter_dimension=0, tiled=True),
            ("dp", "expert"),
        ).astype(F32)
        sums = tuple(reduce_rows(v) for v in (
            mm_tn(attn_input, dq_low), mm_tn(attn_input, dk_low), mm_tn(attn_input, dv_low),
            mm_tn(mixed, attn_grad_low), misc[:8].T,
            jnp.sum(input_total * residual * root, axis=0), jnp.sum(misc[8:16], axis=0),
        ))
        mixture = sum(v.astype(F32) for v in (y_own, y_in[0], *y_far))
        mixture = mixture + jnp.where(between, y_in[1].astype(F32), 0.0)
        layer_out = (hidden + mixture).astype(BF)
        ff = gate_weight.shape[2]
        wide = grads_shard.astype(F32)
        expert_sums = [wide[:, :, i * ff : (i + 1) * ff] for i in range(3)]
    return (layer_out[None], grad_tokens[None], *sums, *expert_sums)


def solution(mesh):
    both = ("dp", "expert")
    token_spec = P(both, "context", None)
    row_spec = P("context", None)
    expert_out = P("expert", ("dp", "context"), None)
    return jax.shard_map(
        body,
        mesh=mesh,
        in_specs=(
            token_spec, token_spec, P(both, None), token_spec, token_spec,
            row_spec, row_spec, row_spec, row_spec, row_spec, P("context"), P("context"),
            P("expert", None, None), P("expert", None, None), P("expert", None, None),
        ),
        out_specs=(
            token_spec, token_spec, row_spec, row_spec, row_spec, row_spec, row_spec,
            P("context"), P("context"), expert_out, expert_out, expert_out,
        ),
        check_vma=False,
    )
```
